32 devices in a mesh: dp: 16 (over z, y, x), tensor: 2 (over core).
Axes of the slice: x: 2, y: 2, z: 4, core: 2. Of those that a mesh axis runs over, the one named last changes fastest.
Arguments:
- tokens: bfloat16 [32, 1024, 768], P(None, ('dp', 'tensor')), may hold values from -6 to 6
- encoder: bfloat16 [32, 128, 768], P('dp', 'tensor'), may hold values from -6 to 6
- lengths: int32 [32], replicated, may hold values from 256 to 1024, as said below
- deal: int32 [32], replicated, may hold values from 0 to 31, as said below
- self_project: bfloat16 [768, 3, 768], P('dp', None, 'tensor'), may hold values from -0.21875 to 0.21875
- self_output: bfloat16 [768, 768], P('tensor', 'dp'), may hold values from -1.75 to 1.75
- cross_query: bfloat16 [768, 768], P('dp', 'tensor'), may hold values from -0.21875 to 0.21875
- cross_memory: bfloat16 [768, 2, 768], P('dp', None, 'tensor'), may hold values from -0.21875 to 0.21875
- cross_output: bfloat16 [768, 768], P('tensor', 'dp'), may hold values from -1.75 to 1.75
- hidden_in: bfloat16 [768, 3072], P('dp', 'tensor'), may hold values from -0.21875 to 0.21875
- hidden_out: bfloat16 [3072, 768], P('tensor', 'dp'), may hold values from -0.109375 to 0.109375
- in_bias: float32 [4, 768], P(None, 'tensor'), may hold values from -3 to 3
- out_bias: float32 [3, 768], replicated, may hold values from -3 to 3
- hidden_bias: float32 [3072], P('tensor'), may hold values from -3 to 3
- norm_gain: float32 [3, 768], replicated, may hold values from 0.5 to 1.5
- norm_bias: float32 [3, 768], replicated, may hold values from -2 to 2
- cotangent: bfloat16 [32, 1024, 768], P(None, ('dp', 'tensor')), may hold values from -6 to 6
Outputs:
- output: bfloat16 [32, 1024, 768], P(None, ('dp', 'tensor'))
- grad_tokens: bfloat16 [32, 1024, 768], P(None, ('dp', 'tensor'))
- grad_encoder: bfloat16 [32, 128, 768], P('dp', 'tensor')
- grad_self_project: float32 [768, 3, 768], P('dp', None, 'tensor')
- grad_self_output: float32 [768, 768], P('tensor', 'dp')
- grad_cross_query: float32 [768, 768], P('dp', 'tensor')
- grad_cross_memory: float32 [768, 2, 768], P('dp', None, 'tensor')
- grad_cross_output: float32 [768, 768], P('tensor', 'dp')
- grad_hidden_in: float32 [768, 3072], P('dp', 'tensor')
- grad_hidden_out: float32 [3072, 768], P('tensor', 'dp')
- grad_in_bias: float32 [4, 768], P(None, 'tensor')
- grad_out_bias: float32 [3, 768], replicated
- grad_hidden_bias: float32 [3072], P('tensor')
- grad_norm_gain: float32 [3, 768], replicated
- grad_norm_bias: float32 [3, 768], replicated
The draws below stay inside these ranges and needn't reach their ends.
Inputs may be any that keep to these rules, and one draw needn't show every extreme that they name: A permutation: dealt slot t holds initial sequence deal[t]; slots 2 i and 2 i + 1 belong to index i of dp; the lengths of those two sequences sum to at most 1536, and to exactly 1536 for some i. `lengths`: 1024 is reached.
All inputs are finite; a program needn't handle non-finite values.
Results may differ from the reference program's by a relative error of at most 0.022.
Values may be sent and summed in bfloat16 or wider, within the bound.
No kernel may reach another device: no remote copies, remote signals or barrier semaphores. Data moves between devices by JAX's collectives and lax.ppermute only.
A program may use at most 256 MiB of HBM per device.

```python
import math
import jax
import jax.numpy as jnp
from jax import lax

D = 768
HEADS = 12
FF = 3072
HD = 64
LMAX = 1024
LMIN = 256
CAP = 1536
ENC = 128
NSEQ = 32


def dealt_pairs(key):
    base_key = jax.random.fold_in(key, 11)
    key_order, key_first, key_second, key_pick, key_swap = jax.random.split(base_key, 5)
    pair_count = NSEQ // 2
    permuted = jax.random.permutation(key_order, NSEQ).astype(jnp.int32)
    first_len = jax.random.randint(key_first, (pair_count,), LMIN, LMAX + 1, dtype=jnp.int32)
    chosen_pair = jax.random.randint(key_pick, (), 0, pair_count, dtype=jnp.int32)
    is_full = jnp.arange(pair_count, dtype=jnp.int32) == chosen_pair
    first_len = jnp.where(is_full, LMAX, first_len)
    room_left = jnp.minimum(CAP - first_len, LMAX)
    second_len = jax.random.randint(key_second, (pair_count,), LMIN, room_left + 1, dtype=jnp.int32)
    second_len = jnp.where(is_full, CAP - LMAX, second_len)
    swapped = jax.random.randint(key_swap, (pair_count,), 0, 2, dtype=jnp.int32) == 1
    lead_len = jnp.where(swapped, second_len, first_len)
    trail_len = jnp.where(swapped, first_len, second_len)
    pair_lens = jnp.stack([lead_len, trail_len], 1).reshape(NSEQ)
    lengths = jnp.zeros((NSEQ,), jnp.int32).at[permuted].set(pair_lens)
    return (permuted, lengths)


def draw_deal(key, part):
    return dealt_pairs(key)[0]


def draw_lengths(key, part):
    return dealt_pairs(key)[1]


def block_scale(rng, shape, cuts, smallest, high):
    def one(position, parts):
        draws = jax.random.uniform(jax.random.fold_in(jax.random.fold_in(rng, 6), position), (parts,), jnp.float32, smallest / len(cuts), high / len(cuts))
        return jnp.repeat(jnp.exp(draws), shape[position] // parts).reshape((-1,) + (1,) * (len(shape) - position - 1))

    factor_of = one(*cuts[0])
    for cut in cuts[1:]:
        factor_of = factor_of * one(*cut)
    return factor_of


def noise(rng, dims, deviation, bound, shards=(), kind=jnp.bfloat16):
    result = jax.random.normal(rng, dims, jnp.float32) * deviation
    if len(shards) > 0:
        result = block_scale(rng, dims, shards, -0.22, 0.18) * result
    return jnp.clip(result, min=-bound, max=bound).astype(kind)


def setup_inputs(seed: int = 0) -> dict:
    arg_keys = jax.random.split(jax.random.key(seed), 18)
    tokens = noise(arg_keys[0], (NSEQ, LMAX, D), 1.0, 6.0, ((1, 32),))
    encoder = noise(arg_keys[1], (NSEQ, ENC, D), 1.0, 6.0, ((0, 16), (1, 2)))
    lengths = draw_lengths(jax.random.fold_in(arg_keys[17], 71), 0)
    deal = draw_deal(jax.random.fold_in(arg_keys[17], 71), 0)
    self_project = noise(arg_keys[4], (D, 3, D), D ** -0.5, 0.21875, ((0, 16), (2, 2)))
    self_output = noise(arg_keys[5], (D, D), (D // 64) ** -0.5, 1.75, ((0, 2), (1, 16)))
    cross_query = noise(arg_keys[6], (D, D), D ** -0.5, 0.21875, ((0, 16), (1, 2)))
    cross_memory = noise(arg_keys[7], (D, 2, D), D ** -0.5, 0.21875, ((0, 16), (2, 2)))
    cross_output = noise(arg_keys[8], (D, D), (D // 64) ** -0.5, 1.75, ((0, 2), (1, 16)))
    hidden_in = noise(arg_keys[9], (D, FF), D ** -0.5, 0.21875, ((0, 16), (1, 2)))
    hidden_out = noise(arg_keys[10], (FF, D), FF ** -0.5, 0.109375, ((0, 2), (1, 16)))
    in_bias = noise(arg_keys[11], (4, D), 0.5, 3.0, ((1, 2),), jnp.float32)
    out_bias = noise(arg_keys[12], (3, D), 0.5, 3.0, (), jnp.float32)
    hidden_bias = noise(arg_keys[13], (FF,), 0.5, 3.0, ((0, 2),), jnp.float32)
    norm_gain = jnp.clip(1.0 + 0.1 * jax.random.normal(arg_keys[14], (3, D), jnp.float32), 0.5, 1.5)
    norm_bias = noise(arg_keys[15], (3, D), 0.3, 2.0, (), jnp.float32)
    cotangent = noise(arg_keys[16], (NSEQ, LMAX, D), 1.0, 6.0, ((1, 32),))
    return {"tokens": tokens, "encoder": encoder, "lengths": lengths, "deal": deal, "self_project": self_project, "self_output": self_output, "cross_query": cross_query, "cross_memory": cross_memory, "cross_output": cross_output, "hidden_in": hidden_in, "hidden_out": hidden_out, "in_bias": in_bias, "out_bias": out_bias, "hidden_bias": hidden_bias, "norm_gain": norm_gain, "norm_bias": norm_bias, "cotangent": cotangent}


HIGHEST = lax.Precision.HIGHEST
EPSILON = 1e-05
MASKED = -1e+30

@jax.custom_vjp
def low(v):
    return lax.optimization_barrier(v.astype(jnp.bfloat16)).astype(jnp.float32)

@jax.custom_vjp
def low_back(v):
    return v

def low_keep(v):
    return (low(v), None)

def low_pass(kept, grad):
    return (grad,)

def back_keep(v):
    return (v, None)

def back_low(kept, grad):
    return (low(grad),)
low.defvjp(low_keep, low_pass)
low_back.defvjp(back_keep, back_low)

def matmul(left_side, right_side):
    return jnp.dot(left_side, right_side, precision=HIGHEST, preferred_element_type=jnp.float32)

def layer_norm(hidden, gain_row, shift_row):
    center = hidden - lax.optimization_barrier(jnp.mean(hidden, -1, keepdims=True))
    spread = lax.optimization_barrier(jnp.mean(center * center, -1, keepdims=True))
    return center * lax.rsqrt(spread + EPSILON) * gain_row + shift_row

def attention(queries, keys_in, values_in, allowed):
    query_count = queries.shape[0]
    key_count = keys_in.shape[0]
    query_heads = queries.reshape(query_count, HEADS, HD)
    key_heads = keys_in.reshape(key_count, HEADS, HD)
    value_heads = values_in.reshape(key_count, HEADS, HD)
    scores = low_back(jnp.einsum('qhd,khd->hqk', query_heads, key_heads, precision=HIGHEST))
    scores = jnp.where(allowed[None], scores, MASKED)
    probability = jax.nn.softmax(scores, axis=-1)
    attended = jnp.einsum('hqk,khd->qhd', low(probability), value_heads, precision=HIGHEST)
    return low(low_back(attended.reshape(query_count, HEADS * HD)))

def sequence(params, token_rows, memory_rows, length):
    project_weight, self_out_weight, query_weight, memory_weight, cross_out_weight, expand_weight, reduce_weight, in_bias, out_bias, hidden_bias, norm_gain, norm_bias = params
    score_scale = 1.0 / math.sqrt(HD)
    row_count = token_rows.shape[0]
    memory_count = memory_rows.shape[0]
    positions = jnp.arange(row_count, dtype=jnp.int32)
    valid_rows = positions < length
    self_allowed = (positions[None, :] <= positions[:, None]) & valid_rows[None, :]
    mixed_proj = matmul(token_rows, project_weight.reshape(D, 3 * D)).reshape(row_count, 3, D)
    queries = low(low_back((mixed_proj[:, 0] + in_bias[0]) * score_scale))
    keys_self = low(low_back(mixed_proj[:, 1]))
    values_self = low(low_back(mixed_proj[:, 2] + in_bias[1]))
    attended = attention(queries, keys_self, values_self, self_allowed)
    branch_self = low_back(matmul(attended, self_out_weight) + out_bias[0])
    normed_one = layer_norm(token_rows + branch_self, norm_gain[0], norm_bias[0])
    cross_in = low(normed_one)
    cross_queries = low(low_back((matmul(cross_in, query_weight) + in_bias[2]) * score_scale))
    memory_kv = matmul(memory_rows, memory_weight.reshape(D, 2 * D)).reshape(memory_count, 2, D)
    keys_cross = low(low_back(memory_kv[:, 0]))
    values_cross = low(low_back(memory_kv[:, 1] + in_bias[3]))
    cross_allowed = jnp.ones((row_count, memory_count), dtype=jnp.bool_)
    cross_attended = attention(cross_queries, keys_cross, values_cross, cross_allowed)
    branch_cross = low_back(matmul(cross_attended, cross_out_weight) + out_bias[1])
    normed_two = layer_norm(normed_one + branch_cross, norm_gain[1], norm_bias[1])
    hidden_rows = low(normed_two)
    pre_act = low_back(matmul(hidden_rows, expand_weight) + hidden_bias)
    activated = low(jax.nn.gelu(pre_act, approximate=False))
    branch_ffn = low_back(matmul(activated, reduce_weight) + out_bias[2])
    final_rows = layer_norm(normed_two + branch_ffn, norm_gain[2], norm_bias[2])
    return jnp.where(valid_rows[:, None], final_rows, 0.0)

def whole_layer(params, token_values, memory_values, lengths):

    def one_step(carry, item):
        token_rows, memory_rows, length = item
        return (carry, jax.checkpoint(sequence)(params, token_rows, memory_rows, length))
    _, outputs = lax.scan(one_step, jnp.zeros((), jnp.float32), (token_values, memory_values, lengths))
    return outputs

def reference(tokens, encoder, lengths, deal, self_project, self_output, cross_query, cross_memory, cross_output, hidden_in, hidden_out, in_bias, out_bias, hidden_bias, norm_gain, norm_bias, cotangent):
    inverse = jnp.zeros_like(deal).at[deal].set(jnp.arange(deal.shape[0], dtype=jnp.int32))
    params = (self_project.astype(jnp.float32), self_output.astype(jnp.float32), cross_query.astype(jnp.float32), cross_memory.astype(jnp.float32), cross_output.astype(jnp.float32), hidden_in.astype(jnp.float32), hidden_out.astype(jnp.float32), in_bias.astype(jnp.float32), out_bias.astype(jnp.float32), hidden_bias.astype(jnp.float32), norm_gain.astype(jnp.float32), norm_bias.astype(jnp.float32))

    def forward(layer_params, token_values, memory_values):
        memory_orig = jnp.take(memory_values, inverse, axis=0)
        return whole_layer(layer_params, token_values, memory_orig, lengths)
    final_rows, pullback = jax.vjp(forward, params, tokens.astype(jnp.float32), encoder.astype(jnp.float32))
    valid_rows = jnp.arange(tokens.shape[1], dtype=jnp.int32)[None, :] < lengths[:, None]
    seed_grad = jnp.where(valid_rows[:, :, None], cotangent.astype(jnp.float32), 0.0)
    grad_params, grad_tokens, grad_encoder = pullback(seed_grad)
    return (final_rows.astype(jnp.bfloat16), grad_tokens.astype(jnp.bfloat16), grad_encoder.astype(jnp.bfloat16), grad_params[0], grad_params[1], grad_params[2], grad_params[3], grad_params[4], grad_params[5], grad_params[6], grad_params[7], grad_params[8], grad_params[9], grad_params[10], grad_params[11])
```

```python
import functools
import math

import jax
import jax.numpy as jnp
from jax import lax
from jax.experimental import pallas as pl
from jax.experimental.pallas import tpu as pltpu
from jax.sharding import PartitionSpec as P

HD = 64
EPSILON = 1e-05
MASKED = -1e30
BLOCK = 128
F32 = jnp.float32
BF16 = jnp.bfloat16


def dot_nn(left, right):
    return lax.dot_general(left, right, (((1,), (0,)), ((), ())), preferred_element_type=F32)


def dot_nt(left, right):
    return lax.dot_general(left, right, (((1,), (1,)), ((), ())), preferred_element_type=F32)


def dot_tn(left, right):
    return lax.dot_general(left, right, (((0,), (0,)), ((), ())), preferred_element_type=F32)


def lane_low(shape):
    return lax.broadcasted_iota(jnp.int32, shape, 1) < HD


def stack_heads(rows):
    low = lane_low(rows.shape)
    zero = jnp.zeros_like(rows)
    return jnp.concatenate([jnp.where(low, rows, zero), jnp.where(low, zero, rows)], 0)


def unstack_heads(transposed):
    both = transposed.T
    low = lane_low((BLOCK, 2 * HD))
    return jnp.where(low, both[:BLOCK], both[BLOCK:])


def block_place(meta):
    block = pl.program_id(1)
    first_blocks = meta[0]
    second = block >= first_blocks
    start = jnp.where(second, first_blocks, 0)
    return block, block - start, start, second.astype(jnp.int32), block < meta[1]


def diagonal_mask(own, piece, tensor_index):
    key = lax.broadcasted_iota(jnp.int32, (BLOCK, 2 * BLOCK), 0)
    query = lax.broadcasted_iota(jnp.int32, (BLOCK, 2 * BLOCK), 1) & (BLOCK - 1)
    if own:
        return key <= query
    shift = piece.bit_length() - 1
    return (key >> shift) < (query >> shift) + tensor_index


def mask_scores(scores, mask):
    keys = scores.shape[0]
    last = jnp.where(mask, scores[keys - BLOCK :], MASKED)
    if keys == BLOCK:
        return last
    return jnp.concatenate([scores[: keys - BLOCK], last], 0)


def forward_kernel(parts, causal, piece, spans, meta, q_ref, *refs):
    keys = refs[:parts]
    values = refs[parts : 2 * parts]
    out_ref, lse_ref = refs[2 * parts : 2 * parts + 2]
    flipped = refs[2 * parts + 2 :]
    block, local, start, second, active = block_place(meta)

    @pl.when(block == 0)
    def _():
        for part in range(parts):
            flipped[part][...] = values[part][...].astype(F32).T.astype(BF16)

    def run(base, span):
        stacked = stack_heads(q_ref[...])
        scores = []
        for part in range(parts):
            tile = dot_nt(keys[part][pl.ds(base, span), :], stacked)
            if causal:
                tile = mask_scores(tile, diagonal_mask(part == 0, piece, meta[2]))
            scores.append(tile)
        top = functools.reduce(
            jnp.maximum, [jnp.max(tile, 0, keepdims=True) for tile in scores]
        )
        exps = [jnp.exp(tile - top) for tile in scores]
        total = functools.reduce(jnp.add, [jnp.sum(tile, 0, keepdims=True) for tile in exps])
        result = functools.reduce(
            jnp.add,
            [
                dot_nn(flipped[part][:, pl.ds(base, span)], exps[part].astype(BF16))
                for part in range(parts)
            ],
        )
        out_ref[...] = unstack_heads(result / total).astype(BF16)
        lse_ref[...] = jnp.broadcast_to(top + jnp.log(total), (1, 1, 8, 2 * BLOCK))

    if causal:
        base = pl.multiple_of(start * BLOCK, BLOCK)
        for step in range(spans):
            pl.when(active & (local == step))(functools.partial(run, base, (step + 1) * BLOCK))
    else:
        pl.when(active)(functools.partial(run, pl.multiple_of(second * BLOCK, BLOCK), BLOCK))

    @pl.when(jnp.logical_not(active))
    def _():
        out_ref[...] = jnp.zeros_like(out_ref)
        lse_ref[...] = jnp.zeros_like(lse_ref)


def backward_kernel(parts, causal, piece, spans, meta, q_ref, g_ref, lse_ref, *refs):
    keys = refs[:parts]
    values = refs[parts : 2 * parts]
    dq_ref = refs[2 * parts]
    dk_out = refs[2 * parts + 1 : 3 * parts + 1]
    dv_out = refs[3 * parts + 1 : 4 * parts + 1]
    flipped = refs[4 * parts + 1 : 5 * parts + 1]
    dk_sum = refs[5 * parts + 1 : 6 * parts + 1]
    dv_sum = refs[6 * parts + 1 : 7 * parts + 1]
    block, local, start, second, active = block_place(meta)

    @pl.when(block == 0)
    def _():
        for part in range(parts):
            flipped[part][...] = keys[part][...].astype(F32).T.astype(BF16)
            dk_sum[part][...] = jnp.zeros_like(dk_sum[part])
            dv_sum[part][...] = jnp.zeros_like(dv_sum[part])

    def run(base, span):
        queries = stack_heads(q_ref[...])
        grads = stack_heads(g_ref[...])
        lse = lse_ref[0, 0, 0:1, :]
        probs = []
        grad_probs = []
        for part in range(parts):
            tile = dot_nt(keys[part][pl.ds(base, span), :], queries)
            if causal:
                tile = mask_scores(tile, diagonal_mask(part == 0, piece, meta[2]))
            probs.append(jnp.exp(tile - lse))
            grad_probs.append(dot_nt(values[part][pl.ds(base, span), :], grads))
        row_dot = functools.reduce(
            jnp.add,
            [jnp.sum(p * g, 0, keepdims=True) for p, g in zip(probs, grad_probs)],
        )
        grad_query = None
        for part in range(parts):
            grad_score = (probs[part] * (grad_probs[part] - row_dot)).astype(BF16)
            place = pl.ds(base, span)
            dv_sum[part][place, :] += dot_nn(probs[part].astype(BF16), grads)
            dk_sum[part][place, :] += dot_nn(grad_score, queries)
            term = dot_nn(flipped[part][:, place], grad_score)
            grad_query = term if grad_query is None else grad_query + term
        dq_ref[...] = unstack_heads(grad_query).astype(BF16)

    if causal:
        base = pl.multiple_of(start * BLOCK, BLOCK)
        for step in range(spans):
            pl.when(active & (local == step))(functools.partial(run, base, (step + 1) * BLOCK))
    else:
        pl.when(active)(functools.partial(run, pl.multiple_of(second * BLOCK, BLOCK), BLOCK))

    @pl.when(jnp.logical_not(active))
    def _():
        dq_ref[...] = jnp.zeros_like(dq_ref)

    @pl.when(block == pl.num_programs(1) - 1)
    def _():
        for part in range(parts):
            dk_out[part][...] = dk_sum[part][...].astype(dk_out[part].dtype)
            dv_out[part][...] = dv_sum[part][...].astype(dv_out[part].dtype)


def row_spec():
    return pl.BlockSpec((BLOCK, 2 * HD), lambda pair, block, meta: (block, pair))


def whole_spec(rows):
    return pl.BlockSpec((rows, 2 * HD), lambda pair, block, meta: (0, pair))


def lse_spec():
    return pl.BlockSpec((1, 1, 8, 2 * BLOCK), lambda pair, block, meta: (pair, block, 0, 0))


def attend_forward(meta, queries, keys, values, causal, piece, spans):
    rows, width = queries.shape
    parts = len(keys)
    pairs, blocks = width // (2 * HD), rows // BLOCK
    key_rows = keys[0].shape[0]
    work = pairs * blocks * parts * 4 * BLOCK * 2 * BLOCK * (2 * BLOCK if causal else BLOCK)
    return pl.pallas_call(
        functools.partial(forward_kernel, parts, causal, piece, spans),
        grid_spec=pltpu.PrefetchScalarGridSpec(
            num_scalar_prefetch=1,
            grid=(pairs, blocks),
            in_specs=[row_spec()] + [whole_spec(key_rows)] * (2 * parts),
            out_specs=[row_spec(), lse_spec()],
            scratch_shapes=[pltpu.VMEM((2 * HD, key_rows), BF16)] * parts,
        ),
        out_shape=[
            jax.ShapeDtypeStruct((rows, width), BF16),
            jax.ShapeDtypeStruct((pairs, blocks, 8, 2 * BLOCK), F32),
        ],
        cost_estimate=pl.CostEstimate(
            flops=4 * work, bytes_accessed=8 * rows * width, transcendentals=work // 256
        ),
        name="attend_forward",
    )(meta, queries, *keys, *values)


def attend_backward(meta, queries, grads, lse, keys, values, causal, piece, spans, kinds):
    rows, width = queries.shape
    parts = len(keys)
    pairs, blocks = width // (2 * HD), rows // BLOCK
    key_rows = keys[0].shape[0]
    work = pairs * blocks * parts * 4 * BLOCK * 2 * BLOCK * (2 * BLOCK if causal else BLOCK)
    results = pl.pallas_call(
        functools.partial(backward_kernel, parts, causal, piece, spans),
        grid_spec=pltpu.PrefetchScalarGridSpec(
            num_scalar_prefetch=1,
            grid=(pairs, blocks),
            in_specs=[row_spec(), row_spec(), lse_spec()] + [whole_spec(key_rows)] * (2 * parts),
            out_specs=[row_spec()] + [whole_spec(key_rows)] * (2 * parts),
            scratch_shapes=[pltpu.VMEM((2 * HD, key_rows), BF16)] * parts
            + [pltpu.VMEM((key_rows, 2 * HD), F32)] * (2 * parts),
        ),
        out_shape=[jax.ShapeDtypeStruct((rows, width), BF16)]
        + [jax.ShapeDtypeStruct((key_rows, width), kind) for kind in kinds + kinds],
        cost_estimate=pl.CostEstimate(
            flops=10 * work, bytes_accessed=16 * rows * width, transcendentals=work // 256
        ),
        name="attend_backward",
    )(meta, queries, grads, lse, *keys, *values)
    return results[0], results[1 : 1 + parts], results[1 + parts :]


def norm_forward(hidden, gain, shift):
    center = hidden - jnp.mean(hidden, -1, keepdims=True)
    spread = jnp.mean(center * center, -1, keepdims=True)
    scale = lax.rsqrt(spread + EPSILON)
    unit = center * scale
    return unit * gain + shift, unit, scale


def norm_backward(grad, unit, scale, gain):
    gain_grad = jnp.sum(grad * unit, 0)
    shift_grad = jnp.sum(grad, 0)
    inner = grad * gain
    mean_inner = jnp.mean(inner, -1, keepdims=True)
    mean_unit = jnp.mean(inner * unit, -1, keepdims=True)
    return scale * (inner - mean_inner - unit * mean_unit), gain_grad, shift_grad


def swap(value):
    return lax.ppermute(value, "tensor", [(0, 1), (1, 0)])


def body(
    tokens,
    encoder,
    lengths,
    deal,
    self_project,
    self_output,
    cross_query,
    cross_memory,
    cross_output,
    hidden_in,
    hidden_out,
    in_bias,
    out_bias,
    hidden_bias,
    norm_gain,
    norm_bias,
    cotangent,
):
    score_scale = 1.0 / math.sqrt(HD)
    dp_count = lax.axis_size("dp")
    dp_index = lax.axis_index("dp")
    tensor_index = lax.axis_index("tensor")
    piece = tokens.shape[1]
    width = tokens.shape[2]
    slots = piece * dp_count
    half = self_project.shape[2]
    units = hidden_in.shape[1]
    shard = self_project.shape[0]
    memory_rows = encoder.shape[1]
    spans = slots // BLOCK
    blocks = (slots + slots // 2) // BLOCK + 1
    rows = blocks * BLOCK
    per_block = BLOCK // piece

    pair_ids = lax.dynamic_slice_in_dim(deal, 2 * dp_index, 2)
    pair_len = jnp.take(lengths, pair_ids)
    pieces_used = (pair_len + 2 * piece - 1) // (2 * piece)
    blocks_used = (pieces_used * piece + BLOCK - 1) // BLOCK
    first_blocks = blocks_used[0]
    all_blocks = first_blocks + blocks_used[1]
    meta = jnp.stack([first_blocks, all_blocks, tensor_index]).astype(jnp.int32)

    block_ids = jnp.arange(blocks, dtype=jnp.int32)
    block_seq = (block_ids >= first_blocks).astype(jnp.int32)
    block_local = jnp.minimum(block_ids - block_seq * first_blocks, spans - 1)
    piece_ids = (
        (block_local[:, None] * per_block + jnp.arange(per_block, dtype=jnp.int32)[None, :]) * 2
        + block_seq[:, None]
    ).reshape(-1)
    slot_ids = block_local[:, None] * BLOCK + jnp.arange(BLOCK, dtype=jnp.int32)[None, :]
    positions = ((slot_ids // piece) * 2 + tensor_index) * piece + slot_ids % piece
    row_valid = (
        (positions < jnp.where(block_seq == 1, pair_len[1], pair_len[0])[:, None])
        & (block_ids < all_blocks)[:, None]
    ).reshape(rows, 1)

    def exchange(value):
        ordered = jnp.take(value, deal, axis=0)
        arrived = lax.all_to_all(ordered, "dp", split_axis=0, concat_axis=0, tiled=True)
        return jnp.take(arrived, piece_ids, axis=0).reshape(rows, width)

    send_piece = jnp.arange(dp_count, dtype=jnp.int32)
    send_block = send_piece // per_block
    send_ids = jnp.stack(
        [
            jnp.minimum(send_block, blocks_used[0] - 1) * per_block,
            (first_blocks + jnp.minimum(send_block, blocks_used[1] - 1)) * per_block,
        ],
        1,
    ) + (send_piece % per_block)[:, None]
    send_pos = (send_piece[:, None, None] * 2 + tensor_index) * piece + jnp.arange(
        piece, dtype=jnp.int32
    )[None, None, :]
    send_valid = (send_pos < pair_len[None, :, None]).reshape(2 * dp_count, piece, 1)
    inverse = jnp.zeros_like(deal).at[deal].set(jnp.arange(deal.shape[0], dtype=jnp.int32))

    def send_home(value):
        pieces = value.reshape(rows // piece, piece, width)
        outgoing = jnp.where(
            send_valid, jnp.take(pieces, send_ids.reshape(-1), axis=0), jnp.zeros((), value.dtype)
        )
        back = lax.all_to_all(outgoing, "dp", split_axis=0, concat_axis=0, tiled=True)
        return jnp.take(back, inverse, axis=0)

    inputs = exchange(tokens)

    def gather(value):
        own = lax.all_gather(value, "dp", axis=0, tiled=True)
        return (own, swap(own))

    qkv_weight = gather(self_project.reshape(shard, 3 * half))
    mid_weight = gather(
        jnp.concatenate(
            [self_output.T, cross_query, cross_memory.reshape(shard, 2 * half), cross_output.T], 1
        )
    )
    ffn_weight = gather(jnp.concatenate([hidden_in, hidden_out.T], 1))
    both = (0, 1)

    def columns(pair, start, count):
        return [lax.slice_in_dim(pair[h], start, start + count, axis=1) for h in both]

    project_q = columns(qkv_weight, 0, half)
    project_k = columns(qkv_weight, half, half)
    project_v = columns(qkv_weight, 2 * half, half)
    self_out = columns(mid_weight, 0, half)
    query_w = columns(mid_weight, half, half)
    memory_k = columns(mid_weight, 2 * half, half)
    memory_v = columns(mid_weight, 3 * half, half)
    cross_out = columns(mid_weight, 4 * half, half)
    expand = columns(ffn_weight, 0, units)
    reduce = columns(ffn_weight, units, units)

    biases = jnp.concatenate([in_bias.reshape(-1), hidden_bias])
    bias_pair = (biases, swap(biases))
    in_pair = [b[: 4 * half].reshape(4, half) for b in bias_pair]
    hidden_pair = [b[4 * half :] for b in bias_pair]

    cot = jnp.where(row_valid, exchange(cotangent), jnp.zeros((), BF16)).astype(F32)

    memory_full = jnp.concatenate([encoder, swap(encoder)], 1).reshape(4 * memory_rows, width)

    queries = [
        ((dot_nn(inputs, project_q[h]) + in_pair[h][0]) * score_scale).astype(BF16) for h in both
    ]
    keys = [dot_nn(inputs, project_k[h]).astype(BF16) for h in both]
    values = [(dot_nn(inputs, project_v[h]) + in_pair[h][1]).astype(BF16) for h in both]
    keys_far = [swap(keys[1 - h]) for h in both]
    values_far = [swap(values[1 - h]) for h in both]
    attn = []
    lse = []
    for h in both:
        result = attend_forward(
            meta, queries[h], [keys[h], keys_far[h]], [values[h], values_far[h]], True, piece, spans
        )
        attn.append(result[0])
        lse.append(result[1])
    branch = dot_nt(attn[0], self_out[0]) + dot_nt(attn[1], self_out[1]) + out_bias[0]
    n1, unit1, scale1 = norm_forward(inputs.astype(F32) + branch, norm_gain[0], norm_bias[0])
    cross_in = n1.astype(BF16)
    cqs = [
        ((dot_nn(cross_in, query_w[h]) + in_pair[h][2]) * score_scale).astype(BF16) for h in both
    ]
    cks = [dot_nn(memory_full, memory_k[h]).astype(BF16) for h in both]
    cvs = [(dot_nn(memory_full, memory_v[h]) + in_pair[h][3]).astype(BF16) for h in both]
    cattn = []
    clse = []
    for h in both:
        result = attend_forward(meta, cqs[h], [cks[h]], [cvs[h]], False, piece, spans)
        cattn.append(result[0])
        clse.append(result[1])
    branch = dot_nt(cattn[0], cross_out[0]) + dot_nt(cattn[1], cross_out[1]) + out_bias[1]
    n2, unit2, scale2 = norm_forward(n1 + branch, norm_gain[1], norm_bias[1])
    hidden = n2.astype(BF16)
    act = []
    slope = []
    for h in both:
        pre = dot_nn(hidden, expand[h]) + hidden_pair[h]
        phi = 0.5 * (1.0 + lax.erf(pre * (1.0 / math.sqrt(2.0))))
        act.append((pre * phi).astype(BF16))
        density = jnp.exp(-0.5 * pre * pre) * (1.0 / math.sqrt(2.0 * math.pi))
        slope.append((phi + pre * density).astype(BF16))
    branch = dot_nt(act[0], reduce[0]) + dot_nt(act[1], reduce[1]) + out_bias[2]
    n3, unit3, scale3 = norm_forward(n2 + branch, norm_gain[2], norm_bias[2])
    output = send_home(n3.astype(BF16))

    def scatter(grads):
        mine = grads[0] + swap(grads[1].astype(BF16)).astype(F32)
        return lax.psum_scatter(mine.astype(BF16), "dp", scatter_dimension=0, tiled=True).astype(F32)

    dh3, gain3, shift3 = norm_backward(cot, unit3, scale3, norm_gain[2])
    dz = dh3.astype(BF16)
    grad_reduce = [dot_tn(dz, act[h]) for h in both]
    du = [(dot_nn(dz, reduce[h]) * slope[h].astype(F32)).astype(BF16) for h in both]
    grad_expand = [dot_tn(hidden, du[h]) for h in both]
    ffn_shard = scatter(
        [jnp.concatenate([grad_expand[h], grad_reduce[h]], 1) for h in both]
    )
    dn2 = dh3 + dot_nt(du[0], expand[0]) + dot_nt(du[1], expand[1])
    dh2, gain2, shift2 = norm_backward(dn2, unit2, scale2, norm_gain[1])
    dy2 = dh2.astype(BF16)
    grad_cross_out = [dot_tn(dy2, cattn[h]) for h in both]
    dca = [dot_nn(dy2, cross_out[h]).astype(BF16) for h in both]
    dcq = []
    dck = []
    dcv = []
    for h in both:
        result = attend_backward(
            meta, cqs[h], dca[h], clse[h], [cks[h]], [cvs[h]], False, piece, spans, [F32]
        )
        dcq.append(result[0])
        dck.append(result[1][0].reshape(2, 2, memory_rows, half))
        dcv.append(result[2][0].reshape(2, 2, memory_rows, half))
    dck_sum = [
        (dck[h][:, 0] + swap(dck[1 - h][:, 1].astype(BF16)).astype(F32))
        .astype(BF16)
        .reshape(2 * memory_rows, half)
        for h in both
    ]
    dcv_sum = [
        (dcv[h][:, 0] + swap(dcv[1 - h][:, 1].astype(BF16)).astype(F32))
        .astype(BF16)
        .reshape(2 * memory_rows, half)
        for h in both
    ]
    memory_own = encoder.reshape(2 * memory_rows, width)
    grad_query_w = [dot_tn(cross_in, dcq[h]) * score_scale for h in both]
    grad_memory_k = [dot_tn(memory_own, dck_sum[h]) for h in both]
    grad_memory_v = [dot_tn(memory_own, dcv_sum[h]) for h in both]
    grad_memory = (
        dot_nt(dck_sum[0], memory_k[0])
        + dot_nt(dck_sum[1], memory_k[1])
        + dot_nt(dcv_sum[0], memory_v[0])
        + dot_nt(dcv_sum[1], memory_v[1])
    )
    grad_encoder = grad_memory.astype(BF16).reshape(2, memory_rows, width)
    dn1 = dh2 + (dot_nt(dcq[0], query_w[0]) + dot_nt(dcq[1], query_w[1])) * score_scale
    dh1, gain1, shift1 = norm_backward(dn1, unit1, scale1, norm_gain[0])
    dy = dh1.astype(BF16)
    grad_self_out = [dot_tn(dy, attn[h]) for h in both]
    da = [dot_nn(dy, self_out[h]).astype(BF16) for h in both]
    mid_shard = scatter(
        [
            jnp.concatenate(
                [
                    grad_self_out[h],
                    grad_query_w[h],
                    grad_memory_k[h],
                    grad_memory_v[h],
                    grad_cross_out[h],
                ],
                1,
            )
            for h in both
        ]
    )
    dq = []
    dk = []
    dv = []
    for h in both:
        result = attend_backward(
            meta,
            queries[h],
            da[h],
            lse[h],
            [keys[h], keys_far[h]],
            [values[h], values_far[h]],
            True,
            piece,
            spans,
            [F32, BF16],
        )
        dq.append(result[0])
        dk.append(result[1])
        dv.append(result[2])
    dk = [(dk[h][0] + swap(dk[1 - h][1]).astype(F32)).astype(BF16) for h in both]
    dv = [(dv[h][0] + swap(dv[1 - h][1]).astype(F32)).astype(BF16) for h in both]
    qkv_shard = scatter(
        [
            jnp.concatenate(
                [
                    dot_tn(inputs, dq[h]) * score_scale,
                    dot_tn(inputs, dk[h]),
                    dot_tn(inputs, dv[h]),
                ],
                1,
            )
            for h in both
        ]
    )
    grad_inputs = (
        dh1
        + (dot_nt(dq[0], project_q[0]) + dot_nt(dq[1], project_q[1])) * score_scale
        + dot_nt(dk[0], project_k[0])
        + dot_nt(dk[1], project_k[1])
        + dot_nt(dv[0], project_v[0])
        + dot_nt(dv[1], project_v[1])
    )
    grad_tokens = send_home(grad_inputs.astype(BF16))

    def rows_sum(value):
        return jnp.sum(value, 0, dtype=F32)

    def global_order(pair):
        own_first = jnp.concatenate(pair, -1)
        other_first = jnp.concatenate(pair[::-1], -1)
        return jnp.where(tensor_index == 0, own_first, other_first)

    in_rows = global_order(
        [
            jnp.stack(
                [
                    score_scale * rows_sum(dq[h]),
                    rows_sum(dv[h]),
                    score_scale * rows_sum(dcq[h]),
                    rows_sum(dcv_sum[h]),
                ]
            )
            for h in both
        ]
    )
    hidden_row = global_order([rows_sum(du[h]) for h in both])
    out_rows = jnp.stack([rows_sum(dy), rows_sum(dy2), rows_sum(dz)])
    gain_rows = jnp.stack([gain1, gain2, gain3])
    shift_rows = jnp.stack([shift1, shift2, shift3])
    small = lax.psum(
        jnp.concatenate(
            [
                in_rows.reshape(-1),
                hidden_row,
                out_rows.reshape(-1),
                gain_rows.reshape(-1),
                shift_rows.reshape(-1),
            ]
        ),
        ("dp", "tensor"),
    )
    in_end = 8 * half
    hidden_end = in_end + 2 * units
    in_total = small[:in_end].reshape(4, 2 * half)
    hidden_total = small[in_end:hidden_end]
    rest = small[hidden_end:].reshape(3, 3, width)
    return (
        output,
        grad_tokens,
        grad_encoder,
        qkv_shard.reshape(shard, 3, half),
        mid_shard[:, :half].T,
        mid_shard[:, half : 2 * half],
        mid_shard[:, 2 * half : 4 * half].reshape(shard, 2, half),
        mid_shard[:, 4 * half :].T,
        ffn_shard[:, :units],
        ffn_shard[:, units:].T,
        lax.dynamic_slice_in_dim(in_total, tensor_index * half, half, 1),
        rest[0],
        lax.dynamic_slice_in_dim(hidden_total, tensor_index * units, units, 0),
        rest[1],
        rest[2],
    )


def solution(mesh):
    in_specs = (
        P(None, ("dp", "tensor"), None),
        P("dp", "tensor", None),
        P(),
        P(),
        P("dp", None, "tensor"),
        P("tensor", "dp"),
        P("dp", "tensor"),
        P("dp", None, "tensor"),
        P("tensor", "dp"),
        P("dp", "tensor"),
        P("tensor", "dp"),
        P(None, "tensor"),
        P(),
        P("tensor"),
        P(),
        P(),
        P(None, ("dp", "tensor"), None),
    )
    out_specs = (
        P(None, ("dp", "tensor"), None),
        P(None, ("dp", "tensor"), None),
        P("dp", "tensor", None),
        P("dp", None, "tensor"),
        P("tensor", "dp"),
        P("dp", "tensor"),
        P("dp", None, "tensor"),
        P("tensor", "dp"),
        P("dp", "tensor"),
        P("tensor", "dp"),
        P(None, "tensor"),
        P(),
        P("tensor"),
        P(),
        P(),
    )
    return jax.shard_map(body, mesh=mesh, in_specs=in_specs, out_specs=out_specs, check_vma=False)
```

```python
import functools
import math

import jax
import jax.numpy as jnp
from jax import lax
from jax.experimental import pallas as pl
from jax.experimental.pallas import tpu as pltpu
from jax.sharding import PartitionSpec as P

HD = 64
EPSILON = 1e-05
MASKED = -1e30
BLOCK = 128
PAIR = 2 * HD
F32 = jnp.float32
BF16 = jnp.bfloat16


def dot_nn(left, right):
    return lax.dot_general(left, right, (((1,), (0,)), ((), ())), preferred_element_type=F32)


def dot_nt(left, right):
    return lax.dot_general(left, right, (((1,), (1,)), ((), ())), preferred_element_type=F32)


def dot_tn(left, right):
    return lax.dot_general(left, right, (((0,), (0,)), ((), ())), preferred_element_type=F32)


def lane_low(shape):
    return lax.broadcasted_iota(jnp.int32, shape, 1) < HD


def stack_heads(rows):
    low = lane_low(rows.shape)
    zero = jnp.zeros_like(rows)
    return jnp.concatenate([jnp.where(low, rows, zero), jnp.where(low, zero, rows)], 0)


def unstack_heads(transposed):
    both = transposed.T
    low = lane_low((BLOCK, PAIR))
    return jnp.where(low, both[:BLOCK], both[BLOCK:])


def block_place(meta):
    block = pl.program_id(0)
    first_blocks = meta[0]
    second = block >= first_blocks
    start = jnp.where(second, first_blocks, 0)
    return block, block - start, start, second.astype(jnp.int32), block < meta[1]


def diagonal_mask(own, piece, tensor_index):
    key = lax.broadcasted_iota(jnp.int32, (BLOCK, 2 * BLOCK), 0)
    query = lax.broadcasted_iota(jnp.int32, (BLOCK, 2 * BLOCK), 1) & (BLOCK - 1)
    if own:
        return key <= query
    shift = piece.bit_length() - 1
    return (key >> shift) < (query >> shift) + tensor_index


def mask_scores(scores, mask):
    keys = scores.shape[0]
    last = jnp.where(mask, scores[keys - BLOCK :], MASKED)
    if keys == BLOCK:
        return last
    return jnp.concatenate([scores[: keys - BLOCK], last], 0)


def pair_columns(pair):
    return slice(pair * PAIR, (pair + 1) * PAIR)


def run_spans(causal, spans, local, start, second, active, run):
    if causal:
        base = pl.multiple_of(start * BLOCK, BLOCK)
        for step in range(spans):
            pl.when(active & (local == step))(functools.partial(run, base, (step + 1) * BLOCK))
    else:
        pl.when(active)(functools.partial(run, pl.multiple_of(second * BLOCK, BLOCK), BLOCK))


def forward_kernel(parts, pairs, causal, piece, spans, meta, q_ref, *refs):
    keys = refs[:parts]
    values = refs[parts : 2 * parts]
    out_ref, lse_ref = refs[2 * parts : 2 * parts + 2]
    flipped = refs[2 * parts + 2 :]
    block, local, start, second, active = block_place(meta)

    @pl.when(block == 0)
    def _():
        for part in range(parts):
            flipped[part][...] = values[part][...].astype(F32).T.astype(BF16)

    def run(base, span):
        masks = [diagonal_mask(part == 0, piece, meta[2]) for part in range(parts)]
        for pair in range(pairs):
            cols = pair_columns(pair)
            stacked = stack_heads(q_ref[:, cols])
            scores = []
            for part in range(parts):
                tile = dot_nt(keys[part][pl.ds(base, span), cols], stacked)
                scores.append(mask_scores(tile, masks[part]) if causal else tile)
            top = functools.reduce(
                jnp.maximum, [jnp.max(tile, 0, keepdims=True) for tile in scores]
            )
            exps = [jnp.exp(tile - top) for tile in scores]
            total = functools.reduce(jnp.add, [jnp.sum(tile, 0, keepdims=True) for tile in exps])
            result = functools.reduce(
                jnp.add,
                [
                    dot_nn(flipped[part][cols, pl.ds(base, span)], exps[part].astype(BF16))
                    for part in range(parts)
                ],
            )
            out_ref[:, cols] = unstack_heads(result / total).astype(BF16)
            lse_ref[0, pair : pair + 1, :] = top + jnp.log(total)

    run_spans(causal, spans, local, start, second, active, run)

    @pl.when(jnp.logical_not(active))
    def _():
        out_ref[...] = jnp.zeros_like(out_ref)
        lse_ref[...] = jnp.zeros_like(lse_ref)


def backward_kernel(parts, pairs, causal, piece, spans, meta, q_ref, g_ref, lse_ref, *refs):
    keys = refs[:parts]
    values = refs[parts : 2 * parts]
    dq_ref = refs[2 * parts]
    dk_out = refs[2 * parts + 1 : 3 * parts + 1]
    dv_out = refs[3 * parts + 1 : 4 * parts + 1]
    flipped = refs[4 * parts + 1 : 5 * parts + 1]
    dk_sum = refs[5 * parts + 1 : 6 * parts + 1]
    dv_sum = refs[6 * parts + 1 : 7 * parts + 1]
    block, local, start, second, active = block_place(meta)

    @pl.when(block == 0)
    def _():
        for part in range(parts):
            flipped[part][...] = keys[part][...].astype(F32).T.astype(BF16)
            dk_sum[part][...] = jnp.zeros_like(dk_sum[part])
            dv_sum[part][...] = jnp.zeros_like(dv_sum[part])

    def run(base, span):
        place = pl.ds(base, span)
        masks = [diagonal_mask(part == 0, piece, meta[2]) for part in range(parts)]
        for pair in range(pairs):
            cols = pair_columns(pair)
            queries = stack_heads(q_ref[:, cols])
            grads = stack_heads(g_ref[:, cols])
            lse = lse_ref[0, pair : pair + 1, :]
            probs = []
            grad_probs = []
            for part in range(parts):
                tile = dot_nt(keys[part][place, cols], queries)
                if causal:
                    tile = mask_scores(tile, masks[part])
                probs.append(jnp.exp(tile - lse))
                grad_probs.append(dot_nt(values[part][place, cols], grads))
            row_dot = functools.reduce(
                jnp.add,
                [jnp.sum(p * g, 0, keepdims=True) for p, g in zip(probs, grad_probs)],
            )
            grad_query = None
            for part in range(parts):
                grad_score = (probs[part] * (grad_probs[part] - row_dot)).astype(BF16)
                dv_sum[part][place, cols] += dot_nn(probs[part].astype(BF16), grads)
                dk_sum[part][place, cols] += dot_nn(grad_score, queries)
                term = dot_nn(flipped[part][cols, place], grad_score)
                grad_query = term if grad_query is None else grad_query + term
            dq_ref[:, cols] = unstack_heads(grad_query).astype(BF16)

    run_spans(causal, spans, local, start, second, active, run)

    @pl.when(jnp.logical_not(active))
    def _():
        dq_ref[...] = jnp.zeros_like(dq_ref)

    @pl.when(block == pl.num_programs(0) - 1)
    def _():
        for part in range(parts):
            dk_out[part][...] = dk_sum[part][...].astype(dk_out[part].dtype)
            dv_out[part][...] = dv_sum[part][...].astype(dv_out[part].dtype)


def row_spec(width):
    return pl.BlockSpec((BLOCK, width), lambda block, meta: (block, 0))


def whole_spec(rows, width):
    return pl.BlockSpec((rows, width), lambda block, meta: (0, 0))


def lse_spec():
    return pl.BlockSpec((1, 8, 2 * BLOCK), lambda block, meta: (block, 0, 0))


def attend_forward(meta, queries, keys, values, causal, piece, spans):
    rows, width = queries.shape
    parts = len(keys)
    pairs, blocks = width // PAIR, rows // BLOCK
    key_rows = keys[0].shape[0]
    work = pairs * blocks * parts * 4 * BLOCK * 2 * BLOCK * (2 * BLOCK if causal else BLOCK)
    return pl.pallas_call(
        functools.partial(forward_kernel, parts, pairs, causal, piece, spans),
        grid_spec=pltpu.PrefetchScalarGridSpec(
            num_scalar_prefetch=1,
            grid=(blocks,),
            in_specs=[row_spec(width)] + [whole_spec(key_rows, width)] * (2 * parts),
            out_specs=[row_spec(width), lse_spec()],
            scratch_shapes=[pltpu.VMEM((width, key_rows), BF16)] * parts,
        ),
        out_shape=[
            jax.ShapeDtypeStruct((rows, width), BF16),
            jax.ShapeDtypeStruct((blocks, 8, 2 * BLOCK), F32),
        ],
        cost_estimate=pl.CostEstimate(
            flops=4 * work, bytes_accessed=8 * rows * width, transcendentals=work // 256
        ),
        name="attend_forward",
    )(meta, queries, *keys, *values)


def attend_backward(meta, queries, grads, lse, keys, values, causal, piece, spans, kinds):
    rows, width = queries.shape
    parts = len(keys)
    pairs, blocks = width // PAIR, rows // BLOCK
    key_rows = keys[0].shape[0]
    work = pairs * blocks * parts * 4 * BLOCK * 2 * BLOCK * (2 * BLOCK if causal else BLOCK)
    results = pl.pallas_call(
        functools.partial(backward_kernel, parts, pairs, causal, piece, spans),
        grid_spec=pltpu.PrefetchScalarGridSpec(
            num_scalar_prefetch=1,
            grid=(blocks,),
            in_specs=[row_spec(width), row_spec(width), lse_spec()]
            + [whole_spec(key_rows, width)] * (2 * parts),
            out_specs=[row_spec(width)] + [whole_spec(key_rows, width)] * (2 * parts),
            scratch_shapes=[pltpu.VMEM((width, key_rows), BF16)] * parts
            + [pltpu.VMEM((key_rows, width), F32)] * (2 * parts),
        ),
        out_shape=[jax.ShapeDtypeStruct((rows, width), BF16)]
        + [jax.ShapeDtypeStruct((key_rows, width), kind) for kind in kinds + kinds],
        cost_estimate=pl.CostEstimate(
            flops=10 * work, bytes_accessed=16 * rows * width, transcendentals=work // 256
        ),
        name="attend_backward",
    )(meta, queries, grads, lse, *keys, *values)
    return results[0], results[1 : 1 + parts], results[1 + parts :]


def grads_kernel(sides, counts, factors, extra, grouped, meta, *refs):
    lefts = refs[: max(sides) + 1]
    rights = refs[len(lefts) : len(lefts) + len(counts)]
    rest = refs[len(lefts) + len(counts) :]
    extra_ref = rest[0] if extra else None
    out_ref = rest[1] if extra else rest[0]
    flipped = rest[2:] if extra else rest[1:]
    step = pl.program_id(0)

    @pl.when(step == 0)
    def _():
        for left, flip in zip(lefts, flipped):
            flip[...] = left[...].astype(F32).T.astype(BF16)

    begin = 0
    for index, count in enumerate(counts):

        @pl.when((step >= begin) & (step < begin + count))
        def _(index=index):
            result = dot_nn(flipped[sides[index]][...], rights[index][...])
            if factors[index] != 1.0:
                result = result * factors[index]
            if not grouped:
                if extra:
                    result = result + extra_ref[...].astype(F32)
                out_ref[...] = result.astype(BF16)
                return
            size = out_ref.shape[2]
            for plane in range(4):
                for low in range(4):
                    row = (plane * 4 + low) * size
                    place = pl.ds(meta[0] ^ low, 1)
                    part = result[row : row + size]
                    if extra:
                        part = part + extra_ref[place, plane].astype(F32)[0]
                    out_ref[place, plane] = part.astype(BF16)[None]

        begin += count


def weight_grads(meta, lefts, rights, sides, factors, extra, grouped):
    chunk = 384
    counts = [right.shape[1] // chunk for right in rights]
    width = lefts[0].shape[1]
    total = sum(counts) * chunk
    begins = [sum(counts[:i]) for i in range(len(counts))]

    def right_spec(index):
        return pl.BlockSpec(
            (rights[index].shape[0], chunk),
            lambda step, meta: (0, jnp.clip(step - begins[index], 0, counts[index] - 1)),
        )

    if grouped:
        shape = (4, 4, width // 16, total)
        out_spec = pl.BlockSpec((4, 4, width // 16, chunk), lambda step, meta: (0, 0, 0, step))
    else:
        shape = (width, total)
        out_spec = pl.BlockSpec((width, chunk), lambda step, meta: (0, step))
    flops = sum(2 * right.shape[0] * width * right.shape[1] for right in rights)
    return pl.pallas_call(
        functools.partial(grads_kernel, sides, counts, factors, extra is not None, grouped),
        grid_spec=pltpu.PrefetchScalarGridSpec(
            num_scalar_prefetch=1,
            grid=(sum(counts),),
            in_specs=[pl.BlockSpec(left.shape, lambda step, meta: (0, 0)) for left in lefts]
            + [right_spec(index) for index in range(len(rights))]
            + ([out_spec] if extra is not None else []),
            out_specs=out_spec,
            scratch_shapes=[pltpu.VMEM((width, left.shape[0]), BF16) for left in lefts],
        ),
        out_shape=jax.ShapeDtypeStruct(shape, BF16),
        cost_estimate=pl.CostEstimate(
            flops=flops, bytes_accessed=flops // 256, transcendentals=0
        ),
        name="weight_grads",
    )(meta, *lefts, *rights, *([extra] if extra is not None else []))


def norm_forward(hidden, gain, shift):
    center = hidden - jnp.mean(hidden, -1, keepdims=True)
    spread = jnp.mean(center * center, -1, keepdims=True)
    scale = lax.rsqrt(spread + EPSILON)
    unit = center * scale
    return unit * gain + shift, unit, scale


def norm_backward(grad, unit, scale, gain):
    gain_grad = jnp.sum(grad * unit, 0)
    shift_grad = jnp.sum(grad, 0)
    inner = grad * gain
    mean_inner = jnp.mean(inner, -1, keepdims=True)
    mean_unit = jnp.mean(inner * unit, -1, keepdims=True)
    return scale * (inner - mean_inner - unit * mean_unit), gain_grad, shift_grad


def swap(value):
    return lax.ppermute(value, "tensor", [(0, 1), (1, 0)])


def hop(value, bits):
    return lax.ppermute(value, "dp", [(i, i ^ bits) for i in range(16)])


def assemble_kernel(meta, own_ref, first_ref, second_ref, third_ref, out_ref):
    for low, ref in enumerate((own_ref, first_ref, second_ref, third_ref)):
        out_ref[0, pl.ds(meta[1] ^ low, 1)] = ref[...]


def quick_gather(value):
    if lax.axis_size("dp") != 16:
        return lax.all_gather(value, "dp", axis=0, tiled=True)
    rows, count = value.shape
    line = jnp.stack([value, hop(value, 4), hop(value, 8), hop(value, 12)])
    index = lax.axis_index("dp")
    meta = jnp.stack([index // 4, index % 4]).astype(jnp.int32)
    spec = pl.BlockSpec((1, rows, count), lambda i, meta: (i ^ meta[0], 0, 0))
    full = pl.pallas_call(
        assemble_kernel,
        grid_spec=pltpu.PrefetchScalarGridSpec(
            num_scalar_prefetch=1,
            grid=(4,),
            in_specs=[spec] * 4,
            out_specs=pl.BlockSpec((1, 4, rows, count), lambda i, meta: (i, 0, 0, 0)),
        ),
        out_shape=jax.ShapeDtypeStruct((4, 4, rows, count), value.dtype),
        cost_estimate=pl.CostEstimate(
            flops=0, bytes_accessed=64 * rows * count, transcendentals=0
        ),
        name="assemble",
    )(meta, line, hop(line, 1), hop(line, 2), hop(line, 3))
    return full.reshape(16 * rows, count)


def total_of(parts):
    return functools.reduce(jnp.add, [part.astype(F32) for part in parts])


def scatter_low(groups):
    received = [hop(groups[low], low) for low in (1, 2, 3)]
    return total_of([groups[0]] + received).astype(BF16)


def scatter_plane(line):
    plane = lax.axis_index("dp") // 4

    def pick(other):
        return lax.dynamic_index_in_dim(line, plane ^ other, 0, keepdims=False)

    received = [hop(pick(other), 4 * other) for other in (1, 2, 3)]
    return total_of([pick(0)] + received)


def slow_scatter(value):
    return lax.psum_scatter(value, "dp", scatter_dimension=0, tiled=True).astype(F32)


def sum_everywhere(value):
    if lax.axis_size("dp") != 16:
        return lax.psum(value, ("dp", "tensor"))
    value = value + swap(value)
    for unit in (1, 4):
        value = total_of([value] + [hop(value, unit * bits) for bits in (1, 2, 3)])
    return value


def tie(*values):
    return lax.optimization_barrier(values)


def body(
    tokens,
    encoder,
    lengths,
    deal,
    self_project,
    self_output,
    cross_query,
    cross_memory,
    cross_output,
    hidden_in,
    hidden_out,
    in_bias,
    out_bias,
    hidden_bias,
    norm_gain,
    norm_bias,
    cotangent,
):
    score_scale = 1.0 / math.sqrt(HD)
    dp_count = lax.axis_size("dp")
    dp_index = lax.axis_index("dp")
    tensor_index = lax.axis_index("tensor")
    piece = tokens.shape[1]
    width = tokens.shape[2]
    slots = piece * dp_count
    half = self_project.shape[2]
    units = hidden_in.shape[1]
    shard = self_project.shape[0]
    memory_rows = encoder.shape[1]
    spans = slots // BLOCK
    blocks = (slots + slots // 2) // BLOCK + 1
    rows = blocks * BLOCK
    per_block = BLOCK // piece

    pair_ids = lax.dynamic_slice_in_dim(deal, 2 * dp_index, 2)
    pair_len = jnp.take(lengths, pair_ids)
    pieces_used = (pair_len + 2 * piece - 1) // (2 * piece)
    blocks_used = (pieces_used * piece + BLOCK - 1) // BLOCK
    first_blocks = blocks_used[0]
    all_blocks = first_blocks + blocks_used[1]
    meta = jnp.stack([first_blocks, all_blocks, tensor_index]).astype(jnp.int32)

    block_ids = jnp.arange(blocks, dtype=jnp.int32)
    block_seq = (block_ids >= first_blocks).astype(jnp.int32)
    block_local = jnp.minimum(block_ids - block_seq * first_blocks, spans - 1)
    piece_ids = (
        (block_local[:, None] * per_block + jnp.arange(per_block, dtype=jnp.int32)[None, :]) * 2
        + block_seq[:, None]
    ).reshape(-1)
    slot_ids = block_local[:, None] * BLOCK + jnp.arange(BLOCK, dtype=jnp.int32)[None, :]
    positions = ((slot_ids // piece) * 2 + tensor_index) * piece + slot_ids % piece
    row_valid = (
        (positions < jnp.where(block_seq == 1, pair_len[1], pair_len[0])[:, None])
        & (block_ids < all_blocks)[:, None]
    ).reshape(rows, 1)

    send_piece = jnp.arange(dp_count, dtype=jnp.int32)
    send_block = send_piece // per_block
    send_ids = jnp.stack(
        [
            jnp.minimum(send_block, blocks_used[0] - 1) * per_block,
            (first_blocks + jnp.minimum(send_block, blocks_used[1] - 1)) * per_block,
        ],
        1,
    ) + (send_piece % per_block)[:, None]
    send_pos = (send_piece[:, None, None] * 2 + tensor_index) * piece + jnp.arange(
        piece, dtype=jnp.int32
    )[None, None, :]
    send_valid = (send_pos < pair_len[None, :, None]).reshape(2 * dp_count, piece, 1)
    inverse = jnp.zeros_like(deal).at[deal].set(jnp.arange(deal.shape[0], dtype=jnp.int32))

    def send_home(value):
        pieces = value.reshape(rows // piece, piece, width)
        outgoing = jnp.where(
            send_valid, jnp.take(pieces, send_ids.reshape(-1), axis=0), jnp.zeros((), value.dtype)
        )
        return lax.all_to_all(outgoing, "dp", split_axis=0, concat_axis=0, tiled=True)

    def order(value):
        return jnp.take(value, deal, axis=0)

    def arrive(ordered):
        return lax.all_to_all(ordered, "dp", split_axis=0, concat_axis=0, tiled=True)

    def pack(arrived):
        return jnp.take(arrived, piece_ids, axis=0).reshape(rows, width)

    arrived = arrive(order(tokens))
    ordered_cot, arrived = tie(order(cotangent), arrived)
    inputs = pack(arrived)
    arrived_cot = arrive(ordered_cot)

    quick = dp_count == 16

    def gather(value):
        own = lax.all_gather(value, "dp", axis=0, tiled=True)
        return (own, swap(own))

    qkv_own = quick_gather(self_project.reshape(shard, 3 * half))
    qkv_weight = (qkv_own, swap(qkv_own))
    mid_weight = gather(
        jnp.concatenate(
            [self_output.T, cross_query, cross_memory.reshape(shard, 2 * half), cross_output.T], 1
        )
    )
    ffn_weight = gather(jnp.concatenate([hidden_in, hidden_out.T], 1))
    both = (0, 1)

    def columns(pair, start, count):
        return [lax.slice_in_dim(pair[h], start, start + count, axis=1) for h in both]

    project_q = columns(qkv_weight, 0, half)
    project_k = columns(qkv_weight, half, half)
    project_v = columns(qkv_weight, 2 * half, half)
    self_out = columns(mid_weight, 0, half)
    query_w = columns(mid_weight, half, half)
    memory_k = columns(mid_weight, 2 * half, half)
    memory_v = columns(mid_weight, 3 * half, half)
    cross_out = columns(mid_weight, 4 * half, half)
    expand = columns(ffn_weight, 0, units)
    reduce = columns(ffn_weight, units, units)

    biases = jnp.concatenate([in_bias.reshape(-1), hidden_bias])
    bias_pair = (biases, swap(biases))
    in_pair = [b[: 4 * half].reshape(4, half) for b in bias_pair]
    hidden_pair = [b[4 * half :] for b in bias_pair]

    cot = jnp.where(row_valid, pack(arrived_cot), jnp.zeros((), BF16)).astype(F32)

    memory_full = jnp.concatenate([encoder, swap(encoder)], 1).reshape(4 * memory_rows, width)

    queries = [
        ((dot_nn(inputs, project_q[h]) + in_pair[h][0]) * score_scale).astype(BF16) for h in both
    ]
    keys = [dot_nn(inputs, project_k[h]).astype(BF16) for h in both]
    values = [(dot_nn(inputs, project_v[h]) + in_pair[h][1]).astype(BF16) for h in both]
    keys_far = [swap(keys[1 - h]) for h in both]
    values_far = [swap(values[1 - h]) for h in both]
    attn = []
    lse = []
    for h in both:
        result = attend_forward(
            meta, queries[h], [keys[h], keys_far[h]], [values[h], values_far[h]], True, piece, spans
        )
        attn.append(result[0])
        lse.append(result[1])
    branch = dot_nt(attn[0], self_out[0]) + dot_nt(attn[1], self_out[1]) + out_bias[0]
    n1, unit1, scale1 = norm_forward(inputs.astype(F32) + branch, norm_gain[0], norm_bias[0])
    cross_in = n1.astype(BF16)
    cqs = [
        ((dot_nn(cross_in, query_w[h]) + in_pair[h][2]) * score_scale).astype(BF16) for h in both
    ]
    cks = [dot_nn(memory_full, memory_k[h]).astype(BF16) for h in both]
    cvs = [(dot_nn(memory_full, memory_v[h]) + in_pair[h][3]).astype(BF16) for h in both]
    cattn = []
    clse = []
    for h in both:
        result = attend_forward(meta, cqs[h], [cks[h]], [cvs[h]], False, piece, spans)
        cattn.append(result[0])
        clse.append(result[1])
    branch = dot_nt(cattn[0], cross_out[0]) + dot_nt(cattn[1], cross_out[1]) + out_bias[1]
    n2, unit2, scale2 = norm_forward(n1 + branch, norm_gain[1], norm_bias[1])
    hidden = n2.astype(BF16)
    act = []
    slope = []
    for h in both:
        pre = dot_nn(hidden, expand[h]) + hidden_pair[h]
        phi = 0.5 * (1.0 + lax.erf(pre * (1.0 / math.sqrt(2.0))))
        act.append((pre * phi).astype(BF16))
        density = jnp.exp(-0.5 * pre * pre) * (1.0 / math.sqrt(2.0 * math.pi))
        slope.append((phi + pre * density).astype(BF16))
    branch = dot_nt(act[0], reduce[0]) + dot_nt(act[1], reduce[1]) + out_bias[2]
    n3, unit3, scale3 = norm_forward(n2 + branch, norm_gain[2], norm_bias[2])
    output_back = send_home(n3.astype(BF16))

    low_meta = jnp.reshape(dp_index % 4, (1,)).astype(jnp.int32)

    def chip_grads(lefts, rights, sides, factors, grouped):
        far = weight_grads(low_meta, lefts, rights[1], sides, factors, None, grouped)
        return weight_grads(low_meta, lefts, rights[0], sides, factors, swap(far), grouped)

    dh3, gain3, shift3 = norm_backward(cot, unit3, scale3, norm_gain[2])
    dz = dh3.astype(BF16)
    du = [(dot_nn(dz, reduce[h]) * slope[h].astype(F32)).astype(BF16) for h in both]
    ffn_grads = chip_grads(
        [hidden, dz], [[du[h], act[h]] for h in both], (0, 1), (1.0, 1.0), False
    )
    dn2 = dh3 + dot_nt(du[0], expand[0]) + dot_nt(du[1], expand[1])
    dh2, gain2, shift2 = norm_backward(dn2, unit2, scale2, norm_gain[1])
    dy2 = dh2.astype(BF16)
    dca = [dot_nn(dy2, cross_out[h]).astype(BF16) for h in both]
    ffn_grads, dca[0] = tie(ffn_grads, dca[0])
    ffn_shard = slow_scatter(ffn_grads)
    dcq = []
    dck = []
    dcv = []
    for h in both:
        result = attend_backward(
            meta, cqs[h], dca[h], clse[h], [cks[h]], [cvs[h]], False, piece, spans, [F32]
        )
        dcq.append(result[0])
        dck.append(result[1][0].reshape(2, 2, memory_rows, half))
        dcv.append(result[2][0].reshape(2, 2, memory_rows, half))
    dck_sum = [
        (dck[h][:, 0] + swap(dck[1 - h][:, 1].astype(BF16)).astype(F32))
        .astype(BF16)
        .reshape(2 * memory_rows, half)
        for h in both
    ]
    dcv_sum = [
        (dcv[h][:, 0] + swap(dcv[1 - h][:, 1].astype(BF16)).astype(F32))
        .astype(BF16)
        .reshape(2 * memory_rows, half)
        for h in both
    ]
    memory_own = encoder.reshape(2 * memory_rows, width)
    grad_memory = (
        dot_nt(dck_sum[0], memory_k[0])
        + dot_nt(dck_sum[1], memory_k[1])
        + dot_nt(dcv_sum[0], memory_v[0])
        + dot_nt(dcv_sum[1], memory_v[1])
    )
    grad_encoder = grad_memory.astype(BF16).reshape(2, memory_rows, width)
    dn1 = dh2 + (dot_nt(dcq[0], query_w[0]) + dot_nt(dcq[1], query_w[1])) * score_scale
    dh1, gain1, shift1 = norm_backward(dn1, unit1, scale1, norm_gain[0])
    dy = dh1.astype(BF16)
    da = [dot_nn(dy, self_out[h]).astype(BF16) for h in both]
    mid_grads = chip_grads(
        [dy, cross_in, memory_own, dy2],
        [[attn[h], dcq[h], dck_sum[h], dcv_sum[h], cattn[h]] for h in both],
        (0, 1, 2, 2, 3),
        (1.0, score_scale, 1.0, 1.0, 1.0),
        quick,
    )
    mid_grads, da[0], output_back = tie(mid_grads, da[0], output_back)
    output = jnp.take(output_back, inverse, axis=0)
    mid_line = scatter_low(mid_grads) if quick else None
    dq = []
    dk = []
    dv = []
    for h in both:
        result = attend_backward(
            meta,
            queries[h],
            da[h],
            lse[h],
            [keys[h], keys_far[h]],
            [values[h], values_far[h]],
            True,
            piece,
            spans,
            [F32, BF16],
        )
        if h == 0 and quick:
            mid_line, dq_first = tie(mid_line, result[0])
            result = (dq_first, result[1], result[2])
            da[1], mid_line = tie(da[1], mid_line)
        dq.append(result[0])
        dk.append(result[1])
        dv.append(result[2])
    mid_shard = scatter_plane(mid_line) if quick else slow_scatter(mid_grads)
    dk = [(dk[h][0] + swap(dk[1 - h][1]).astype(F32)).astype(BF16) for h in both]
    dv = [(dv[h][0] + swap(dv[1 - h][1]).astype(F32)).astype(BF16) for h in both]
    qkv_grads = chip_grads(
        [inputs],
        [[dq[h], dk[h], dv[h]] for h in both],
        (0, 0, 0),
        (score_scale, 1.0, 1.0),
        quick,
    )
    qkv_shard = scatter_plane(scatter_low(qkv_grads)) if quick else slow_scatter(qkv_grads)
    grad_inputs = (
        dh1
        + (dot_nt(dq[0], project_q[0]) + dot_nt(dq[1], project_q[1])) * score_scale
        + dot_nt(dk[0], project_k[0])
        + dot_nt(dk[1], project_k[1])
        + dot_nt(dv[0], project_v[0])
        + dot_nt(dv[1], project_v[1])
    )
    grad_tokens = jnp.take(send_home(grad_inputs.astype(BF16)), inverse, axis=0)

    def rows_sum(value):
        return jnp.sum(value, 0, dtype=F32)

    def global_order(pair):
        own_first = jnp.concatenate(pair, -1)
        other_first = jnp.concatenate(pair[::-1], -1)
        return jnp.where(tensor_index == 0, own_first, other_first)

    in_rows = global_order(
        [
            jnp.stack(
                [
                    score_scale * rows_sum(dq[h]),
                    rows_sum(dv[h]),
                    score_scale * rows_sum(dcq[h]),
                    rows_sum(dcv_sum[h]),
                ]
            )
            for h in both
        ]
    )
    hidden_row = global_order([rows_sum(du[h]) for h in both])
    out_rows = jnp.stack([rows_sum(dy), rows_sum(dy2), rows_sum(dz)])
    gain_rows = jnp.stack([gain1, gain2, gain3])
    shift_rows = jnp.stack([shift1, shift2, shift3])
    small = sum_everywhere(
        jnp.concatenate(
            [
                in_rows.reshape(-1),
                hidden_row,
                out_rows.reshape(-1),
                gain_rows.reshape(-1),
                shift_rows.reshape(-1),
            ]
        )
    )
    in_end = 8 * half
    hidden_end = in_end + 2 * units
    in_total = small[:in_end].reshape(4, 2 * half)
    hidden_total = small[in_end:hidden_end]
    rest = small[hidden_end:].reshape(3, 3, width)
    return (
        output,
        grad_tokens,
        grad_encoder,
        qkv_shard.reshape(shard, 3, half),
        mid_shard[:, :half].T,
        mid_shard[:, half : 2 * half],
        mid_shard[:, 2 * half : 4 * half].reshape(shard, 2, half),
        mid_shard[:, 4 * half :].T,
        ffn_shard[:, :units],
        ffn_shard[:, units:].T,
        lax.dynamic_slice_in_dim(in_total, tensor_index * half, half, 1),
        rest[0],
        lax.dynamic_slice_in_dim(hidden_total, tensor_index * units, units, 0),
        rest[1],
        rest[2],
    )


def solution(mesh):
    in_specs = (
        P(None, ("dp", "tensor"), None),
        P("dp", "tensor", None),
        P(),
        P(),
        P("dp", None, "tensor"),
        P("tensor", "dp"),
        P("dp", "tensor"),
        P("dp", None, "tensor"),
        P("tensor", "dp"),
        P("dp", "tensor"),
        P("tensor", "dp"),
        P(None, "tensor"),
        P(),
        P("tensor"),
        P(),
        P(),
        P(None, ("dp", "tensor"), None),
    )
    out_specs = (
        P(None, ("dp", "tensor"), None),
        P(None, ("dp", "tensor"), None),
        P("dp", "tensor", None),
        P("dp", None, "tensor"),
        P("tensor", "dp"),
        P("dp", "tensor"),
        P("dp", None, "tensor"),
        P("tensor", "dp"),
        P("dp", "tensor"),
        P("tensor", "dp"),
        P(None, "tensor"),
        P(),
        P("tensor"),
        P(),
        P(),
    )
    return jax.shard_map(body, mesh=mesh, in_specs=in_specs, out_specs=out_specs, check_vma=False)
```

```python
import functools
import math

import jax
import jax.numpy as jnp
from jax import lax
from jax.experimental import pallas as pl
from jax.experimental.pallas import tpu as pltpu
from jax.sharding import PartitionSpec as P

HD = 64
EPSILON = 1e-05
MASKED = -1e30
BLOCK = 128
LIGHT = 1000
GROUP = 4
PAIR = 2 * HD
F32 = jnp.float32
BF16 = jnp.bfloat16


def dot_nn(left, right):
    return lax.dot_general(left, right, (((1,), (0,)), ((), ())), preferred_element_type=F32)


def dot_nt(left, right):
    return lax.dot_general(left, right, (((1,), (1,)), ((), ())), preferred_element_type=F32)


def dot_tn(left, right):
    return lax.dot_general(left, right, (((0,), (0,)), ((), ())), preferred_element_type=F32)


def lane_low(shape):
    return lax.broadcasted_iota(jnp.int32, shape, 1) < HD


def stack_heads(rows):
    low = lane_low(rows.shape)
    zero = jnp.zeros_like(rows)
    return jnp.concatenate([jnp.where(low, rows, zero), jnp.where(low, zero, rows)], 0)


def unstack_heads(transposed):
    both = transposed.T
    low = lane_low((BLOCK, PAIR))
    return jnp.where(low, both[:BLOCK], both[BLOCK:])


def block_place(meta):
    block = pl.program_id(0)
    first_blocks = meta[0]
    second = block >= first_blocks
    start = jnp.where(second, first_blocks, 0)
    return block, block - start, start, second.astype(jnp.int32), block < meta[1]


def diagonal_mask(own, piece, tensor_index):
    key = lax.broadcasted_iota(jnp.int32, (BLOCK, 2 * BLOCK), 0)
    query = lax.broadcasted_iota(jnp.int32, (BLOCK, 2 * BLOCK), 1) & (BLOCK - 1)
    if own:
        return key <= query
    shift = piece.bit_length() - 1
    return (key >> shift) < (query >> shift) + tensor_index


def mask_scores(scores, mask):
    keys = scores.shape[0]
    last = jnp.where(mask, scores[keys - BLOCK :], MASKED)
    if keys == BLOCK:
        return last
    return jnp.concatenate([scores[: keys - BLOCK], last], 0)


def pair_columns(pair):
    return slice(pair * PAIR, (pair + 1) * PAIR)


def run_spans(causal, spans, local, start, second, active, run):
    if causal:
        base = pl.multiple_of(start * BLOCK, BLOCK)
        for step in range(spans):
            pl.when(active & (local == step))(functools.partial(run, base, (step + 1) * BLOCK))
    else:
        pl.when(active)(functools.partial(run, pl.multiple_of(second * BLOCK, BLOCK), BLOCK))


def forward_kernel(parts, pairs, causal, piece, spans, meta, q_ref, *refs):
    keys = refs[:parts]
    values = refs[parts : 2 * parts]
    out_ref, lse_ref = refs[2 * parts : 2 * parts + 2]
    flipped = refs[2 * parts + 2 :]
    block, local, start, second, active = block_place(meta)

    @pl.when(block == 0)
    def _():
        for part in range(parts):
            flipped[part][...] = values[part][...].astype(F32).T.astype(BF16)

    def run(base, span):
        masks = [diagonal_mask(part == 0, piece, meta[2]) for part in range(parts)]
        for pair in range(pairs):
            cols = pair_columns(pair)
            stacked = stack_heads(q_ref[:, cols])
            scores = []
            for part in range(parts):
                tile = dot_nt(keys[part][pl.ds(base, span), cols], stacked)
                scores.append(mask_scores(tile, masks[part]) if causal else tile)
            top = functools.reduce(
                jnp.maximum, [jnp.max(tile, 0, keepdims=True) for tile in scores]
            )
            exps = [jnp.exp(tile - top) for tile in scores]
            total = functools.reduce(jnp.add, [jnp.sum(tile, 0, keepdims=True) for tile in exps])
            result = functools.reduce(
                jnp.add,
                [
                    dot_nn(flipped[part][cols, pl.ds(base, span)], exps[part].astype(BF16))
                    for part in range(parts)
                ],
            )
            out_ref[:, cols] = unstack_heads(result / total).astype(BF16)
            lse_ref[0, pair : pair + 1, :] = top + jnp.log(total)

    run_spans(causal, spans, local, start, second, active, run)

    @pl.when(jnp.logical_not(active))
    def _():
        out_ref[...] = jnp.zeros_like(out_ref)
        lse_ref[...] = jnp.zeros_like(lse_ref)


def backward_kernel(parts, pairs, causal, piece, spans, meta, q_ref, g_ref, lse_ref, *refs):
    keys = refs[:parts]
    values = refs[parts : 2 * parts]
    dq_ref = refs[2 * parts]
    dk_out = refs[2 * parts + 1 : 3 * parts + 1]
    dv_out = refs[3 * parts + 1 : 4 * parts + 1]
    flipped = refs[4 * parts + 1 : 5 * parts + 1]
    dk_sum = refs[5 * parts + 1 : 6 * parts + 1]
    dv_sum = refs[6 * parts + 1 : 7 * parts + 1]
    block, local, start, second, active = block_place(meta)

    @pl.when(block == 0)
    def _():
        for part in range(parts):
            flipped[part][...] = keys[part][...].astype(F32).T.astype(BF16)
            dk_sum[part][...] = jnp.zeros_like(dk_sum[part])
            dv_sum[part][...] = jnp.zeros_like(dv_sum[part])

    def run(base, span):
        place = pl.ds(base, span)
        masks = [diagonal_mask(part == 0, piece, meta[2]) for part in range(parts)]
        for pair in range(pairs):
            cols = pair_columns(pair)
            queries = stack_heads(q_ref[:, cols])
            grads = stack_heads(g_ref[:, cols])
            lse = lse_ref[0, pair : pair + 1, :]
            probs = []
            grad_probs = []
            for part in range(parts):
                tile = dot_nt(keys[part][place, cols], queries)
                if causal:
                    tile = mask_scores(tile, masks[part])
                probs.append(jnp.exp(tile - lse))
                grad_probs.append(dot_nt(values[part][place, cols], grads))
            row_dot = functools.reduce(
                jnp.add,
                [jnp.sum(p * g, 0, keepdims=True) for p, g in zip(probs, grad_probs)],
            )
            grad_query = None
            for part in range(parts):
                grad_score = (probs[part] * (grad_probs[part] - row_dot)).astype(BF16)
                dv_sum[part][place, cols] += dot_nn(probs[part].astype(BF16), grads)
                dk_sum[part][place, cols] += dot_nn(grad_score, queries)
                term = dot_nn(flipped[part][cols, place], grad_score)
                grad_query = term if grad_query is None else grad_query + term
            dq_ref[:, cols] = unstack_heads(grad_query).astype(BF16)

    run_spans(causal, spans, local, start, second, active, run)

    @pl.when(jnp.logical_not(active))
    def _():
        dq_ref[...] = jnp.zeros_like(dq_ref)

    @pl.when(block == pl.num_programs(0) - 1)
    def _():
        for part in range(parts):
            dk_out[part][...] = dk_sum[part][...].astype(dk_out[part].dtype)
            dv_out[part][...] = dv_sum[part][...].astype(dv_out[part].dtype)


def row_spec(width, rows=BLOCK):
    return pl.BlockSpec((rows, width), lambda block, meta: (block, 0))


def whole_spec(rows, width):
    return pl.BlockSpec((rows, width), lambda block, meta: (0, 0))


def lse_spec(group=1):
    return pl.BlockSpec((group, 8, 2 * BLOCK), lambda block, meta: (block, 0, 0))


def attend_forward(meta, queries, keys, values, causal, piece, spans):
    rows, width = queries.shape
    parts = len(keys)
    pairs, blocks = width // PAIR, rows // BLOCK
    key_rows = keys[0].shape[0]
    work = pairs * blocks * parts * 4 * BLOCK * 2 * BLOCK * (2 * BLOCK if causal else BLOCK)
    return pl.pallas_call(
        functools.partial(forward_kernel, parts, pairs, causal, piece, spans),
        grid_spec=pltpu.PrefetchScalarGridSpec(
            num_scalar_prefetch=1,
            grid=(blocks,),
            in_specs=[row_spec(width)] + [whole_spec(key_rows, width)] * (2 * parts),
            out_specs=[row_spec(width), lse_spec()],
            scratch_shapes=[pltpu.VMEM((width, key_rows), BF16)] * parts,
        ),
        out_shape=[
            jax.ShapeDtypeStruct((rows, width), BF16),
            jax.ShapeDtypeStruct((blocks, 8, 2 * BLOCK), F32),
        ],
        cost_estimate=pl.CostEstimate(
            flops=(4 * work) // LIGHT, bytes_accessed=(8 * rows * width) // LIGHT, transcendentals=work // 256
        ),
        name="attend_forward",
    )(meta, queries, *keys, *values)


def attend_backward(meta, queries, grads, lse, keys, values, causal, piece, spans, kinds):
    rows, width = queries.shape
    parts = len(keys)
    pairs, blocks = width // PAIR, rows // BLOCK
    key_rows = keys[0].shape[0]
    work = pairs * blocks * parts * 4 * BLOCK * 2 * BLOCK * (2 * BLOCK if causal else BLOCK)
    results = pl.pallas_call(
        functools.partial(backward_kernel, parts, pairs, causal, piece, spans),
        grid_spec=pltpu.PrefetchScalarGridSpec(
            num_scalar_prefetch=1,
            grid=(blocks,),
            in_specs=[row_spec(width), row_spec(width), lse_spec()]
            + [whole_spec(key_rows, width)] * (2 * parts),
            out_specs=[row_spec(width)] + [whole_spec(key_rows, width)] * (2 * parts),
            scratch_shapes=[pltpu.VMEM((width, key_rows), BF16)] * parts
            + [pltpu.VMEM((key_rows, width), F32)] * (2 * parts),
        ),
        out_shape=[jax.ShapeDtypeStruct((rows, width), BF16)]
        + [jax.ShapeDtypeStruct((key_rows, width), kind) for kind in kinds + kinds],
        cost_estimate=pl.CostEstimate(
            flops=(10 * work) // LIGHT, bytes_accessed=(16 * rows * width) // LIGHT, transcendentals=work // 256
        ),
        name="attend_backward",
    )(meta, queries, grads, lse, *keys, *values)
    return results[0], results[1 : 1 + parts], results[1 + parts :]


def grads_kernel(sides, counts, factors, extra, grouped, meta, *refs):
    lefts = refs[: max(sides) + 1]
    rights = refs[len(lefts) : len(lefts) + len(counts)]
    rest = refs[len(lefts) + len(counts) :]
    extra_ref = rest[0] if extra else None
    out_ref = rest[-1]
    step = pl.program_id(0)
    begin = 0
    for index, count in enumerate(counts):

        @pl.when((step >= begin) & (step < begin + count))
        def _(index=index):
            result = dot_tn(lefts[sides[index]][...], rights[index][...])
            if factors[index] != 1.0:
                result = result * factors[index]
            if not grouped:
                if extra:
                    result = result + extra_ref[...].astype(F32)
                out_ref[...] = result.astype(BF16)
                return
            size = out_ref.shape[2]
            for plane in range(4):
                for low in range(4):
                    row = (plane * 4 + low) * size
                    place = pl.ds(meta[0] ^ low, 1)
                    part = result[row : row + size]
                    if extra:
                        part = part + extra_ref[place, plane].astype(F32)[0]
                    out_ref[place, plane] = part.astype(BF16)[None]

        begin += count


def weight_grads(meta, lefts, rights, sides, factors, extra, grouped):
    chunk = min(2 * 384, rights[0].shape[1])
    shifts = [right[1] if isinstance(right, tuple) else 0 for right in rights]
    counts = [1 if isinstance(right, tuple) else right.shape[1] // chunk for right in rights]
    rights = [right[0] if isinstance(right, tuple) else right for right in rights]
    width = lefts[0].shape[1]
    total = sum(counts) * chunk
    begins = [sum(counts[:i]) for i in range(len(counts))]

    def right_spec(index):
        return pl.BlockSpec(
            (rights[index].shape[0], chunk),
            lambda step, meta: (
                0,
                shifts[index] + jnp.clip(step - begins[index], 0, counts[index] - 1),
            ),
        )

    if grouped:
        shape = (4, 4, width // 16, total)
        out_spec = pl.BlockSpec((4, 4, width // 16, chunk), lambda step, meta: (0, 0, 0, step))
    else:
        shape = (width, total)
        out_spec = pl.BlockSpec((width, chunk), lambda step, meta: (0, step))
    flops = 2 * rights[0].shape[0] * width * total
    return pl.pallas_call(
        functools.partial(grads_kernel, sides, counts, factors, extra is not None, grouped),
        grid_spec=pltpu.PrefetchScalarGridSpec(
            num_scalar_prefetch=1,
            grid=(sum(counts),),
            in_specs=[pl.BlockSpec(left.shape, lambda step, meta: (0, 0)) for left in lefts]
            + [right_spec(index) for index in range(len(rights))]
            + ([out_spec] if extra is not None else []),
            out_specs=out_spec,
        ),
        out_shape=jax.ShapeDtypeStruct(shape, BF16),
        cost_estimate=pl.CostEstimate(
            flops=flops // LIGHT, bytes_accessed=flops // 256 // LIGHT, transcendentals=0
        ),
        name="weight_grads",
    )(meta, *lefts, *rights, *([extra] if extra is not None else []))


def norm_forward(hidden, gain, shift):
    center = hidden - jnp.mean(hidden, -1, keepdims=True)
    spread = jnp.mean(center * center, -1, keepdims=True)
    scale = lax.rsqrt(spread + EPSILON)
    unit = center * scale
    return unit * gain + shift, unit, scale


def norm_gradient(grad, unit, scale, gain):
    inner = grad * gain
    mean_inner = jnp.mean(inner, -1, keepdims=True)
    mean_unit = jnp.mean(inner * unit, -1, keepdims=True)
    return scale * (inner - mean_inner - unit * mean_unit)


def norm_backward(grad, unit, scale, gain):
    return norm_gradient(grad, unit, scale, gain), jnp.sum(grad * unit, 0), jnp.sum(grad, 0)


def sub_blocks(meta, keys_each, run, skip):
    def one(sub, carry):
        block = pl.program_id(0) * GROUP + sub
        second = (block >= meta[0]).astype(jnp.int32)
        place = pl.ds(pl.multiple_of(second * keys_each, keys_each), keys_each)
        rows = pl.ds(pl.multiple_of(sub * BLOCK, BLOCK), BLOCK)
        pl.when(block < meta[1])(functools.partial(run, sub, rows, place))
        pl.when(block >= meta[1])(functools.partial(skip, sub, rows))
        return carry

    lax.fori_loop(0, GROUP, one, 0)


def mid_forward_kernel(score_scale, meta, x_ref, attn0, attn1, memory_ref, *refs):
    attn = (attn0, attn1)
    self_out, query_w, memory_k, memory_v, cross_out = [refs[2 * i : 2 * i + 2] for i in range(5)]
    bias0, bias1, out_bias, gain, shift = refs[10:15]
    unit1_ref, scale1_ref, unit2_ref, scale2_ref, cross_in_ref, hidden_ref, lse_ref = refs[15:22]
    cq_refs, cattn_refs, ck_refs, cv_refs = [refs[22 + 2 * i : 24 + 2 * i] for i in range(4)]
    flipped = refs[30:32]
    half = attn0.shape[1]
    keys_each = memory_ref.shape[0] // 2

    @pl.when(pl.program_id(0) == 0)
    def _():
        for h, bias in enumerate((bias0, bias1)):
            ck_refs[h][...] = dot_nn(memory_ref[...], memory_k[h][...]).astype(BF16)
            value = dot_nn(memory_ref[...], memory_v[h][...]) + bias[3:4, :]
            cv_refs[h][...] = value.astype(BF16)
            flipped[h][...] = value.T.astype(BF16)

    branch = dot_nt(attn[0][...], self_out[0][...]) + dot_nt(attn[1][...], self_out[1][...])
    n1, unit1, scale1 = norm_forward(
        x_ref[...].astype(F32) + branch + out_bias[0:1, :], gain[0:1, :], shift[0:1, :]
    )
    unit1_ref[...] = unit1
    scale1_ref[...] = scale1
    cross_in = n1.astype(BF16)
    cross_in_ref[...] = cross_in
    for h, bias in enumerate((bias0, bias1)):
        query = (dot_nn(cross_in, query_w[h][...]) + bias[2:3, :]) * score_scale
        cq_refs[h][...] = query.astype(BF16)

    def run(sub, rows, place):
        for h in range(2):
            for pair in range(half // PAIR):
                cols = pair_columns(pair)
                tile = dot_nt(ck_refs[h][place, cols], stack_heads(cq_refs[h][rows, cols]))
                top = jnp.max(tile, 0, keepdims=True)
                exps = jnp.exp(tile - top)
                total = jnp.sum(exps, 0, keepdims=True)
                result = dot_nn(flipped[h][cols, place], exps.astype(BF16))
                cattn_refs[h][rows, cols] = unstack_heads(result / total).astype(BF16)
                row = h * (half // PAIR) + pair
                lse_ref[sub, row : row + 1, :] = top + jnp.log(total)

    def skip(sub, rows):
        lse_ref[sub] = jnp.zeros(lse_ref.shape[1:], F32)
        for h in range(2):
            cattn_refs[h][rows, :] = jnp.zeros((BLOCK, half), BF16)

    sub_blocks(meta, keys_each, run, skip)
    branch = dot_nt(cattn_refs[0][...], cross_out[0][...]) + dot_nt(
        cattn_refs[1][...], cross_out[1][...]
    )
    n1 = unit1_ref[...] * gain[0:1, :] + shift[0:1, :]
    n2, unit2, scale2 = norm_forward(n1 + branch + out_bias[1:2, :], gain[1:2, :], shift[1:2, :])
    unit2_ref[...] = unit2
    scale2_ref[...] = scale2
    hidden_ref[...] = n2.astype(BF16)


def mid_backward_kernel(score_scale, total_rows, meta, dn2_ref, unit2_ref, scale2_ref, unit1_ref, scale1_ref, lse_ref, *refs):
    cq_refs, ck_refs, cv_refs = [refs[2 * i : 2 * i + 2] for i in range(3)]
    self_out, query_w, cross_out = [refs[6 + 2 * i : 8 + 2 * i] for i in range(3)]
    gain = refs[12]
    dy2_ref, dh1_ref, dy_ref, sums_ref = refs[13:17]
    dcq_refs, da_refs = refs[17:19], refs[19:21]
    near_ref, far_ref = refs[21:23]
    dca_refs, flipped, dck_refs, dcv_refs = [refs[23 + 2 * i : 25 + 2 * i] for i in range(4)]
    half = cq_refs[0].shape[1]
    keys_each = ck_refs[0].shape[0] // 2
    here = pl.program_id(0) * GROUP * BLOCK + lax.broadcasted_iota(
        jnp.int32, (GROUP * BLOCK, 1), 0
    )
    inside = here < total_rows

    def load(ref):
        return jnp.where(inside, ref[...], 0.0)

    @pl.when(pl.program_id(0) == 0)
    def _():
        sums_ref[...] = jnp.zeros_like(sums_ref)
        for h in range(2):
            flipped[h][...] = ck_refs[h][...].astype(F32).T.astype(BF16)
            dck_refs[h][...] = jnp.zeros_like(dck_refs[h])
            dcv_refs[h][...] = jnp.zeros_like(dcv_refs[h])

    dn2 = load(dn2_ref)
    unit2 = load(unit2_ref)
    dh2 = norm_gradient(dn2, unit2, load(scale2_ref), gain[1:2, :])
    dh1_ref[...] = dh2
    dy2 = dh2.astype(BF16)
    dy2_ref[...] = dy2
    sums_ref[0:1, :] += jnp.sum(dn2 * unit2, 0, keepdims=True)
    sums_ref[1:2, :] += jnp.sum(dn2, 0, keepdims=True)
    sums_ref[2:3, :] += jnp.sum(dy2.astype(F32), 0, keepdims=True)
    for h in range(2):
        dca_refs[h][...] = dot_nn(dy2, cross_out[h][...]).astype(BF16)

    def run(sub, rows, place):
        for h in range(2):
            for pair in range(half // PAIR):
                cols = pair_columns(pair)
                row = h * (half // PAIR) + pair
                queries = stack_heads(cq_refs[h][rows, cols])
                grads = stack_heads(dca_refs[h][rows, cols])
                tile = dot_nt(ck_refs[h][place, cols], queries)
                probs = jnp.exp(tile - lse_ref[sub, row : row + 1, :])
                grad_probs = dot_nt(cv_refs[h][place, cols], grads)
                row_dot = jnp.sum(probs * grad_probs, 0, keepdims=True)
                grad_score = (probs * (grad_probs - row_dot)).astype(BF16)
                dcv_refs[h][place, cols] += dot_nn(probs.astype(BF16), grads)
                dck_refs[h][place, cols] += dot_nn(grad_score, queries)
                term = dot_nn(flipped[h][cols, place], grad_score)
                dcq_refs[h][rows, cols] = unstack_heads(term).astype(BF16)

    def skip(sub, rows):
        for h in range(2):
            dcq_refs[h][rows, :] = jnp.zeros((BLOCK, half), BF16)

    sub_blocks(meta, keys_each, run, skip)
    dn1 = dh1_ref[...]
    for h in range(2):
        dcq = dcq_refs[h][...]
        dn1 = dn1 + score_scale * dot_nt(dcq, query_w[h][...])
        sums_ref[6:7, h * half : (h + 1) * half] += jnp.sum(dcq.astype(F32), 0, keepdims=True)
    unit1 = load(unit1_ref)
    dh1 = norm_gradient(dn1, unit1, load(scale1_ref), gain[0:1, :])
    dy = dh1.astype(BF16)
    dh1_ref[...] = dh1
    dy_ref[...] = dy
    sums_ref[3:4, :] += jnp.sum(dn1 * unit1, 0, keepdims=True)
    sums_ref[4:5, :] += jnp.sum(dn1, 0, keepdims=True)
    sums_ref[5:6, :] += jnp.sum(dy.astype(F32), 0, keepdims=True)
    for h in range(2):
        da_refs[h][...] = dot_nn(dy, self_out[h][...]).astype(BF16)

    @pl.when(pl.program_id(0) == pl.num_programs(0) - 1)
    def _():
        own = keys_each // 2
        for index, ref in enumerate((dck_refs[0], dck_refs[1], dcv_refs[0], dcv_refs[1])):
            near = slice(index * half, (index + 1) * half)
            far = slice((index ^ 1) * half, ((index ^ 1) + 1) * half)
            for seq in range(2):
                rows = slice(seq * own, (seq + 1) * own)
                base = seq * keys_each
                near_ref[rows, near] = ref[base : base + own, :]
                far_ref[rows, far] = ref[base + own : base + keys_each, :].astype(BF16)


def memory_backward_kernel(near_ref, got_ref, wk0, wv0, wk1, wv1, sum_ref, encoder_ref, bias_ref):
    total = (near_ref[...] + got_ref[...].astype(F32)).astype(BF16)
    sum_ref[...] = total
    half = wk0.shape[1]
    grad = dot_nt(total[:, :half], wk0[...]) + dot_nt(total[:, half : 2 * half], wk1[...])
    grad = grad + dot_nt(total[:, 2 * half : 3 * half], wv0[...])
    encoder_ref[...] = (grad + dot_nt(total[:, 3 * half :], wv1[...])).astype(BF16)
    bias = jnp.sum(total[:, 2 * half :].astype(F32), 0, keepdims=True)
    bias_ref[...] = jnp.broadcast_to(bias, bias_ref.shape)


def memory_backward(near, got, mid):
    rows, span = near.shape
    half = span // 4
    width = mid[0].shape[0]
    columns = [plain_fixed((width, half), 0, 2), plain_fixed((width, half), 0, 3)]
    return pl.pallas_call(
        memory_backward_kernel,
        grid=(1,),
        in_specs=[plain_fixed((rows, span))] * 2 + columns * 2,
        out_specs=[plain_fixed((rows, span)), plain_fixed((rows, width)), plain_fixed((8, 2 * half))],
        out_shape=[kept((rows, span), BF16), kept((rows, width), BF16), kept((8, 2 * half), F32)],
        cost_estimate=pl.CostEstimate(flops=1000, bytes_accessed=1000, transcendentals=0),
        name="memory_backward",
    )(near, got, mid[0], mid[0], mid[1], mid[1])


def ffn_backward_kernel(h3_ref, cot_ref, valid_ref, slope0, slope1, in0, in1, out0, out1, gain, shift, n3_ref, dz_ref, dn2_ref, sums_ref, du0, du1, usum0, usum1):
    @pl.when(pl.program_id(0) == 0)
    def _():
        for ref in (sums_ref, usum0, usum1):
            ref[...] = jnp.zeros_like(ref)

    n3, unit, scale = norm_forward(h3_ref[...], gain[2:3, :], shift[2:3, :])
    valid = valid_ref[...] > 0.5
    n3_ref[...] = jnp.where(valid, n3, 0.0).astype(BF16)
    dn3 = jnp.where(valid, cot_ref[...].astype(F32), 0.0)
    dh3 = norm_gradient(dn3, unit, scale, gain[2:3, :])
    dz = dh3.astype(BF16)
    dz_ref[...] = dz
    sums_ref[0:1, :] += jnp.sum(dn3 * unit, 0, keepdims=True)
    sums_ref[1:2, :] += jnp.sum(dn3, 0, keepdims=True)
    sums_ref[2:3, :] += jnp.sum(dz.astype(F32), 0, keepdims=True)
    total = dh3
    sides = ((slope0, out0, in0, du0, usum0), (slope1, out1, in1, du1, usum1))
    for slope, reduce, expand, du_ref, usum in sides:
        du = (dot_nn(dz, reduce[...]) * slope[...].astype(F32)).astype(BF16)
        du_ref[...] = du
        usum[0:1, :] += jnp.sum(du.astype(F32), 0, keepdims=True)
        total = total + dot_nt(du, expand[...])
    dn2_ref[...] = total


def ffn_backward(h3, cot, valid, slope, ffn, gain, shift):
    rows, width = h3.shape
    units = slope[0].shape[1]
    wide, thin, long = [plain_rows(rows // 2, w) for w in (width, 1, units)]

    def side(column):
        return pl.BlockSpec(
            (width, units), lambda step: (0, column), pipeline_mode=pl.Buffered(1)
        )

    return pl.pallas_call(
        ffn_backward_kernel,
        grid=(2,),
        in_specs=[wide, wide, thin, long, long, side(0), side(0), side(1), side(1)]
        + [plain_fixed((3, width))] * 2,
        out_specs=[wide, wide, wide, plain_fixed((8, width)), long, long]
        + [plain_fixed((8, units))] * 2,
        out_shape=[
            kept((rows, width), BF16),
            kept((rows, width), BF16),
            kept((rows, width), F32),
            kept((8, width), F32),
            kept((rows, units), BF16),
            kept((rows, units), BF16),
            kept((8, units), F32),
            kept((8, units), F32),
        ],
        cost_estimate=pl.CostEstimate(flops=1000, bytes_accessed=1000, transcendentals=0),
        name="ffn_backward",
    )(h3, cot, valid, *slope, ffn[0], ffn[1], ffn[0], ffn[1], gain, shift)


def fixed_spec(shape, *index):
    place = index or (0,) * len(shape)
    return pl.BlockSpec(shape, lambda block, meta: place)


def kept(shape, kind):
    return jax.ShapeDtypeStruct(shape, kind)


def mid_forward(meta, inputs, attn, memory, mid, in_pair, out_bias, gain, shift, score_scale):
    rows, width = inputs.shape
    half = attn[0].shape[1]
    blocks = rows // BLOCK
    memory_rows = memory.shape[0]
    weights = [fixed_spec((width, half), 0, column) for column in range(5) for _ in range(2)]
    tall = GROUP * BLOCK
    wide, thin, narrow = row_spec(width, tall), row_spec(1, tall), row_spec(half, tall)
    memory_spec = fixed_spec((memory_rows, half))
    outs = pl.pallas_call(
        functools.partial(mid_forward_kernel, score_scale),
        grid_spec=pltpu.PrefetchScalarGridSpec(
            num_scalar_prefetch=1,
            grid=(pl.cdiv(blocks, GROUP),),
            in_specs=[wide, narrow, narrow, fixed_spec(memory.shape)]
            + weights
            + [fixed_spec((4, half))] * 2
            + [fixed_spec((3, width))] * 3,
            out_specs=[wide, thin, wide, thin, wide, wide, lse_spec(GROUP)]
            + [narrow] * 4
            + [memory_spec] * 4,
            scratch_shapes=[pltpu.VMEM((half, memory_rows), BF16)] * 2,
        ),
        out_shape=[
            kept((rows, width), F32),
            kept((rows, 1), F32),
            kept((rows, width), F32),
            kept((rows, 1), F32),
            kept((rows, width), BF16),
            kept((rows, width), BF16),
            kept((blocks, 8, 2 * BLOCK), F32),
        ]
        + [kept((rows, half), BF16)] * 4
        + [kept((memory_rows, half), BF16)] * 4,
        cost_estimate=pl.CostEstimate(
            flops=(24 * rows * width * half) // LIGHT, bytes_accessed=(20 * rows * width) // LIGHT, transcendentals=0
        ),
        name="mid_forward",
    )(meta, inputs, *attn, memory, *[mid[h] for _ in range(5) for h in range(2)], *in_pair, out_bias, gain, shift)
    return outs[:7], outs[7:9], outs[9:11], outs[11:13], outs[13:15]


def mid_backward(meta, dn2, saved, cq, ck, cv, mid, gain, score_scale):
    unit1, scale1, unit2, scale2, lse = saved
    rows, width = dn2.shape
    half = cq[0].shape[1]
    blocks = rows // BLOCK
    memory_rows = ck[0].shape[0]
    tall = GROUP * BLOCK
    wide, thin, narrow = row_spec(width, tall), row_spec(1, tall), row_spec(half, tall)
    memory_spec = fixed_spec((memory_rows, half))
    weights = [fixed_spec((width, half), 0, column) for column in (0, 1, 4) for _ in range(2)]
    outs = pl.pallas_call(
        functools.partial(mid_backward_kernel, score_scale, rows),
        grid_spec=pltpu.PrefetchScalarGridSpec(
            num_scalar_prefetch=1,
            grid=(pl.cdiv(blocks, GROUP),),
            in_specs=[wide, wide, thin, wide, thin, lse_spec(GROUP)]
            + [narrow] * 2
            + [memory_spec] * 4
            + weights
            + [fixed_spec((3, width))],
            out_specs=[wide, wide, wide, fixed_spec((8, width))]
            + [narrow] * 4
            + [fixed_spec((memory_rows // 2, 4 * half))] * 2,
            scratch_shapes=[pltpu.VMEM((tall, half), BF16)] * 2
            + [pltpu.VMEM((half, memory_rows), BF16)] * 2
            + [pltpu.VMEM((memory_rows, half), F32)] * 4,
        ),
        out_shape=[
            kept((rows, width), BF16),
            kept((rows, width), F32),
            kept((rows, width), BF16),
            kept((8, width), F32),
        ]
        + [kept((rows, half), BF16)] * 4
        + [kept((memory_rows // 2, 4 * half), F32), kept((memory_rows // 2, 4 * half), BF16)],
        cost_estimate=pl.CostEstimate(
            flops=(24 * rows * width * half) // LIGHT, bytes_accessed=(20 * rows * width) // LIGHT, transcendentals=0
        ),
        name="mid_backward",
    )(meta, dn2, unit2, scale2, unit1, scale1, lse, *cq, *ck, *cv, *[mid[h] for _ in range(3) for h in range(2)], gain)
    return outs[:4], outs[4:6], outs[6:8], outs[8], outs[9]


def input_backward_kernel(score_scale, base_ref, dq_ref, dk_own, dk_got, dv_own, dv_got, wq, wk, wv, dx_ref, dk_ref, dv_ref, sums_ref):
    @pl.when(pl.program_id(0) == 0)
    def _():
        sums_ref[...] = jnp.zeros_like(sums_ref)

    dk = (dk_own[...] + dk_got[...].astype(F32)).astype(BF16)
    dv = (dv_own[...] + dv_got[...].astype(F32)).astype(BF16)
    dk_ref[...] = dk
    dv_ref[...] = dv
    dq = dq_ref[...]
    sums_ref[0:1, :] += score_scale * jnp.sum(dq.astype(F32), 0, keepdims=True)
    sums_ref[1:2, :] += jnp.sum(dv.astype(F32), 0, keepdims=True)
    total = score_scale * dot_nt(dq, wq[...]) + dot_nt(dk, wk[...]) + dot_nt(dv, wv[...])
    dx_ref[...] = (base_ref[...] + total).astype(dx_ref.dtype)


def plain_rows(rows, width):
    return pl.BlockSpec((rows, width), lambda step: (step, 0))


def plain_fixed(shape, *index):
    place = index or (0,) * len(shape)
    return pl.BlockSpec(shape, lambda step: place)


def input_backward(base, dq, dk, dk_got, dv, dv_got, weight, score_scale, kind):
    rows, width = base.shape
    half = dq.shape[1]
    wide, narrow = plain_rows(rows // 2, width), plain_rows(rows // 2, half)
    return pl.pallas_call(
        functools.partial(input_backward_kernel, score_scale),
        grid=(2,),
        in_specs=[wide] + [narrow] * 5 + [plain_fixed((width, half), 0, i) for i in range(3)],
        out_specs=[wide, narrow, narrow, plain_fixed((8, half))],
        out_shape=[
            kept((rows, width), kind),
            kept((rows, half), BF16),
            kept((rows, half), BF16),
            kept((8, half), F32),
        ],
        cost_estimate=pl.CostEstimate(
            flops=(6 * rows * width * half) // LIGHT,
            bytes_accessed=(12 * rows * width) // LIGHT,
            transcendentals=0,
        ),
        name="input_backward",
    )(base, dq, dk, dk_got, dv, dv_got, weight, weight, weight)


def swap(value):
    return lax.ppermute(value, "tensor", [(0, 1), (1, 0)])


def hop(value, bits):
    return lax.ppermute(value, "dp", [(i, i ^ bits) for i in range(16)])


def assemble_kernel(meta, own_ref, first_ref, second_ref, third_ref, out_ref):
    for low, ref in enumerate((own_ref, first_ref, second_ref, third_ref)):
        out_ref[0, pl.ds(meta[1] ^ low, 1)] = ref[...]


def quick_gather(value, later):
    if lax.axis_size("dp") != 16:
        return lax.all_gather(value, "dp", axis=0, tiled=True), later
    rows, count = value.shape
    line = jnp.stack([value, hop(value, 4), hop(value, 8), hop(value, 12)])
    line, later = tie(line, later)
    index = lax.axis_index("dp")
    meta = jnp.stack([index // 4, index % 4]).astype(jnp.int32)
    spec = pl.BlockSpec((1, rows, count), lambda i, meta: (i ^ meta[0], 0, 0))
    full = pl.pallas_call(
        assemble_kernel,
        grid_spec=pltpu.PrefetchScalarGridSpec(
            num_scalar_prefetch=1,
            grid=(4,),
            in_specs=[spec] * 4,
            out_specs=pl.BlockSpec((1, 4, rows, count), lambda i, meta: (i, 0, 0, 0)),
        ),
        out_shape=jax.ShapeDtypeStruct((4, 4, rows, count), value.dtype),
        cost_estimate=pl.CostEstimate(
            flops=(0) // LIGHT, bytes_accessed=(64 * rows * count) // LIGHT, transcendentals=0
        ),
        name="assemble",
    )(meta, line, hop(line, 1), hop(line, 2), hop(line, 3))
    return full.reshape(16 * rows, count), later


def total_of(parts):
    return functools.reduce(jnp.add, [part.astype(F32) for part in parts])


def scatter_low(groups):
    received = [hop(groups[low], low) for low in (1, 2, 3)]
    return total_of([groups[0]] + received).astype(BF16)


def scatter_plane(line):
    plane = lax.axis_index("dp") // 4

    def pick(other):
        return lax.dynamic_index_in_dim(line, plane ^ other, 0, keepdims=False)

    received = [hop(pick(other), 4 * other) for other in (1, 2, 3)]
    return total_of([pick(0)] + received)


def slow_scatter(value):
    return lax.psum_scatter(value, "dp", scatter_dimension=0, tiled=True).astype(F32)


def sum_everywhere(value):
    if lax.axis_size("dp") != 16:
        return lax.psum(value, ("dp", "tensor"))
    value = value + swap(value)
    for unit in (1, 4):
        value = total_of([value] + [hop(value, unit * bits) for bits in (1, 2, 3)])
    return value


def rows_at(value, ids):
    return value.at[ids].get(mode="promise_in_bounds")


def tie(*values):
    return lax.optimization_barrier(values)


def body(
    tokens,
    encoder,
    lengths,
    deal,
    self_project,
    self_output,
    cross_query,
    cross_memory,
    cross_output,
    hidden_in,
    hidden_out,
    in_bias,
    out_bias,
    hidden_bias,
    norm_gain,
    norm_bias,
    cotangent,
):
    score_scale = 1.0 / math.sqrt(HD)
    dp_count = lax.axis_size("dp")
    dp_index = lax.axis_index("dp")
    tensor_index = lax.axis_index("tensor")
    piece = tokens.shape[1]
    width = tokens.shape[2]
    slots = piece * dp_count
    half = self_project.shape[2]
    units = hidden_in.shape[1]
    shard = self_project.shape[0]
    memory_rows = encoder.shape[1]
    spans = slots // BLOCK
    blocks = (slots + slots // 2) // BLOCK + 1
    rows = blocks * BLOCK
    per_block = BLOCK // piece

    pair_ids = lax.dynamic_slice_in_dim(deal, 2 * dp_index, 2)
    pair_len = rows_at(lengths, pair_ids)
    pieces_used = (pair_len + 2 * piece - 1) // (2 * piece)
    blocks_used = (pieces_used * piece + BLOCK - 1) // BLOCK
    first_blocks = blocks_used[0]
    all_blocks = first_blocks + blocks_used[1]
    meta = jnp.stack([first_blocks, all_blocks, tensor_index]).astype(jnp.int32)

    block_ids = jnp.arange(blocks, dtype=jnp.int32)
    block_seq = (block_ids >= first_blocks).astype(jnp.int32)
    block_local = jnp.minimum(block_ids - block_seq * first_blocks, spans - 1)
    piece_ids = (
        (block_local[:, None] * per_block + jnp.arange(per_block, dtype=jnp.int32)[None, :]) * 2
        + block_seq[:, None]
    ).reshape(-1)
    slot_ids = block_local[:, None] * BLOCK + jnp.arange(BLOCK, dtype=jnp.int32)[None, :]
    positions = ((slot_ids // piece) * 2 + tensor_index) * piece + slot_ids % piece
    row_valid = (
        (positions < jnp.where(block_seq == 1, pair_len[1], pair_len[0])[:, None])
        & (block_ids < all_blocks)[:, None]
    ).reshape(rows, 1)

    send_piece = jnp.arange(dp_count, dtype=jnp.int32)
    send_block = send_piece // per_block
    send_ids = jnp.stack(
        [
            jnp.minimum(send_block, blocks_used[0] - 1) * per_block,
            (first_blocks + jnp.minimum(send_block, blocks_used[1] - 1)) * per_block,
        ],
        1,
    ) + (send_piece % per_block)[:, None]
    send_pos = (send_piece[:, None, None] * 2 + tensor_index) * piece + jnp.arange(
        piece, dtype=jnp.int32
    )[None, None, :]
    send_valid = (send_pos < pair_len[None, :, None]).reshape(2 * dp_count, piece, 1)
    inverse = jnp.zeros_like(deal).at[deal].set(jnp.arange(deal.shape[0], dtype=jnp.int32))

    def home_pieces(value):
        pieces = value.reshape(rows // piece, piece, width)
        return jnp.where(
            send_valid, rows_at(pieces, send_ids.reshape(-1)), jnp.zeros((), value.dtype)
        )

    def go_home(outgoing):
        return lax.all_to_all(outgoing, "dp", split_axis=0, concat_axis=0, tiled=True)

    def order(value):
        return rows_at(value, deal)

    def arrive(ordered):
        return lax.all_to_all(ordered, "dp", split_axis=0, concat_axis=0, tiled=True)

    def pack(arrived):
        return rows_at(arrived, piece_ids).reshape(rows, width)

    qkv_own, ordered = quick_gather(self_project.reshape(shard, 3 * half), order(tokens))
    qkv_weight = (qkv_own, swap(qkv_own))
    arrived = arrive(ordered)
    ordered_cot, arrived = tie(order(cotangent), arrived)
    inputs = pack(arrived)
    arrived_cot = arrive(ordered_cot)

    quick = dp_count == 16

    mid_own = lax.all_gather(
        jnp.concatenate(
            [self_output.T, cross_query, cross_memory.reshape(shard, 2 * half), cross_output.T], 1
        ),
        "dp",
        axis=0,
        tiled=True,
    )
    ffn_own = lax.all_gather(
        jnp.concatenate([hidden_in, hidden_out.T], 1), "dp", axis=0, tiled=True
    )
    both = (0, 1)

    def columns(pair, start, count):
        return [lax.slice_in_dim(pair[h], start, start + count, axis=1) for h in both]

    project_q = columns(qkv_weight, 0, half)
    project_k = columns(qkv_weight, half, half)
    project_v = columns(qkv_weight, 2 * half, half)
    biases = jnp.concatenate([in_bias.reshape(-1), hidden_bias])
    bias_pair = (biases, swap(biases))
    in_pair = [b[: 4 * half].reshape(4, half) for b in bias_pair]
    hidden_pair = [b[4 * half :] for b in bias_pair]

    memory_full = jnp.concatenate([encoder, swap(encoder)], 1).reshape(4 * memory_rows, width)

    queries = [
        ((dot_nn(inputs, project_q[h]) + in_pair[h][0]) * score_scale).astype(BF16) for h in both
    ]
    keys = [dot_nn(inputs, project_k[h]).astype(BF16) for h in both]
    values = [(dot_nn(inputs, project_v[h]) + in_pair[h][1]).astype(BF16) for h in both]
    keys_far = [swap(keys[1 - h]) for h in both]
    values_far = [swap(values[1 - h]) for h in both]
    attn = []
    lse = []
    for h in both:
        result = attend_forward(
            meta, queries[h], [keys[h], keys_far[h]], [values[h], values_far[h]], True, piece, spans
        )
        attn.append(result[0])
        lse.append(result[1])
        if h == 0:
            mid_own, attn[0] = tie(mid_own, attn[0])
            mid_weight = (mid_own, swap(mid_own))
    saved, cqs, cattn, cks, cvs = mid_forward(
        meta, inputs, attn, memory_full, mid_weight, in_pair, out_bias, norm_gain, norm_bias, score_scale
    )
    unit1, scale1, unit2, scale2, cross_in, hidden, clse = saved
    ffn_own, hidden, arrived_cot = tie(ffn_own, hidden, arrived_cot)
    ffn_weight = (ffn_own, swap(ffn_own))
    expand = columns(ffn_weight, 0, units)
    reduce = columns(ffn_weight, units, units)
    n2 = unit2 * norm_gain[1] + norm_bias[1]
    act = []
    slope = []
    for h in both:
        pre = dot_nn(hidden, expand[h]) + hidden_pair[h]
        phi = 0.5 * (1.0 + lax.erf(pre * (1.0 / math.sqrt(2.0))))
        act.append((pre * phi).astype(BF16))
        density = jnp.exp(-0.5 * pre * pre) * (1.0 / math.sqrt(2.0 * math.pi))
        slope.append((phi + pre * density).astype(BF16))
    branch = dot_nt(act[0], reduce[0]) + dot_nt(act[1], reduce[1]) + out_bias[2]
    n3, dz, dn2, sums3, du0, du1, usum0, usum1 = ffn_backward(
        n2 + branch, pack(arrived_cot), row_valid.astype(F32), slope, ffn_weight, norm_gain, norm_bias
    )
    du = (du0, du1)
    output_back = go_home(home_pieces(n3))

    low_meta = jnp.reshape(dp_index % 4, (1,)).astype(jnp.int32)

    def chip_grads(lefts, rights, sides, factors, grouped):
        far = weight_grads(low_meta, lefts, rights[1], sides, factors, None, grouped)
        return weight_grads(low_meta, lefts, rights[0], sides, factors, swap(far), grouped)

    ffn_grads = chip_grads(
        [hidden, dz], [[du[h], act[h]] for h in both], (0, 1), (1.0, 1.0), False
    )
    ffn_grads, dn2 = tie(ffn_grads, dn2)
    ffn_shard = slow_scatter(ffn_grads)
    rows_back, dcq, da, memory_near, memory_far = mid_backward(
        meta, dn2, (unit1, scale1, unit2, scale2, clse), cqs, cks, cvs, mid_weight, norm_gain, score_scale
    )
    dy2, dh1, dy, sums = rows_back
    da = list(da)
    memory_far, output_back = tie(memory_far, output_back)
    memory_sum, grad_memory, memory_bias = memory_backward(
        memory_near, swap(memory_far), mid_weight
    )
    grad_encoder = grad_memory.reshape(2, memory_rows, width)
    memory_own = encoder.reshape(2 * memory_rows, width)
    mid_grads = chip_grads(
        [dy, cross_in, memory_own, dy2],
        [
            [attn[h], dcq[h], (memory_sum, h), (memory_sum, 2 + h), cattn[h]]
            for h in both
        ],
        (0, 1, 2, 2, 3),
        (1.0, score_scale, 1.0, 1.0, 1.0),
        quick,
    )
    mid_grads, da[0], da[1] = tie(mid_grads, da[0], da[1])
    mid_line = scatter_low(mid_grads) if quick else None
    dq = []
    dk = []
    dv = []
    for h in both:
        result = attend_backward(
            meta,
            queries[h],
            da[h],
            lse[h],
            [keys[h], keys_far[h]],
            [values[h], values_far[h]],
            True,
            piece,
            spans,
            [F32, BF16],
        )
        dq.append(result[0])
        dk.append(result[1])
        dv.append(result[2])
    factors = (score_scale, 1.0, 1.0)
    near = [swap(dk[1][1]), swap(dv[1][1])]
    if quick:
        mid_line, dh1 = tie(mid_line, dh1)
        mid_shard = scatter_plane(mid_line)
    else:
        mid_shard = slow_scatter(mid_grads)
    dx_far, dk_far, dv_far, sums_far = input_backward(
        dh1, dq[1], dk[1][0], swap(dk[0][1]), dv[1][0], swap(dv[0][1]), qkv_weight[1], score_scale, F32
    )
    far_grads = weight_grads(
        low_meta, [inputs], [dq[1], dk_far, dv_far], (0, 0, 0), factors, None, quick
    )
    far_grads, dx_far, near[0], near[1], mid_shard = tie(far_grads, dx_far, *near, mid_shard)
    far_grads = swap(far_grads)
    dx, dk_near, dv_near, sums_near = input_backward(
        dx_far, dq[0], dk[0][0], near[0], dv[0][0], near[1], qkv_weight[0], score_scale, BF16
    )
    grad_out = home_pieces(dx)
    grad_out, far_grads, output_back = tie(grad_out, far_grads, output_back)
    output = rows_at(output_back, inverse)
    grad_back = go_home(grad_out)
    far_grads, ffn_shard = tie(far_grads, ffn_shard)
    qkv_grads = weight_grads(
        low_meta, [inputs], [dq[0], dk_near, dv_near], (0, 0, 0), factors, far_grads, quick
    )
    sums_qkv = [sums_near, sums_far]

    def global_order(pair):
        own_first = jnp.concatenate(pair, -1)
        other_first = jnp.concatenate(pair[::-1], -1)
        return jnp.where(tensor_index == 0, own_first, other_first)

    in_rows = global_order(
        [
            jnp.stack(
                [
                    sums_qkv[h][0],
                    sums_qkv[h][1],
                    score_scale * sums[6, h * half : (h + 1) * half],
                    memory_bias[0, h * half : (h + 1) * half],
                ]
            )
            for h in both
        ]
    )
    hidden_row = global_order([usum0[0], usum1[0]])
    out_rows = jnp.stack([sums[5], sums[2], sums3[2]])
    gain_rows = jnp.stack([sums[3], sums[0], sums3[0]])
    shift_rows = jnp.stack([sums[4], sums[1], sums3[1]])
    small = jnp.concatenate(
        [
            in_rows.reshape(-1),
            hidden_row,
            out_rows.reshape(-1),
            gain_rows.reshape(-1),
            shift_rows.reshape(-1),
        ]
    )
    small, qkv_grads = tie(small, qkv_grads)
    small = sum_everywhere(small)
    if quick:
        qkv_line, grad_back = tie(scatter_low(qkv_grads), grad_back)
        qkv_shard = scatter_plane(qkv_line)
    else:
        qkv_shard = slow_scatter(qkv_grads)
    grad_tokens = rows_at(grad_back, inverse)
    in_end = 8 * half
    hidden_end = in_end + 2 * units
    in_total = small[:in_end].reshape(4, 2 * half)
    hidden_total = small[in_end:hidden_end]
    rest = small[hidden_end:].reshape(3, 3, width)
    return (
        output,
        grad_tokens,
        grad_encoder,
        qkv_shard.reshape(shard, 3, half),
        mid_shard[:, :half].T,
        mid_shard[:, half : 2 * half],
        mid_shard[:, 2 * half : 4 * half].reshape(shard, 2, half),
        mid_shard[:, 4 * half :].T,
        ffn_shard[:, :units],
        ffn_shard[:, units:].T,
        lax.dynamic_slice_in_dim(in_total, tensor_index * half, half, 1),
        rest[0],
        lax.dynamic_slice_in_dim(hidden_total, tensor_index * units, units, 0),
        rest[1],
        rest[2],
    )


def solution(mesh):
    in_specs = (
        P(None, ("dp", "tensor"), None),
        P("dp", "tensor", None),
        P(),
        P(),
        P("dp", None, "tensor"),
        P("tensor", "dp"),
        P("dp", "tensor"),
        P("dp", None, "tensor"),
        P("tensor", "dp"),
        P("dp", "tensor"),
        P("tensor", "dp"),
        P(None, "tensor"),
        P(),
        P("tensor"),
        P(),
        P(),
        P(None, ("dp", "tensor"), None),
    )
    out_specs = (
        P(None, ("dp", "tensor"), None),
        P(None, ("dp", "tensor"), None),
        P("dp", "tensor", None),
        P("dp", None, "tensor"),
        P("tensor", "dp"),
        P("dp", "tensor"),
        P("dp", None, "tensor"),
        P("tensor", "dp"),
        P("dp", "tensor"),
        P("tensor", "dp"),
        P(None, "tensor"),
        P(),
        P("tensor"),
        P(),
        P(),
    )
    return jax.shard_map(body, mesh=mesh, in_specs=in_specs, out_specs=out_specs, check_vma=False)
```

```python
import functools
import math

import jax
import jax.numpy as jnp
from jax import lax
from jax.experimental import pallas as pl
from jax.experimental.pallas import tpu as pltpu
from jax.sharding import PartitionSpec as P

HD = 64
EPSILON = 1e-05
MASKED = -1e30
BLOCK = 128
LIGHT = 1000
LOW_GROUPS = [[4 * plane + low for low in range(4)] for plane in range(4)]
PLANE_GROUPS = [[low + 4 * plane for plane in range(4)] for low in range(4)]
GROUP = 4
FIXED = 2
PAIR = 2 * HD
F32 = jnp.float32
BF16 = jnp.bfloat16


def dot_nn(left, right):
    return lax.dot_general(left, right, (((1,), (0,)), ((), ())), preferred_element_type=F32)


def dot_nt(left, right):
    return lax.dot_general(left, right, (((1,), (1,)), ((), ())), preferred_element_type=F32)


def dot_tn(left, right):
    return lax.dot_general(left, right, (((0,), (0,)), ((), ())), preferred_element_type=F32)


def lane_low(shape):
    return lax.broadcasted_iota(jnp.int32, shape, 1) < HD


def stack_heads(rows):
    low = lane_low(rows.shape)
    zero = jnp.zeros_like(rows)
    return jnp.concatenate([jnp.where(low, rows, zero), jnp.where(low, zero, rows)], 0)


def unstack_heads(transposed):
    both = transposed.T
    low = lane_low((BLOCK, PAIR))
    return jnp.where(low, both[:BLOCK], both[BLOCK:])


def block_place(meta):
    block = pl.program_id(0)
    first_blocks = meta[0]
    second = block >= first_blocks
    start = jnp.where(second, first_blocks, 0)
    return block, block - start, start, second.astype(jnp.int32), block < meta[1]


def diagonal_mask(own, piece, tensor_index):
    key = lax.broadcasted_iota(jnp.int32, (BLOCK, 2 * BLOCK), 0)
    query = lax.broadcasted_iota(jnp.int32, (BLOCK, 2 * BLOCK), 1) & (BLOCK - 1)
    if own:
        return key <= query
    shift = piece.bit_length() - 1
    return (key >> shift) < (query >> shift) + tensor_index


def mask_scores(scores, mask):
    keys = scores.shape[0]
    last = jnp.where(mask, scores[keys - BLOCK :], MASKED)
    if keys == BLOCK:
        return last
    return jnp.concatenate([scores[: keys - BLOCK], last], 0)


def pair_columns(pair):
    return slice(pair * PAIR, (pair + 1) * PAIR)


def run_spans(spans, local, start, active, run):
    base = pl.multiple_of(start * BLOCK, BLOCK)
    for step in range(spans):
        pl.when(active & (local == step))(functools.partial(run, base, (step + 1) * BLOCK))


def forward_kernel(piece, spans, meta, q_ref, *refs):
    pairs_in = refs[:2]
    out_ref, lse_ref = refs[2:4]
    flipped = refs[4:6]
    block, local, start, _, active = block_place(meta)
    half = q_ref.shape[1]

    @pl.when(block == 0)
    def _():
        for part in range(2):
            flipped[part][...] = pairs_in[part][:, half:].astype(F32).T.astype(BF16)

    def run(base, span):
        place = pl.ds(base, span)
        masks = [diagonal_mask(part == 0, piece, meta[2]) for part in range(2)]
        for pair in range(half // PAIR):
            cols = pair_columns(pair)
            stacked = stack_heads(q_ref[:, cols])
            scores = [
                mask_scores(dot_nt(pairs_in[part][place, cols], stacked), masks[part])
                for part in range(2)
            ]
            top = jnp.maximum(
                jnp.max(scores[0], 0, keepdims=True), jnp.max(scores[1], 0, keepdims=True)
            )
            exps = [jnp.exp(tile - top) for tile in scores]
            total = jnp.sum(exps[0], 0, keepdims=True) + jnp.sum(exps[1], 0, keepdims=True)
            result = dot_nn(flipped[0][cols, place], exps[0].astype(BF16)) + dot_nn(
                flipped[1][cols, place], exps[1].astype(BF16)
            )
            out_ref[:, cols] = unstack_heads(result / total).astype(BF16)
            lse_ref[0, pair : pair + 1, :] = top + jnp.log(total)

    run_spans(spans, local, start, active, run)

    @pl.when(jnp.logical_not(active))
    def _():
        out_ref[...] = jnp.zeros_like(out_ref)
        lse_ref[...] = jnp.zeros_like(lse_ref)


def backward_kernel(piece, spans, meta, q_ref, g_ref, lse_ref, *refs):
    pairs_in = refs[:2]
    dq_ref = refs[2]
    outs = refs[3:5]
    flipped = refs[5:7]
    sums = refs[7:9]
    block, local, start, _, active = block_place(meta)
    half = q_ref.shape[1]

    @pl.when(block == 0)
    def _():
        for part in range(2):
            flipped[part][...] = pairs_in[part][:, :half].astype(F32).T.astype(BF16)
            sums[part][...] = jnp.zeros_like(sums[part])

    def run(base, span):
        place = pl.ds(base, span)
        masks = [diagonal_mask(part == 0, piece, meta[2]) for part in range(2)]
        for pair in range(half // PAIR):
            cols = pair_columns(pair)
            value_cols = slice(half + pair * PAIR, half + (pair + 1) * PAIR)
            queries = stack_heads(q_ref[:, cols])
            grads = stack_heads(g_ref[:, cols])
            lse = lse_ref[0, pair : pair + 1, :]
            probs = []
            grad_probs = []
            for part in range(2):
                tile = mask_scores(dot_nt(pairs_in[part][place, cols], queries), masks[part])
                probs.append(jnp.exp(tile - lse))
                grad_probs.append(dot_nt(pairs_in[part][place, value_cols], grads))
            row_dot = jnp.sum(probs[0] * grad_probs[0], 0, keepdims=True) + jnp.sum(
                probs[1] * grad_probs[1], 0, keepdims=True
            )
            grad_query = None
            for part in range(2):
                grad_score = (probs[part] * (grad_probs[part] - row_dot)).astype(BF16)
                sums[part][place, value_cols] += dot_nn(probs[part].astype(BF16), grads)
                sums[part][place, cols] += dot_nn(grad_score, queries)
                term = dot_nn(flipped[part][cols, place], grad_score)
                grad_query = term if grad_query is None else grad_query + term
            dq_ref[:, cols] = unstack_heads(grad_query).astype(BF16)

    run_spans(spans, local, start, active, run)

    @pl.when(jnp.logical_not(active))
    def _():
        dq_ref[...] = jnp.zeros_like(dq_ref)

    @pl.when(block == pl.num_programs(0) - 1)
    def _():
        for part in range(2):
            outs[part][...] = sums[part][...].astype(outs[part].dtype)


def row_spec(width, rows=BLOCK):
    return pl.BlockSpec((rows, width), lambda block, meta: (block, 0))


def whole_spec(rows, width):
    return pl.BlockSpec((rows, width), lambda block, meta: (0, 0))


def lse_spec(group=1):
    return pl.BlockSpec((group, 8, 2 * BLOCK), lambda block, meta: (block, 0, 0))


def kept(shape, kind):
    return jax.ShapeDtypeStruct(shape, kind)


def light_cost():
    return pl.CostEstimate(flops=1000, bytes_accessed=1000, transcendentals=0)


def attend_forward(meta, queries, near, far, piece, spans):
    rows, half = queries.shape
    blocks = rows // BLOCK
    return pl.pallas_call(
        functools.partial(forward_kernel, piece, spans),
        grid_spec=pltpu.PrefetchScalarGridSpec(
            num_scalar_prefetch=1,
            grid=(blocks,),
            in_specs=[row_spec(half)] + [whole_spec(rows, 2 * half)] * 2,
            out_specs=[row_spec(half), lse_spec()],
            scratch_shapes=[pltpu.VMEM((half, rows), BF16)] * 2,
        ),
        out_shape=[kept((rows, half), BF16), kept((blocks, 8, 2 * BLOCK), F32)],
        cost_estimate=light_cost(),
        name="attend_forward",
    )(meta, queries, near, far)


def attend_backward(meta, queries, grads, lse, near, far, piece, spans):
    rows, half = queries.shape
    return pl.pallas_call(
        functools.partial(backward_kernel, piece, spans),
        grid_spec=pltpu.PrefetchScalarGridSpec(
            num_scalar_prefetch=1,
            grid=(rows // BLOCK,),
            in_specs=[row_spec(half), row_spec(half), lse_spec()]
            + [whole_spec(rows, 2 * half)] * 2,
            out_specs=[row_spec(half)] + [whole_spec(rows, 2 * half)] * 2,
            scratch_shapes=[pltpu.VMEM((half, rows), BF16)] * 2
            + [pltpu.VMEM((rows, 2 * half), F32)] * 2,
        ),
        out_shape=[
            kept((rows, half), BF16),
            kept((rows, 2 * half), F32),
            kept((rows, 2 * half), BF16),
        ],
        cost_estimate=light_cost(),
        name="attend_backward",
    )(meta, queries, grads, lse, near, far)


def project_kernel(score_scale, x_ref, wq, wk, wv, bias, q_ref, pair_ref):
    rows = x_ref[...]
    half = q_ref.shape[1]
    q_ref[...] = ((dot_nn(rows, wq[...]) + bias[0:1, :]) * score_scale).astype(BF16)
    pair_ref[:, :half] = dot_nn(rows, wk[...]).astype(BF16)
    pair_ref[:, half:] = (dot_nn(rows, wv[...]) + bias[1:2, :]).astype(BF16)


def project(inputs, weight, bias, score_scale):
    rows, width = inputs.shape
    half = bias.shape[1]
    return pl.pallas_call(
        functools.partial(project_kernel, score_scale),
        grid=(2,),
        in_specs=[plain_rows(rows // 2, width)]
        + [plain_fixed((width, half), 0, i) for i in range(3)]
        + [plain_fixed((4, half))],
        out_specs=[plain_rows(rows // 2, half), plain_rows(rows // 2, 2 * half)],
        out_shape=[kept((rows, half), BF16), kept((rows, 2 * half), BF16)],
        cost_estimate=light_cost(),
        name="project",
    )(inputs, weight, weight, weight, bias)


def grads_kernel(sides, counts, factors, extra, grouped, meta, *refs):
    lefts = refs[: max(sides) + 1]
    rights = refs[len(lefts) : len(lefts) + len(counts)]
    rest = refs[len(lefts) + len(counts) :]
    extra_ref = rest[0] if extra else None
    out_ref = rest[-1]
    step = pl.program_id(0)
    begin = 0
    for index, count in enumerate(counts):

        @pl.when((step >= begin) & (step < begin + count))
        def _(index=index):
            result = dot_tn(lefts[sides[index]][...], rights[index][...])
            if factors[index] != 1.0:
                result = result * factors[index]
            if not grouped:
                if extra:
                    result = result + extra_ref[...].astype(F32)
                out_ref[...] = result.astype(BF16)
                return
            size = out_ref.shape[2]
            for plane in range(4):
                for low in range(4):
                    row = (plane * 4 + low) * size
                    place = pl.ds(low if grouped == FIXED else meta[0] ^ low, 1)
                    part = result[row : row + size]
                    if extra:
                        part = part + extra_ref[place, plane].astype(F32)[0]
                    out_ref[place, plane] = part.astype(BF16)[None]

        begin += count


def weight_grads(meta, lefts, rights, sides, factors, extra, grouped):
    chunk = min(2 * 384, rights[0].shape[1])
    shifts = [right[1] if isinstance(right, tuple) else 0 for right in rights]
    counts = [1 if isinstance(right, tuple) else right.shape[1] // chunk for right in rights]
    rights = [right[0] if isinstance(right, tuple) else right for right in rights]
    width = lefts[0].shape[1]
    total = sum(counts) * chunk
    begins = [sum(counts[:i]) for i in range(len(counts))]

    def right_spec(index):
        return pl.BlockSpec(
            (rights[index].shape[0], chunk),
            lambda step, meta: (
                0,
                shifts[index] + jnp.clip(step - begins[index], 0, counts[index] - 1),
            ),
        )

    if grouped:
        shape = (4, 4, width // 16, total)
        out_spec = pl.BlockSpec((4, 4, width // 16, chunk), lambda step, meta: (0, 0, 0, step))
    else:
        shape = (width, total)
        out_spec = pl.BlockSpec((width, chunk), lambda step, meta: (0, step))
    flops = 2 * rights[0].shape[0] * width * total
    return pl.pallas_call(
        functools.partial(grads_kernel, sides, counts, factors, extra is not None, grouped),
        grid_spec=pltpu.PrefetchScalarGridSpec(
            num_scalar_prefetch=1,
            grid=(sum(counts),),
            in_specs=[pl.BlockSpec(left.shape, lambda step, meta: (0, 0)) for left in lefts]
            + [right_spec(index) for index in range(len(rights))]
            + ([out_spec] if extra is not None else []),
            out_specs=out_spec,
        ),
        out_shape=jax.ShapeDtypeStruct(shape, BF16),
        cost_estimate=pl.CostEstimate(
            flops=flops // LIGHT, bytes_accessed=flops // 256 // LIGHT, transcendentals=0
        ),
        name="weight_grads",
    )(meta, *lefts, *rights, *([extra] if extra is not None else []))


def norm_forward(hidden, gain, shift):
    center = hidden - jnp.mean(hidden, -1, keepdims=True)
    spread = jnp.mean(center * center, -1, keepdims=True)
    scale = lax.rsqrt(spread + EPSILON)
    unit = center * scale
    return unit * gain + shift, unit, scale


def norm_gradient(grad, unit, scale, gain):
    inner = grad * gain
    mean_inner = jnp.mean(inner, -1, keepdims=True)
    mean_unit = jnp.mean(inner * unit, -1, keepdims=True)
    return scale * (inner - mean_inner - unit * mean_unit)


def norm_backward(grad, unit, scale, gain):
    return norm_gradient(grad, unit, scale, gain), jnp.sum(grad * unit, 0), jnp.sum(grad, 0)


def sub_blocks(meta, keys_each, run, skip):
    def one(sub, carry):
        block = pl.program_id(0) * GROUP + sub
        second = (block >= meta[0]).astype(jnp.int32)
        place = pl.ds(pl.multiple_of(second * keys_each, keys_each), keys_each)
        rows = pl.ds(pl.multiple_of(sub * BLOCK, BLOCK), BLOCK)
        pl.when(block < meta[1])(functools.partial(run, sub, rows, place))
        pl.when(block >= meta[1])(functools.partial(skip, sub, rows))
        return carry

    lax.fori_loop(0, GROUP, one, 0)


def mid_forward_kernel(score_scale, meta, x_ref, attn0, attn1, memory_ref, *refs):
    attn = (attn0, attn1)
    self_out, query_w, memory_k, memory_v, cross_out = [refs[2 * i : 2 * i + 2] for i in range(5)]
    bias0, bias1, out_bias, gain, shift = refs[10:15]
    unit1_ref, scale1_ref, unit2_ref, scale2_ref, cross_in_ref, hidden_ref, lse_ref = refs[15:22]
    cq_refs, cattn_refs, ck_refs, cv_refs = [refs[22 + 2 * i : 24 + 2 * i] for i in range(4)]
    flipped = refs[30:32]
    half = attn0.shape[1]
    keys_each = memory_ref.shape[0] // 2

    @pl.when(pl.program_id(0) == 0)
    def _():
        for h, bias in enumerate((bias0, bias1)):
            ck_refs[h][...] = dot_nn(memory_ref[...], memory_k[h][...]).astype(BF16)
            value = dot_nn(memory_ref[...], memory_v[h][...]) + bias[3:4, :]
            cv_refs[h][...] = value.astype(BF16)
            flipped[h][...] = value.T.astype(BF16)

    branch = dot_nt(attn[0][...], self_out[0][...]) + dot_nt(attn[1][...], self_out[1][...])
    n1, unit1, scale1 = norm_forward(
        x_ref[...].astype(F32) + branch + out_bias[0:1, :], gain[0:1, :], shift[0:1, :]
    )
    unit1_ref[...] = unit1
    scale1_ref[...] = scale1
    cross_in = n1.astype(BF16)
    cross_in_ref[...] = cross_in
    for h, bias in enumerate((bias0, bias1)):
        query = (dot_nn(cross_in, query_w[h][...]) + bias[2:3, :]) * score_scale
        cq_refs[h][...] = query.astype(BF16)

    def run(sub, rows, place):
        for h in range(2):
            for pair in range(half // PAIR):
                cols = pair_columns(pair)
                tile = dot_nt(ck_refs[h][place, cols], stack_heads(cq_refs[h][rows, cols]))
                top = jnp.max(tile, 0, keepdims=True)
                exps = jnp.exp(tile - top)
                total = jnp.sum(exps, 0, keepdims=True)
                result = dot_nn(flipped[h][cols, place], exps.astype(BF16))
                cattn_refs[h][rows, cols] = unstack_heads(result / total).astype(BF16)
                row = h * (half // PAIR) + pair
                lse_ref[sub, row : row + 1, :] = top + jnp.log(total)

    def skip(sub, rows):
        lse_ref[sub] = jnp.zeros(lse_ref.shape[1:], F32)
        for h in range(2):
            cattn_refs[h][rows, :] = jnp.zeros((BLOCK, half), BF16)

    sub_blocks(meta, keys_each, run, skip)
    branch = dot_nt(cattn_refs[0][...], cross_out[0][...]) + dot_nt(
        cattn_refs[1][...], cross_out[1][...]
    )
    n1 = unit1_ref[...] * gain[0:1, :] + shift[0:1, :]
    n2, unit2, scale2 = norm_forward(n1 + branch + out_bias[1:2, :], gain[1:2, :], shift[1:2, :])
    unit2_ref[...] = unit2
    scale2_ref[...] = scale2
    hidden_ref[...] = n2.astype(BF16)


def mid_backward_kernel(score_scale, total_rows, meta, dn2_ref, unit2_ref, scale2_ref, unit1_ref, scale1_ref, lse_ref, *refs):
    cq_refs, ck_refs, cv_refs = [refs[2 * i : 2 * i + 2] for i in range(3)]
    self_out, query_w, cross_out = [refs[6 + 2 * i : 8 + 2 * i] for i in range(3)]
    gain = refs[12]
    dy2_ref, dh1_ref, dy_ref, sums_ref = refs[13:17]
    dcq_refs, da_refs = refs[17:19], refs[19:21]
    near_ref, far_ref = refs[21:23]
    dca_refs, flipped, dck_refs, dcv_refs = [refs[23 + 2 * i : 25 + 2 * i] for i in range(4)]
    half = cq_refs[0].shape[1]
    keys_each = ck_refs[0].shape[0] // 2
    here = pl.program_id(0) * GROUP * BLOCK + lax.broadcasted_iota(
        jnp.int32, (GROUP * BLOCK, 1), 0
    )
    inside = here < total_rows

    def load(ref):
        return jnp.where(inside, ref[...], 0.0)

    @pl.when(pl.program_id(0) == 0)
    def _():
        sums_ref[...] = jnp.zeros_like(sums_ref)
        for h in range(2):
            flipped[h][...] = ck_refs[h][...].astype(F32).T.astype(BF16)
            dck_refs[h][...] = jnp.zeros_like(dck_refs[h])
            dcv_refs[h][...] = jnp.zeros_like(dcv_refs[h])

    dn2 = load(dn2_ref)
    unit2 = load(unit2_ref)
    dh2 = norm_gradient(dn2, unit2, load(scale2_ref), gain[1:2, :])
    dh1_ref[...] = dh2
    dy2 = dh2.astype(BF16)
    dy2_ref[...] = dy2
    sums_ref[0:1, :] += jnp.sum(dn2 * unit2, 0, keepdims=True)
    sums_ref[1:2, :] += jnp.sum(dn2, 0, keepdims=True)
    sums_ref[2:3, :] += jnp.sum(dy2.astype(F32), 0, keepdims=True)
    for h in range(2):
        dca_refs[h][...] = dot_nn(dy2, cross_out[h][...]).astype(BF16)

    def run(sub, rows, place):
        for h in range(2):
            for pair in range(half // PAIR):
                cols = pair_columns(pair)
                row = h * (half // PAIR) + pair
                queries = stack_heads(cq_refs[h][rows, cols])
                grads = stack_heads(dca_refs[h][rows, cols])
                tile = dot_nt(ck_refs[h][place, cols], queries)
                probs = jnp.exp(tile - lse_ref[sub, row : row + 1, :])
                grad_probs = dot_nt(cv_refs[h][place, cols], grads)
                row_dot = jnp.sum(probs * grad_probs, 0, keepdims=True)
                grad_score = (probs * (grad_probs - row_dot)).astype(BF16)
                dcv_refs[h][place, cols] += dot_nn(probs.astype(BF16), grads)
                dck_refs[h][place, cols] += dot_nn(grad_score, queries)
                term = dot_nn(flipped[h][cols, place], grad_score)
                dcq_refs[h][rows, cols] = unstack_heads(term).astype(BF16)

    def skip(sub, rows):
        for h in range(2):
            dcq_refs[h][rows, :] = jnp.zeros((BLOCK, half), BF16)

    sub_blocks(meta, keys_each, run, skip)
    dn1 = dh1_ref[...]
    for h in range(2):
        dcq = dcq_refs[h][...]
        dn1 = dn1 + score_scale * dot_nt(dcq, query_w[h][...])
        sums_ref[6:7, h * half : (h + 1) * half] += jnp.sum(dcq.astype(F32), 0, keepdims=True)
    unit1 = load(unit1_ref)
    dh1 = norm_gradient(dn1, unit1, load(scale1_ref), gain[0:1, :])
    dy = dh1.astype(BF16)
    dh1_ref[...] = dh1
    dy_ref[...] = dy
    sums_ref[3:4, :] += jnp.sum(dn1 * unit1, 0, keepdims=True)
    sums_ref[4:5, :] += jnp.sum(dn1, 0, keepdims=True)
    sums_ref[5:6, :] += jnp.sum(dy.astype(F32), 0, keepdims=True)
    for h in range(2):
        da_refs[h][...] = dot_nn(dy, self_out[h][...]).astype(BF16)

    @pl.when(pl.program_id(0) == pl.num_programs(0) - 1)
    def _():
        own = keys_each // 2
        for index, ref in enumerate((dck_refs[0], dck_refs[1], dcv_refs[0], dcv_refs[1])):
            near = slice(index * half, (index + 1) * half)
            far = slice((index ^ 1) * half, ((index ^ 1) + 1) * half)
            for seq in range(2):
                rows = slice(seq * own, (seq + 1) * own)
                base = seq * keys_each
                near_ref[rows, near] = ref[base : base + own, :]
                far_ref[rows, far] = ref[base + own : base + keys_each, :].astype(BF16)


def memory_backward_kernel(near_ref, got_ref, wk0, wv0, wk1, wv1, sum_ref, encoder_ref, bias_ref):
    total = (near_ref[...] + got_ref[...].astype(F32)).astype(BF16)
    sum_ref[...] = total
    half = wk0.shape[1]
    grad = dot_nt(total[:, :half], wk0[...]) + dot_nt(total[:, half : 2 * half], wk1[...])
    grad = grad + dot_nt(total[:, 2 * half : 3 * half], wv0[...])
    encoder_ref[...] = (grad + dot_nt(total[:, 3 * half :], wv1[...])).astype(BF16)
    bias = jnp.sum(total[:, 2 * half :].astype(F32), 0, keepdims=True)
    bias_ref[...] = jnp.broadcast_to(bias, bias_ref.shape)


def memory_backward(near, got, mid):
    rows, span = near.shape
    half = span // 4
    width = mid[0].shape[0]
    columns = [plain_fixed((width, half), 0, 2), plain_fixed((width, half), 0, 3)]
    return pl.pallas_call(
        memory_backward_kernel,
        grid=(1,),
        in_specs=[plain_fixed((rows, span))] * 2 + columns * 2,
        out_specs=[plain_fixed((rows, span)), plain_fixed((rows, width)), plain_fixed((8, 2 * half))],
        out_shape=[kept((rows, span), BF16), kept((rows, width), BF16), kept((8, 2 * half), F32)],
        cost_estimate=pl.CostEstimate(flops=1000, bytes_accessed=1000, transcendentals=0),
        name="memory_backward",
    )(near, got, mid[0], mid[0], mid[1], mid[1])


def ffn_forward_kernel(first, hidden_ref, base_ref, expand, reduce, bias, gain, shift, act_ref, slope_ref, total_ref):
    pre = dot_nn(hidden_ref[...], expand[...]) + bias[0:1, :]
    phi = 0.5 * (1.0 + lax.erf(pre * (1.0 / math.sqrt(2.0))))
    density = jnp.exp(-0.5 * pre * pre) * (1.0 / math.sqrt(2.0 * math.pi))
    act = (pre * phi).astype(BF16)
    act_ref[...] = act
    slope_ref[...] = (phi + pre * density).astype(BF16)
    base = base_ref[...]
    if first:
        base = base * gain[0:1, :] + shift[0:1, :]
    total_ref[...] = base + dot_nt(act, reduce[...])


def ffn_forward(first, hidden, base, weight, bias, gain, shift):
    rows, width = hidden.shape
    units = bias.shape[1]
    tall = rows // 4
    wide, long = plain_rows(tall, width), plain_rows(tall, units)

    def side(column):
        return pl.BlockSpec(
            (width, units), lambda step: (0, column), pipeline_mode=pl.Buffered(1)
        )

    return pl.pallas_call(
        functools.partial(ffn_forward_kernel, first),
        grid=(4,),
        in_specs=[wide, wide, side(0), side(1), plain_fixed((1, units))]
        + [plain_fixed((1, width))] * 2,
        out_specs=[long, long, wide],
        out_shape=[
            kept((rows, units), BF16),
            kept((rows, units), BF16),
            kept((rows, width), F32),
        ],
        cost_estimate=light_cost(),
        name="ffn_forward",
    )(hidden, base, weight, weight, bias, gain, shift)


def ffn_backward_kernel(h3_ref, cot_ref, valid_ref, slope0, slope1, in0, in1, out0, out1, gain, shift, n3_ref, dz_ref, dn2_ref, sums_ref, du0, du1, usum0, usum1):
    @pl.when(pl.program_id(0) == 0)
    def _():
        for ref in (sums_ref, usum0, usum1):
            ref[...] = jnp.zeros_like(ref)

    n3, unit, scale = norm_forward(h3_ref[...], gain[2:3, :], shift[2:3, :])
    valid = valid_ref[...] > 0.5
    n3_ref[...] = jnp.where(valid, n3, 0.0).astype(BF16)
    dn3 = jnp.where(valid, cot_ref[...].astype(F32), 0.0)
    dh3 = norm_gradient(dn3, unit, scale, gain[2:3, :])
    dz = dh3.astype(BF16)
    dz_ref[...] = dz
    sums_ref[0:1, :] += jnp.sum(dn3 * unit, 0, keepdims=True)
    sums_ref[1:2, :] += jnp.sum(dn3, 0, keepdims=True)
    sums_ref[2:3, :] += jnp.sum(dz.astype(F32), 0, keepdims=True)
    total = dh3
    sides = ((slope0, out0, in0, du0, usum0), (slope1, out1, in1, du1, usum1))
    for slope, reduce, expand, du_ref, usum in sides:
        du = (dot_nn(dz, reduce[...]) * slope[...].astype(F32)).astype(BF16)
        du_ref[...] = du
        usum[0:1, :] += jnp.sum(du.astype(F32), 0, keepdims=True)
        total = total + dot_nt(du, expand[...])
    dn2_ref[...] = total


def ffn_backward(h3, cot, valid, slope, ffn, gain, shift):
    rows, width = h3.shape
    units = slope[0].shape[1]
    wide, thin, long = [plain_rows(rows // 2, w) for w in (width, 1, units)]

    def side(column):
        return pl.BlockSpec(
            (width, units), lambda step: (0, column), pipeline_mode=pl.Buffered(1)
        )

    return pl.pallas_call(
        ffn_backward_kernel,
        grid=(2,),
        in_specs=[wide, wide, thin, long, long, side(0), side(0), side(1), side(1)]
        + [plain_fixed((3, width))] * 2,
        out_specs=[wide, wide, wide, plain_fixed((8, width)), long, long]
        + [plain_fixed((8, units))] * 2,
        out_shape=[
            kept((rows, width), BF16),
            kept((rows, width), BF16),
            kept((rows, width), F32),
            kept((8, width), F32),
            kept((rows, units), BF16),
            kept((rows, units), BF16),
            kept((8, units), F32),
            kept((8, units), F32),
        ],
        cost_estimate=pl.CostEstimate(flops=1000, bytes_accessed=1000, transcendentals=0),
        name="ffn_backward",
    )(h3, cot, valid, *slope, ffn[0], ffn[1], ffn[0], ffn[1], gain, shift)


def fixed_spec(shape, *index):
    place = index or (0,) * len(shape)
    return pl.BlockSpec(shape, lambda block, meta: place)


def mid_forward(meta, inputs, attn, memory, mid, in_pair, out_bias, gain, shift, score_scale):
    rows, width = inputs.shape
    half = attn[0].shape[1]
    blocks = rows // BLOCK
    memory_rows = memory.shape[0]
    weights = [fixed_spec((width, half), 0, column) for column in range(5) for _ in range(2)]
    tall = GROUP * BLOCK
    wide, thin, narrow = row_spec(width, tall), row_spec(1, tall), row_spec(half, tall)
    memory_spec = fixed_spec((memory_rows, half))
    outs = pl.pallas_call(
        functools.partial(mid_forward_kernel, score_scale),
        grid_spec=pltpu.PrefetchScalarGridSpec(
            num_scalar_prefetch=1,
            grid=(pl.cdiv(blocks, GROUP),),
            in_specs=[wide, narrow, narrow, fixed_spec(memory.shape)]
            + weights
            + [fixed_spec((4, half))] * 2
            + [fixed_spec((3, width))] * 3,
            out_specs=[wide, thin, wide, thin, wide, wide, lse_spec(GROUP)]
            + [narrow] * 4
            + [memory_spec] * 4,
            scratch_shapes=[pltpu.VMEM((half, memory_rows), BF16)] * 2,
        ),
        out_shape=[
            kept((rows, width), F32),
            kept((rows, 1), F32),
            kept((rows, width), F32),
            kept((rows, 1), F32),
            kept((rows, width), BF16),
            kept((rows, width), BF16),
            kept((blocks, 8, 2 * BLOCK), F32),
        ]
        + [kept((rows, half), BF16)] * 4
        + [kept((memory_rows, half), BF16)] * 4,
        cost_estimate=pl.CostEstimate(
            flops=(24 * rows * width * half) // LIGHT, bytes_accessed=(20 * rows * width) // LIGHT, transcendentals=0
        ),
        name="mid_forward",
    )(meta, inputs, *attn, memory, *[mid[h] for _ in range(5) for h in range(2)], *in_pair, out_bias, gain, shift)
    return outs[:7], outs[7:9], outs[9:11], outs[11:13], outs[13:15]


def mid_backward(meta, dn2, saved, cq, ck, cv, mid, gain, score_scale):
    unit1, scale1, unit2, scale2, lse = saved
    rows, width = dn2.shape
    half = cq[0].shape[1]
    blocks = rows // BLOCK
    memory_rows = ck[0].shape[0]
    tall = GROUP * BLOCK
    wide, thin, narrow = row_spec(width, tall), row_spec(1, tall), row_spec(half, tall)
    memory_spec = fixed_spec((memory_rows, half))
    weights = [fixed_spec((width, half), 0, column) for column in (0, 1, 4) for _ in range(2)]
    outs = pl.pallas_call(
        functools.partial(mid_backward_kernel, score_scale, rows),
        grid_spec=pltpu.PrefetchScalarGridSpec(
            num_scalar_prefetch=1,
            grid=(pl.cdiv(blocks, GROUP),),
            in_specs=[wide, wide, thin, wide, thin, lse_spec(GROUP)]
            + [narrow] * 2
            + [memory_spec] * 4
            + weights
            + [fixed_spec((3, width))],
            out_specs=[wide, wide, wide, fixed_spec((8, width))]
            + [narrow] * 4
            + [fixed_spec((memory_rows // 2, 4 * half))] * 2,
            scratch_shapes=[pltpu.VMEM((tall, half), BF16)] * 2
            + [pltpu.VMEM((half, memory_rows), BF16)] * 2
            + [pltpu.VMEM((memory_rows, half), F32)] * 4,
        ),
        out_shape=[
            kept((rows, width), BF16),
            kept((rows, width), F32),
            kept((rows, width), BF16),
            kept((8, width), F32),
        ]
        + [kept((rows, half), BF16)] * 4
        + [kept((memory_rows // 2, 4 * half), F32), kept((memory_rows // 2, 4 * half), BF16)],
        cost_estimate=pl.CostEstimate(
            flops=(24 * rows * width * half) // LIGHT, bytes_accessed=(20 * rows * width) // LIGHT, transcendentals=0
        ),
        name="mid_backward",
    )(meta, dn2, unit2, scale2, unit1, scale1, lse, *cq, *ck, *cv, *[mid[h] for _ in range(3) for h in range(2)], gain)
    return outs[:4], outs[4:6], outs[6:8], outs[8], outs[9]


def input_backward_kernel(score_scale, base_ref, dq_ref, own_ref, got_ref, wq, wk, wv, dx_ref, pair_ref, sums_ref):
    @pl.when(pl.program_id(0) == 0)
    def _():
        sums_ref[...] = jnp.zeros_like(sums_ref)

    half = dq_ref.shape[1]
    pair = (own_ref[...] + got_ref[...].astype(F32)).astype(BF16)
    pair_ref[...] = pair
    dq = dq_ref[...]
    dk, dv = pair[:, :half], pair[:, half:]
    sums_ref[0:1, :] += score_scale * jnp.sum(dq.astype(F32), 0, keepdims=True)
    sums_ref[1:2, :] += jnp.sum(dv.astype(F32), 0, keepdims=True)
    total = score_scale * dot_nt(dq, wq[...]) + dot_nt(dk, wk[...]) + dot_nt(dv, wv[...])
    dx_ref[...] = (base_ref[...] + total).astype(dx_ref.dtype)


def plain_rows(rows, width):
    return pl.BlockSpec((rows, width), lambda step: (step, 0))


def plain_fixed(shape, *index):
    place = index or (0,) * len(shape)
    return pl.BlockSpec(shape, lambda step: place)


def input_backward(base, dq, own, got, weight, score_scale, kind):
    rows, width = base.shape
    half = dq.shape[1]
    tall = rows // 2
    return pl.pallas_call(
        functools.partial(input_backward_kernel, score_scale),
        grid=(2,),
        in_specs=[plain_rows(tall, width), plain_rows(tall, half)]
        + [plain_rows(tall, 2 * half)] * 2
        + [plain_fixed((width, half), 0, i) for i in range(3)],
        out_specs=[plain_rows(tall, width), plain_rows(tall, 2 * half), plain_fixed((8, half))],
        out_shape=[
            kept((rows, width), kind),
            kept((rows, 2 * half), BF16),
            kept((8, half), F32),
        ],
        cost_estimate=light_cost(),
        name="input_backward",
    )(base, dq, own, got, weight, weight, weight)


def swap(value):
    return lax.ppermute(value, "tensor", [(0, 1), (1, 0)])


def hop(value, bits):
    return lax.ppermute(value, "dp", [(i, i ^ bits) for i in range(16)])


def assemble_kernel(meta, own_ref, first_ref, second_ref, third_ref, out_ref):
    for low, ref in enumerate((own_ref, first_ref, second_ref, third_ref)):
        out_ref[0, pl.ds(meta[1] ^ low, 1)] = ref[...]


def plane_line(value):
    return jnp.stack([value, hop(value, 4), hop(value, 8), hop(value, 12)])


def low_groups(line):
    return (line, hop(line, 1), hop(line, 2), hop(line, 3))


def assemble(groups):
    rows, count = groups[0].shape[1:]
    index = lax.axis_index("dp")
    meta = jnp.stack([index // 4, index % 4]).astype(jnp.int32)
    spec = pl.BlockSpec((1, rows, count), lambda i, meta: (i ^ meta[0], 0, 0))
    full = pl.pallas_call(
        assemble_kernel,
        grid_spec=pltpu.PrefetchScalarGridSpec(
            num_scalar_prefetch=1,
            grid=(4,),
            in_specs=[spec] * 4,
            out_specs=pl.BlockSpec((1, 4, rows, count), lambda i, meta: (i, 0, 0, 0)),
        ),
        out_shape=kept((4, 4, rows, count), groups[0].dtype),
        cost_estimate=light_cost(),
        name="assemble",
    )(meta, *groups)
    return full.reshape(16 * rows, count)


def total_of(parts):
    return functools.reduce(jnp.add, [part.astype(F32) for part in parts])


def scatter_low(groups):
    received = [hop(groups[low], low) for low in (1, 2, 3)]
    return total_of([groups[0]] + received).astype(BF16)


def scatter_plane(line):
    plane = lax.axis_index("dp") // 4

    def pick(other):
        return lax.dynamic_index_in_dim(line, plane ^ other, 0, keepdims=False)

    received = [hop(pick(other), 4 * other) for other in (1, 2, 3)]
    return total_of([pick(0)] + received)


def wide_scatter(value, groups=None):
    return lax.psum_scatter(
        value, "dp", scatter_dimension=0, tiled=True, axis_index_groups=groups
    )


def sum_low(value):
    return total_of([value] + [hop(value, bits) for bits in (1, 2, 3)])


def sum_planes(value):
    return total_of([value] + [hop(value, 4 * bits) for bits in (1, 2, 3)])


def rows_at(value, ids):
    return value.at[ids].get(mode="promise_in_bounds")


def tie(*values):
    return lax.optimization_barrier(values)


def body(
    tokens,
    encoder,
    lengths,
    deal,
    self_project,
    self_output,
    cross_query,
    cross_memory,
    cross_output,
    hidden_in,
    hidden_out,
    in_bias,
    out_bias,
    hidden_bias,
    norm_gain,
    norm_bias,
    cotangent,
):
    score_scale = 1.0 / math.sqrt(HD)
    dp_count = lax.axis_size("dp")
    dp_index = lax.axis_index("dp")
    tensor_index = lax.axis_index("tensor")
    piece = tokens.shape[1]
    width = tokens.shape[2]
    slots = piece * dp_count
    half = self_project.shape[2]
    units = hidden_in.shape[1]
    shard = self_project.shape[0]
    memory_rows = encoder.shape[1]
    spans = slots // BLOCK
    blocks = (slots + slots // 2) // BLOCK + 1
    rows = blocks * BLOCK
    per_block = BLOCK // piece

    pair_ids = lax.dynamic_slice_in_dim(deal, 2 * dp_index, 2)
    pair_len = rows_at(lengths, pair_ids)
    pieces_used = (pair_len + 2 * piece - 1) // (2 * piece)
    blocks_used = (pieces_used * piece + BLOCK - 1) // BLOCK
    first_blocks = blocks_used[0]
    all_blocks = first_blocks + blocks_used[1]
    meta = jnp.stack([first_blocks, all_blocks, tensor_index]).astype(jnp.int32)

    block_ids = jnp.arange(blocks, dtype=jnp.int32)
    block_seq = (block_ids >= first_blocks).astype(jnp.int32)
    block_local = jnp.minimum(block_ids - block_seq * first_blocks, spans - 1)
    piece_ids = (
        (block_local[:, None] * per_block + jnp.arange(per_block, dtype=jnp.int32)[None, :]) * 2
        + block_seq[:, None]
    ).reshape(-1)
    slot_ids = block_local[:, None] * BLOCK + jnp.arange(BLOCK, dtype=jnp.int32)[None, :]
    positions = ((slot_ids // piece) * 2 + tensor_index) * piece + slot_ids % piece
    row_valid = (
        (positions < jnp.where(block_seq == 1, pair_len[1], pair_len[0])[:, None])
        & (block_ids < all_blocks)[:, None]
    ).reshape(rows, 1)

    send_piece = jnp.arange(dp_count, dtype=jnp.int32)
    send_block = send_piece // per_block
    send_ids = jnp.stack(
        [
            jnp.minimum(send_block, blocks_used[0] - 1) * per_block,
            (first_blocks + jnp.minimum(send_block, blocks_used[1] - 1)) * per_block,
        ],
        1,
    ) + (send_piece % per_block)[:, None]
    send_pos = (send_piece[:, None, None] * 2 + tensor_index) * piece + jnp.arange(
        piece, dtype=jnp.int32
    )[None, None, :]
    send_valid = (send_pos < pair_len[None, :, None]).reshape(2 * dp_count, piece, 1)
    inverse = jnp.zeros_like(deal).at[deal].set(jnp.arange(deal.shape[0], dtype=jnp.int32))

    def home_pieces(value):
        pieces = value.reshape(rows // piece, piece, width)
        return jnp.where(
            send_valid, rows_at(pieces, send_ids.reshape(-1)), jnp.zeros((), value.dtype)
        )

    def go_home(outgoing):
        return lax.all_to_all(outgoing, "dp", split_axis=0, concat_axis=0, tiled=True)

    def order(value):
        return rows_at(value, deal)

    def arrive(ordered):
        return lax.all_to_all(ordered, "dp", split_axis=0, concat_axis=0, tiled=True)

    def pack(arrived):
        return rows_at(arrived, piece_ids).reshape(rows, width)

    quick = dp_count == 16
    ordered = order(tokens)
    qkv_shard_in = self_project.reshape(shard, 3 * half)
    mid_shard_in = jnp.concatenate(
        [self_output.T, cross_query, cross_memory.reshape(shard, 2 * half), cross_output.T], 1
    )

    def slow_gather(value):
        return lax.all_gather(value, "dp", axis=0, tiled=True)

    ordered_cot = order(cotangent)
    if quick:
        qkv_line = plane_line(qkv_shard_in)
        qkv_line, ordered = tie(qkv_line, ordered)
        qkv_groups = low_groups(qkv_line)
        arrived = arrive(ordered)
        ordered_cot, arrived, qkv_groups = tie(ordered_cot, arrived, qkv_groups)
        qkv_own = assemble(qkv_groups)
    else:
        arrived = arrive(ordered)
        qkv_own = slow_gather(qkv_shard_in)
    qkv_weight = (qkv_own, swap(qkv_own))
    inputs = pack(arrived)
    arrived_cot = arrive(ordered_cot)

    mid_own = slow_gather(mid_shard_in)
    ffn_own = slow_gather(jnp.concatenate([hidden_in, hidden_out.T], 1))
    both = (0, 1)

    def columns(pair, start, count):
        return [lax.slice_in_dim(pair[h], start, start + count, axis=1) for h in both]

    biases = jnp.concatenate([in_bias.reshape(-1), hidden_bias])
    bias_pair = (biases, swap(biases))
    in_pair = [b[: 4 * half].reshape(4, half) for b in bias_pair]
    hidden_pair = [b[4 * half :] for b in bias_pair]

    memory_full = jnp.concatenate([encoder, swap(encoder)], 1).reshape(4 * memory_rows, width)

    queries = [None, None]
    near = [None, None]
    attn = [None, None]
    lse = [None, None]
    for h in both:
        queries[h], near[h] = project(inputs, qkv_weight[h], in_pair[h], score_scale)
    far = [swap(near[1 - h]) for h in both]
    attn[1], lse[1] = attend_forward(meta, queries[1], near[1], far[1], piece, spans)
    mid_own, attn[1], queries[0], valid_rows = tie(
        mid_own, attn[1], queries[0], row_valid.astype(F32)
    )
    mid_weight = (mid_own, swap(mid_own))
    attn[0], lse[0] = attend_forward(meta, queries[0], near[0], far[0], piece, spans)
    saved, cqs, cattn, cks, cvs = mid_forward(
        meta, inputs, attn, memory_full, mid_weight, in_pair, out_bias, norm_gain, norm_bias, score_scale
    )
    unit1, scale1, unit2, scale2, cross_in, hidden, clse = saved
    hidden, ffn_own = tie(hidden, ffn_own)
    ffn_far = swap(ffn_own)
    act = [None, None]
    slope = [None, None]
    affine = (norm_gain[1:2], norm_bias[1:2] + out_bias[2:3])
    act[0], slope[0], total = ffn_forward(
        True, hidden, unit2, ffn_own, hidden_pair[0][None], *affine
    )
    ffn_far, total = tie(ffn_far, total)
    act[1], slope[1], total = ffn_forward(
        False, hidden, total, ffn_far, hidden_pair[1][None], *affine
    )
    arrived_cot, total = tie(arrived_cot, total)
    ffn_weight = (ffn_own, ffn_far)
    n3, dz, dn2, sums3, du0, du1, usum0, usum1 = ffn_backward(
        total, pack(arrived_cot), valid_rows, slope, ffn_weight, norm_gain, norm_bias
    )
    du = (du0, du1)
    output_back = go_home(home_pieces(n3))

    low_meta = jnp.reshape(dp_index % 4, (1,)).astype(jnp.int32)

    def chip_grads(lefts, rights, sides, factors, grouped):
        far = weight_grads(low_meta, lefts, rights[1], sides, factors, None, grouped)
        return weight_grads(low_meta, lefts, rights[0], sides, factors, swap(far), grouped)

    ffn_grads = chip_grads(
        [hidden, dz], [[du[h], act[h]] for h in both], (0, 1), (1.0, 1.0), FIXED if quick else 0
    )
    ffn_grads, dn2 = tie(ffn_grads, dn2)
    ffn_line = wide_scatter(ffn_grads.reshape(width, 2 * units), LOW_GROUPS if quick else None)
    rows_back, dcq, da, memory_near, memory_far = mid_backward(
        meta, dn2, (unit1, scale1, unit2, scale2, clse), cqs, cks, cvs, mid_weight, norm_gain, score_scale
    )
    dy2, dh1, dy, sums = rows_back
    da = list(da)
    memory_far, output_back = tie(memory_far, output_back)
    memory_sum, grad_memory, memory_bias = memory_backward(
        memory_near, swap(memory_far), mid_weight
    )
    grad_encoder = grad_memory.reshape(2, memory_rows, width)
    memory_own = encoder.reshape(2 * memory_rows, width)
    mid_grads = chip_grads(
        [dy, cross_in, memory_own, dy2],
        [
            [attn[h], dcq[h], (memory_sum, h), (memory_sum, 2 + h), cattn[h]]
            for h in both
        ],
        (0, 1, 2, 2, 3),
        (1.0, score_scale, 1.0, 1.0, 1.0),
        FIXED if quick else 0,
    )
    mid_grads, da[0], da[1] = tie(mid_grads, da[0], da[1])
    mid_line = wide_scatter(mid_grads.reshape(width, 5 * half), LOW_GROUPS if quick else None)
    dq = [None, None]
    own = [None, None]
    out = [None, None]
    for h in both:
        dq[h], own[h], out[h] = attend_backward(
            meta, queries[h], da[h], lse[h], near[h], far[h], piece, spans
        )
        if h == 0:
            da[1], dq[0], ffn_line = tie(da[1], dq[0], ffn_line)
    factors = (score_scale, 1.0, 1.0)
    got_far, got_near = swap(out[0]), swap(out[1])
    dx_far, pair_far, sums_far = input_backward(
        dh1, dq[1], own[1], got_far, qkv_weight[1], score_scale, F32
    )
    far_grads = weight_grads(
        low_meta, [inputs], [dq[1], (pair_far, 0), (pair_far, 1)], (0, 0, 0), factors, None, quick
    )
    far_grads, dx_far, got_near, ffn_line = tie(far_grads, dx_far, got_near, ffn_line)
    far_grads = swap(far_grads)
    dx, pair_near, sums_near = input_backward(
        dx_far, dq[0], own[0], got_near, qkv_weight[0], score_scale, BF16
    )
    grad_out = home_pieces(dx)
    grad_out, far_grads, output_back = tie(grad_out, far_grads, output_back)
    output = rows_at(output_back, inverse)
    grad_back = go_home(grad_out)
    far_grads, mid_line = tie(far_grads, mid_line)
    ffn_shard = wide_scatter(ffn_line, PLANE_GROUPS) if quick else ffn_line
    mid_shard = wide_scatter(mid_line, PLANE_GROUPS) if quick else mid_line
    ffn_shard, mid_shard = ffn_shard.astype(F32), mid_shard.astype(F32)
    qkv_grads = weight_grads(
        low_meta, [inputs], [dq[0], (pair_near, 0), (pair_near, 1)], (0, 0, 0), factors, far_grads, quick
    )
    sums_qkv = [sums_near, sums_far]

    def global_order(pair):
        own_first = jnp.concatenate(pair, -1)
        other_first = jnp.concatenate(pair[::-1], -1)
        return jnp.where(tensor_index == 0, own_first, other_first)

    in_rows = global_order(
        [
            jnp.stack(
                [
                    sums_qkv[h][0],
                    sums_qkv[h][1],
                    score_scale * sums[6, h * half : (h + 1) * half],
                    memory_bias[0, h * half : (h + 1) * half],
                ]
            )
            for h in both
        ]
    )
    hidden_row = global_order([usum0[0], usum1[0]])
    out_rows = jnp.stack([sums[5], sums[2], sums3[2]])
    gain_rows = jnp.stack([sums[3], sums[0], sums3[0]])
    shift_rows = jnp.stack([sums[4], sums[1], sums3[1]])
    small = jnp.concatenate(
        [
            in_rows.reshape(-1),
            hidden_row,
            out_rows.reshape(-1),
            gain_rows.reshape(-1),
            shift_rows.reshape(-1),
        ]
    )
    if quick:
        small = small + swap(small)
        small, qkv_grads = tie(small, qkv_grads)
        qkv_line = scatter_low(qkv_grads)
        small = sum_low(small)
        qkv_line, grad_back, mid_shard, ffn_shard, small = tie(
            qkv_line, grad_back, mid_shard, ffn_shard, small
        )
        qkv_shard = scatter_plane(qkv_line)
        small = sum_planes(small)
    else:
        qkv_shard = wide_scatter(qkv_grads).astype(F32)
        small = lax.psum(small, ("dp", "tensor"))
    grad_tokens = rows_at(grad_back, inverse)
    in_end = 8 * half
    hidden_end = in_end + 2 * units
    in_total = small[:in_end].reshape(4, 2 * half)
    hidden_total = small[in_end:hidden_end]
    rest = small[hidden_end:].reshape(3, 3, width)
    return (
        output,
        grad_tokens,
        grad_encoder,
        qkv_shard.reshape(shard, 3, half),
        mid_shard[:, :half].T,
        mid_shard[:, half : 2 * half],
        mid_shard[:, 2 * half : 4 * half].reshape(shard, 2, half),
        mid_shard[:, 4 * half :].T,
        ffn_shard[:, :units],
        ffn_shard[:, units:].T,
        lax.dynamic_slice_in_dim(in_total, tensor_index * half, half, 1),
        rest[0],
        lax.dynamic_slice_in_dim(hidden_total, tensor_index * units, units, 0),
        rest[1],
        rest[2],
    )


def solution(mesh):
    in_specs = (
        P(None, ("dp", "tensor"), None),
        P("dp", "tensor", None),
        P(),
        P(),
        P("dp", None, "tensor"),
        P("tensor", "dp"),
        P("dp", "tensor"),
        P("dp", None, "tensor"),
        P("tensor", "dp"),
        P("dp", "tensor"),
        P("tensor", "dp"),
        P(None, "tensor"),
        P(),
        P("tensor"),
        P(),
        P(),
        P(None, ("dp", "tensor"), None),
    )
    out_specs = (
        P(None, ("dp", "tensor"), None),
        P(None, ("dp", "tensor"), None),
        P("dp", "tensor", None),
        P("dp", None, "tensor"),
        P("tensor", "dp"),
        P("dp", "tensor"),
        P("dp", None, "tensor"),
        P("tensor", "dp"),
        P("dp", "tensor"),
        P("tensor", "dp"),
        P(None, "tensor"),
        P(),
        P("tensor"),
        P(),
        P(),
    )
    return jax.shard_map(body, mesh=mesh, in_specs=in_specs, out_specs=out_specs, check_vma=False)
```

```python
import functools
import math

import jax
import jax.numpy as jnp
from jax import lax
from jax.experimental import pallas as pl
from jax.experimental.pallas import tpu as pltpu
from jax.sharding import PartitionSpec as P

HD = 64
EPSILON = 1e-05
MASKED = -1e30
BLOCK = 128
LIGHT = 1000
LOW_GROUPS = [[4 * plane + low for low in range(4)] for plane in range(4)]
PLANE_GROUPS = [[low + 4 * plane for plane in range(4)] for low in range(4)]
GROUP = 4
PLAIN = 0
RELATIVE = 1
FIXED = 2
PAIR = 2 * HD
F32 = jnp.float32
BF16 = jnp.bfloat16


def dot_nn(left, right):
    return lax.dot_general(left, right, (((1,), (0,)), ((), ())), preferred_element_type=F32)


def dot_nt(left, right):
    return lax.dot_general(left, right, (((1,), (1,)), ((), ())), preferred_element_type=F32)


def dot_tn(left, right):
    return lax.dot_general(left, right, (((0,), (0,)), ((), ())), preferred_element_type=F32)


def lane_low(shape):
    return lax.broadcasted_iota(jnp.int32, shape, 1) < HD


def stack_heads(rows):
    low = lane_low(rows.shape)
    zero = jnp.zeros_like(rows)
    return jnp.concatenate([jnp.where(low, rows, zero), jnp.where(low, zero, rows)], 0)


def unstack_heads(transposed):
    both = transposed.T
    low = lane_low((BLOCK, PAIR))
    return jnp.where(low, both[:BLOCK], both[BLOCK:])


def block_place(meta):
    block = pl.program_id(0)
    first_blocks = meta[0]
    second = block >= first_blocks
    start = jnp.where(second, first_blocks, 0)
    return block, block - start, start, second.astype(jnp.int32), block < meta[1]


def diagonal_mask(own, piece, tensor_index):
    key = lax.broadcasted_iota(jnp.int32, (BLOCK, 2 * BLOCK), 0)
    query = lax.broadcasted_iota(jnp.int32, (BLOCK, 2 * BLOCK), 1) & (BLOCK - 1)
    if own:
        return key <= query
    shift = piece.bit_length() - 1
    return (key >> shift) < (query >> shift) + tensor_index


def mask_scores(scores, mask):
    keys = scores.shape[0]
    last = jnp.where(mask, scores[keys - BLOCK :], MASKED)
    if keys == BLOCK:
        return last
    return jnp.concatenate([scores[: keys - BLOCK], last], 0)


def pair_columns(pair):
    return slice(pair * PAIR, (pair + 1) * PAIR)


def run_spans(spans, local, start, active, run):
    base = pl.multiple_of(start * BLOCK, BLOCK)
    for step in range(spans):
        pl.when(active & (local == step))(functools.partial(run, base, (step + 1) * BLOCK))


def forward_kernel(piece, spans, meta, q_ref, *refs):
    pairs_in = refs[:2]
    out_ref, lse_ref = refs[2:4]
    flipped = refs[4:6]
    block, local, start, _, active = block_place(meta)
    half = q_ref.shape[1]

    @pl.when(block == 0)
    def _():
        for part in range(2):
            flipped[part][...] = pairs_in[part][:, half:].astype(F32).T.astype(BF16)

    def run(base, span):
        place = pl.ds(base, span)
        masks = [diagonal_mask(part == 0, piece, meta[2]) for part in range(2)]
        for pair in range(half // PAIR):
            cols = pair_columns(pair)
            stacked = stack_heads(q_ref[:, cols])
            scores = [
                mask_scores(dot_nt(pairs_in[part][place, cols], stacked), masks[part])
                for part in range(2)
            ]
            top = jnp.maximum(
                jnp.max(scores[0], 0, keepdims=True), jnp.max(scores[1], 0, keepdims=True)
            )
            exps = [jnp.exp(tile - top) for tile in scores]
            total = jnp.sum(exps[0], 0, keepdims=True) + jnp.sum(exps[1], 0, keepdims=True)
            result = dot_nn(flipped[0][cols, place], exps[0].astype(BF16)) + dot_nn(
                flipped[1][cols, place], exps[1].astype(BF16)
            )
            out_ref[:, cols] = unstack_heads(result / total).astype(BF16)
            lse_ref[0, pair : pair + 1, :] = top + jnp.log(total)

    run_spans(spans, local, start, active, run)

    @pl.when(jnp.logical_not(active))
    def _():
        out_ref[...] = jnp.zeros_like(out_ref)
        lse_ref[...] = jnp.zeros_like(lse_ref)


def backward_kernel(piece, spans, meta, q_ref, g_ref, lse_ref, *refs):
    pairs_in = refs[:2]
    dq_ref = refs[2]
    outs = refs[3:5]
    flipped = refs[5:7]
    sums = refs[7:9]
    block, local, start, _, active = block_place(meta)
    half = q_ref.shape[1]

    @pl.when(block == 0)
    def _():
        for part in range(2):
            flipped[part][...] = pairs_in[part][:, :half].astype(F32).T.astype(BF16)
            sums[part][...] = jnp.zeros_like(sums[part])

    def run(base, span):
        place = pl.ds(base, span)
        masks = [diagonal_mask(part == 0, piece, meta[2]) for part in range(2)]
        for pair in range(half // PAIR):
            cols = pair_columns(pair)
            value_cols = slice(half + pair * PAIR, half + (pair + 1) * PAIR)
            queries = stack_heads(q_ref[:, cols])
            grads = stack_heads(g_ref[:, cols])
            lse = lse_ref[0, pair : pair + 1, :]
            probs = []
            grad_probs = []
            for part in range(2):
                tile = mask_scores(dot_nt(pairs_in[part][place, cols], queries), masks[part])
                probs.append(jnp.exp(tile - lse))
                grad_probs.append(dot_nt(pairs_in[part][place, value_cols], grads))
            row_dot = jnp.sum(probs[0] * grad_probs[0], 0, keepdims=True) + jnp.sum(
                probs[1] * grad_probs[1], 0, keepdims=True
            )
            grad_query = None
            for part in range(2):
                grad_score = (probs[part] * (grad_probs[part] - row_dot)).astype(BF16)
                sums[part][place, value_cols] += dot_nn(probs[part].astype(BF16), grads)
                sums[part][place, cols] += dot_nn(grad_score, queries)
                term = dot_nn(flipped[part][cols, place], grad_score)
                grad_query = term if grad_query is None else grad_query + term
            dq_ref[:, cols] = unstack_heads(grad_query).astype(BF16)

    run_spans(spans, local, start, active, run)

    @pl.when(jnp.logical_not(active))
    def _():
        dq_ref[...] = jnp.zeros_like(dq_ref)

    @pl.when(block == pl.num_programs(0) - 1)
    def _():
        for part in range(2):
            outs[part][...] = sums[part][...].astype(outs[part].dtype)


def row_spec(width, rows=BLOCK):
    return pl.BlockSpec((rows, width), lambda block, meta: (block, 0))


def whole_spec(rows, width):
    return pl.BlockSpec((rows, width), lambda block, meta: (0, 0))


def lse_spec(group=1):
    return pl.BlockSpec((group, 8, 2 * BLOCK), lambda block, meta: (block, 0, 0))


def kept(shape, kind):
    return jax.ShapeDtypeStruct(shape, kind)


def light_cost():
    return pl.CostEstimate(flops=1000, bytes_accessed=1000, transcendentals=0)


def attend_forward(meta, queries, near, far, piece, spans):
    rows, half = queries.shape
    blocks = rows // BLOCK
    return pl.pallas_call(
        functools.partial(forward_kernel, piece, spans),
        grid_spec=pltpu.PrefetchScalarGridSpec(
            num_scalar_prefetch=1,
            grid=(blocks,),
            in_specs=[row_spec(half)] + [whole_spec(rows, 2 * half)] * 2,
            out_specs=[row_spec(half), lse_spec()],
            scratch_shapes=[pltpu.VMEM((half, rows), BF16)] * 2,
        ),
        out_shape=[kept((rows, half), BF16), kept((blocks, 8, 2 * BLOCK), F32)],
        cost_estimate=light_cost(),
        name="attend_forward",
    )(meta, queries, near, far)


def attend_backward(meta, queries, grads, lse, near, far, piece, spans):
    rows, half = queries.shape
    return pl.pallas_call(
        functools.partial(backward_kernel, piece, spans),
        grid_spec=pltpu.PrefetchScalarGridSpec(
            num_scalar_prefetch=1,
            grid=(rows // BLOCK,),
            in_specs=[row_spec(half), row_spec(half), lse_spec()]
            + [whole_spec(rows, 2 * half)] * 2,
            out_specs=[row_spec(half)] + [whole_spec(rows, 2 * half)] * 2,
            scratch_shapes=[pltpu.VMEM((half, rows), BF16)] * 2
            + [pltpu.VMEM((rows, 2 * half), F32)] * 2,
        ),
        out_shape=[
            kept((rows, half), BF16),
            kept((rows, 2 * half), F32),
            kept((rows, 2 * half), BF16),
        ],
        cost_estimate=light_cost(),
        name="attend_backward",
    )(meta, queries, grads, lse, near, far)


def project_kernel(score_scale, x_ref, wq, wk, wv, bias, q_ref, pair_ref):
    rows = x_ref[...]
    half = q_ref.shape[1]
    q_ref[...] = ((dot_nn(rows, wq[...]) + bias[0:1, :]) * score_scale).astype(BF16)
    pair_ref[:, :half] = dot_nn(rows, wk[...]).astype(BF16)
    pair_ref[:, half:] = (dot_nn(rows, wv[...]) + bias[1:2, :]).astype(BF16)


def project(inputs, weight, bias, score_scale):
    rows, width = inputs.shape
    half = bias.shape[1]
    return pl.pallas_call(
        functools.partial(project_kernel, score_scale),
        grid=(2,),
        in_specs=[plain_rows(rows // 2, width)]
        + [plain_fixed((width, half), 0, i) for i in range(3)]
        + [plain_fixed((4, half))],
        out_specs=[plain_rows(rows // 2, half), plain_rows(rows // 2, 2 * half)],
        out_shape=[kept((rows, half), BF16), kept((rows, 2 * half), BF16)],
        cost_estimate=light_cost(),
        name="project",
    )(inputs, weight, weight, weight, bias)


def grads_kernel(sides, counts, factors, extra_steps, fills, kind, meta, *refs):
    lefts = refs[: max(sides) + 1]
    rights = refs[len(lefts) : len(lefts) + len(counts)]
    extra_ref = refs[len(lefts) + len(counts)]
    out_ref = refs[-1]
    step = pl.program_id(0)
    begin = 0
    for index, count in enumerate(counts):
        extra = begin < extra_steps

        @pl.when((step >= begin) & (step < begin + count))
        def _(index=index, extra=extra):
            result = dot_tn(lefts[sides[index]][...], rights[index][...])
            if factors[index] != 1.0:
                result = result * factors[index]
            if kind == PLAIN:
                if extra:
                    result = result + extra_ref[...].astype(F32)
                out_ref[...] = result.astype(BF16)
                return
            size = out_ref.shape[2]
            for plane in range(4):
                for low in range(4):
                    row = (plane * 4 + low) * size
                    place = pl.ds(low if kind == FIXED else meta[0] ^ low, 1)
                    part = result[row : row + size]
                    if extra:
                        part = part + extra_ref[place, plane].astype(F32)[0]
                    out_ref[place, plane] = part.astype(BF16)[None]

        begin += count


def weight_grads(meta, lefts, rights, sides, factors, kind, extra=None, room=None, into=None):
    chunk = min(2 * 384, rights[0].shape[1])
    shifts = [right[1] if isinstance(right, tuple) else 0 for right in rights]
    counts = [1 if isinstance(right, tuple) else right.shape[1] // chunk for right in rights]
    rights = [right[0] if isinstance(right, tuple) else right for right in rights]
    width = lefts[0].shape[1]
    steps = sum(counts)
    total = room or steps * chunk
    start = total // chunk - steps if into is not None else 0
    begins = [sum(counts[:i]) for i in range(len(counts))]

    def right_spec(index):
        return pl.BlockSpec(
            (rights[index].shape[0], chunk),
            lambda step, meta: (
                0,
                shifts[index] + jnp.clip(step - begins[index], 0, counts[index] - 1),
            ),
        )

    def tile_spec(place):
        if kind == PLAIN:
            return pl.BlockSpec((width, chunk), lambda step, meta: (0, place(step)))
        return pl.BlockSpec(
            (4, 4, width // 16, chunk), lambda step, meta: (0, 0, 0, place(step))
        )

    extra_steps = extra.shape[-1] // chunk if extra is not None else 0
    operands = [*lefts, *rights]
    specs = [pl.BlockSpec(left.shape, lambda step, meta: (0, 0)) for left in lefts]
    specs += [right_spec(index) for index in range(len(rights))]
    if extra is not None:
        operands.append(extra)
        specs.append(tile_spec(lambda step: jnp.minimum(step, extra_steps - 1)))
    if into is not None:
        operands.append(into)
        specs.append(pl.BlockSpec(memory_space=pl.ANY))
    return pl.pallas_call(
        functools.partial(
            grads_kernel, sides, counts, factors, extra_steps, into is not None, kind
        ),
        grid_spec=pltpu.PrefetchScalarGridSpec(
            num_scalar_prefetch=1,
            grid=(steps,),
            in_specs=specs,
            out_specs=tile_spec(lambda step: start + step),
        ),
        out_shape=jax.ShapeDtypeStruct(
            (width, total) if kind == PLAIN else (4, 4, width // 16, total), BF16
        ),
        input_output_aliases={len(operands): 0} if into is not None else {},
        cost_estimate=light_cost(),
        name="weight_grads",
    )(meta, *operands)


def norm_forward(hidden, gain, shift):
    center = hidden - jnp.mean(hidden, -1, keepdims=True)
    spread = jnp.mean(center * center, -1, keepdims=True)
    scale = lax.rsqrt(spread + EPSILON)
    unit = center * scale
    return unit * gain + shift, unit, scale


def norm_gradient(grad, unit, scale, gain):
    inner = grad * gain
    mean_inner = jnp.mean(inner, -1, keepdims=True)
    mean_unit = jnp.mean(inner * unit, -1, keepdims=True)
    return scale * (inner - mean_inner - unit * mean_unit)


def norm_backward(grad, unit, scale, gain):
    return norm_gradient(grad, unit, scale, gain), jnp.sum(grad * unit, 0), jnp.sum(grad, 0)


def sub_blocks(meta, keys_each, run, skip):
    def one(sub, carry):
        block = pl.program_id(0) * GROUP + sub
        second = (block >= meta[0]).astype(jnp.int32)
        place = pl.ds(pl.multiple_of(second * keys_each, keys_each), keys_each)
        rows = pl.ds(pl.multiple_of(sub * BLOCK, BLOCK), BLOCK)
        pl.when(block < meta[1])(functools.partial(run, sub, rows, place))
        pl.when(block >= meta[1])(functools.partial(skip, sub, rows))
        return carry

    lax.fori_loop(0, GROUP, one, 0)


def mid_forward_kernel(score_scale, meta, x_ref, attn0, attn1, memory_ref, *refs):
    attn = (attn0, attn1)
    self_out, query_w, memory_k, memory_v, cross_out = [refs[2 * i : 2 * i + 2] for i in range(5)]
    bias0, bias1, out_bias, gain, shift = refs[10:15]
    unit1_ref, scale1_ref, unit2_ref, scale2_ref, cross_in_ref, hidden_ref, lse_ref = refs[15:22]
    cq_refs, cattn_refs, ck_refs, cv_refs = [refs[22 + 2 * i : 24 + 2 * i] for i in range(4)]
    flipped = refs[30:32]
    half = attn0.shape[1]
    keys_each = memory_ref.shape[0] // 2

    @pl.when(pl.program_id(0) == 0)
    def _():
        for h, bias in enumerate((bias0, bias1)):
            ck_refs[h][...] = dot_nn(memory_ref[...], memory_k[h][...]).astype(BF16)
            value = dot_nn(memory_ref[...], memory_v[h][...]) + bias[3:4, :]
            cv_refs[h][...] = value.astype(BF16)
            flipped[h][...] = value.T.astype(BF16)

    branch = dot_nt(attn[0][...], self_out[0][...]) + dot_nt(attn[1][...], self_out[1][...])
    n1, unit1, scale1 = norm_forward(
        x_ref[...].astype(F32) + branch + out_bias[0:1, :], gain[0:1, :], shift[0:1, :]
    )
    unit1_ref[...] = unit1
    scale1_ref[...] = scale1
    cross_in = n1.astype(BF16)
    cross_in_ref[...] = cross_in
    for h, bias in enumerate((bias0, bias1)):
        query = (dot_nn(cross_in, query_w[h][...]) + bias[2:3, :]) * score_scale
        cq_refs[h][...] = query.astype(BF16)

    def run(sub, rows, place):
        for h in range(2):
            for pair in range(half // PAIR):
                cols = pair_columns(pair)
                tile = dot_nt(ck_refs[h][place, cols], stack_heads(cq_refs[h][rows, cols]))
                top = jnp.max(tile, 0, keepdims=True)
                exps = jnp.exp(tile - top)
                total = jnp.sum(exps, 0, keepdims=True)
                result = dot_nn(flipped[h][cols, place], exps.astype(BF16))
                cattn_refs[h][rows, cols] = unstack_heads(result / total).astype(BF16)
                row = h * (half // PAIR) + pair
                lse_ref[sub, row : row + 1, :] = top + jnp.log(total)

    def skip(sub, rows):
        lse_ref[sub] = jnp.zeros(lse_ref.shape[1:], F32)
        for h in range(2):
            cattn_refs[h][rows, :] = jnp.zeros((BLOCK, half), BF16)

    sub_blocks(meta, keys_each, run, skip)
    branch = dot_nt(cattn_refs[0][...], cross_out[0][...]) + dot_nt(
        cattn_refs[1][...], cross_out[1][...]
    )
    n1 = unit1_ref[...] * gain[0:1, :] + shift[0:1, :]
    n2, unit2, scale2 = norm_forward(n1 + branch + out_bias[1:2, :], gain[1:2, :], shift[1:2, :])
    unit2_ref[...] = unit2
    scale2_ref[...] = scale2
    hidden_ref[...] = n2.astype(BF16)


def mid_backward_kernel(score_scale, total_rows, meta, dn2_ref, unit2_ref, scale2_ref, unit1_ref, scale1_ref, lse_ref, *refs):
    cq_refs, ck_refs, cv_refs = [refs[2 * i : 2 * i + 2] for i in range(3)]
    self_out, query_w, cross_out = [refs[6 + 2 * i : 8 + 2 * i] for i in range(3)]
    gain = refs[12]
    dy2_ref, dh1_ref, dy_ref, sums_ref = refs[13:17]
    dcq_refs, da_refs = refs[17:19], refs[19:21]
    near_ref, far_ref = refs[21:23]
    dca_refs, flipped, dck_refs, dcv_refs = [refs[23 + 2 * i : 25 + 2 * i] for i in range(4)]
    half = cq_refs[0].shape[1]
    keys_each = ck_refs[0].shape[0] // 2
    here = pl.program_id(0) * GROUP * BLOCK + lax.broadcasted_iota(
        jnp.int32, (GROUP * BLOCK, 1), 0
    )
    inside = here < total_rows

    def load(ref):
        return jnp.where(inside, ref[...], 0.0)

    @pl.when(pl.program_id(0) == 0)
    def _():
        sums_ref[...] = jnp.zeros_like(sums_ref)
        for h in range(2):
            flipped[h][...] = ck_refs[h][...].astype(F32).T.astype(BF16)
            dck_refs[h][...] = jnp.zeros_like(dck_refs[h])
            dcv_refs[h][...] = jnp.zeros_like(dcv_refs[h])

    dn2 = load(dn2_ref)
    unit2 = load(unit2_ref)
    dh2 = norm_gradient(dn2, unit2, load(scale2_ref), gain[1:2, :])
    dh1_ref[...] = dh2
    dy2 = dh2.astype(BF16)
    dy2_ref[...] = dy2
    sums_ref[0:1, :] += jnp.sum(dn2 * unit2, 0, keepdims=True)
    sums_ref[1:2, :] += jnp.sum(dn2, 0, keepdims=True)
    sums_ref[2:3, :] += jnp.sum(dy2.astype(F32), 0, keepdims=True)
    for h in range(2):
        dca_refs[h][...] = dot_nn(dy2, cross_out[h][...]).astype(BF16)

    def run(sub, rows, place):
        for h in range(2):
            for pair in range(half // PAIR):
                cols = pair_columns(pair)
                row = h * (half // PAIR) + pair
                queries = stack_heads(cq_refs[h][rows, cols])
                grads = stack_heads(dca_refs[h][rows, cols])
                tile = dot_nt(ck_refs[h][place, cols], queries)
                probs = jnp.exp(tile - lse_ref[sub, row : row + 1, :])
                grad_probs = dot_nt(cv_refs[h][place, cols], grads)
                row_dot = jnp.sum(probs * grad_probs, 0, keepdims=True)
                grad_score = (probs * (grad_probs - row_dot)).astype(BF16)
                dcv_refs[h][place, cols] += dot_nn(probs.astype(BF16), grads)
                dck_refs[h][place, cols] += dot_nn(grad_score, queries)
                term = dot_nn(flipped[h][cols, place], grad_score)
                dcq_refs[h][rows, cols] = unstack_heads(term).astype(BF16)

    def skip(sub, rows):
        for h in range(2):
            dcq_refs[h][rows, :] = jnp.zeros((BLOCK, half), BF16)

    sub_blocks(meta, keys_each, run, skip)
    dn1 = dh1_ref[...]
    for h in range(2):
        dcq = dcq_refs[h][...]
        dn1 = dn1 + score_scale * dot_nt(dcq, query_w[h][...])
        sums_ref[6:7, h * half : (h + 1) * half] += jnp.sum(dcq.astype(F32), 0, keepdims=True)
    unit1 = load(unit1_ref)
    dh1 = norm_gradient(dn1, unit1, load(scale1_ref), gain[0:1, :])
    dy = dh1.astype(BF16)
    dh1_ref[...] = dh1
    dy_ref[...] = dy
    sums_ref[3:4, :] += jnp.sum(dn1 * unit1, 0, keepdims=True)
    sums_ref[4:5, :] += jnp.sum(dn1, 0, keepdims=True)
    sums_ref[5:6, :] += jnp.sum(dy.astype(F32), 0, keepdims=True)
    for h in range(2):
        da_refs[h][...] = dot_nn(dy, self_out[h][...]).astype(BF16)

    @pl.when(pl.program_id(0) == pl.num_programs(0) - 1)
    def _():
        own = keys_each // 2
        for index, ref in enumerate((dck_refs[0], dck_refs[1], dcv_refs[0], dcv_refs[1])):
            near_ref[:, index * half : (index + 1) * half] = ref[...]
            far = slice((index ^ 1) * half, ((index ^ 1) + 1) * half)
            for seq in range(2):
                base = seq * keys_each
                middle, end = base + own, base + keys_each
                far_ref[middle:end, far] = ref[base:middle, :].astype(BF16)
                far_ref[base:middle, far] = ref[middle:end, :].astype(BF16)


def memory_backward_kernel(near_ref, got_ref, wk0, wv0, wk1, wv1, sum_ref, encoder_ref, bias_ref):
    total = (near_ref[...] + got_ref[...].astype(F32)).astype(BF16)
    half = wk0.shape[1]
    sum_ref[:, :half] = total[:, :half]
    sum_ref[:, half:] = total[:, 2 * half : 3 * half]
    own = total.shape[0] // 4
    mine = jnp.concatenate([total[:own], total[2 * own : 3 * own]], 0)
    grad = dot_nt(mine[:, :half], wk0[...]) + dot_nt(mine[:, half : 2 * half], wk1[...])
    grad = grad + dot_nt(mine[:, 2 * half : 3 * half], wv0[...])
    encoder_ref[...] = (grad + dot_nt(mine[:, 3 * half :], wv1[...])).astype(BF16)
    bias = jnp.sum(mine[:, 2 * half :].astype(F32), 0, keepdims=True)
    bias_ref[...] = jnp.broadcast_to(bias, bias_ref.shape)


def memory_backward(near, got, mid):
    rows, span = near.shape
    half = span // 4
    width = mid[0][0].shape[0]
    columns = [plain_fixed((width, half), 0, m[1] + c) for m in mid for c in (3, 4)]
    return pl.pallas_call(
        memory_backward_kernel,
        grid=(1,),
        in_specs=[plain_fixed((rows, span))] * 2 + columns,
        out_specs=[
            plain_fixed((rows, 2 * half)),
            plain_fixed((rows // 2, width)),
            plain_fixed((8, 2 * half)),
        ],
        out_shape=[
            kept((rows, 2 * half), BF16),
            kept((rows // 2, width), BF16),
            kept((8, 2 * half), F32),
        ],
        cost_estimate=light_cost(),
        name="memory_backward",
    )(near, got, *[m[0] for m in mid for _ in range(2)])


def ffn_forward_kernel(first, hidden_ref, base_ref, expand, reduce, bias, gain, shift, act_ref, slope_ref, total_ref):
    pre = dot_nn(hidden_ref[...], expand[...]) + bias[0:1, :]
    phi = 0.5 * (1.0 + lax.erf(pre * (1.0 / math.sqrt(2.0))))
    density = jnp.exp(-0.5 * pre * pre) * (1.0 / math.sqrt(2.0 * math.pi))
    act = (pre * phi).astype(BF16)
    act_ref[...] = act
    slope_ref[...] = (phi + pre * density).astype(BF16)
    base = base_ref[...]
    if first:
        base = base * gain[0:1, :] + shift[0:1, :]
    total_ref[...] = base + dot_nt(act, reduce[...])


def ffn_forward(first, hidden, base, weight, bias, gain, shift):
    rows, width = hidden.shape
    units = bias.shape[1]
    tall = rows // 4
    wide, long = plain_rows(tall, width), plain_rows(tall, units)

    def side(column):
        return pl.BlockSpec(
            (width, units), lambda step: (0, column), pipeline_mode=pl.Buffered(1)
        )

    return pl.pallas_call(
        functools.partial(ffn_forward_kernel, first),
        grid=(4,),
        in_specs=[wide, wide, side(0), side(1), plain_fixed((1, units))]
        + [plain_fixed((1, width))] * 2,
        out_specs=[long, long, wide],
        out_shape=[
            kept((rows, units), BF16),
            kept((rows, units), BF16),
            kept((rows, width), F32),
        ],
        cost_estimate=light_cost(),
        name="ffn_forward",
    )(hidden, base, weight, weight, bias, gain, shift)


def ffn_backward_kernel(h3_ref, cot_ref, valid_ref, slope0, slope1, in0, in1, out0, out1, gain, shift, n3_ref, dz_ref, dn2_ref, sums_ref, du0, du1, usum0, usum1):
    @pl.when(pl.program_id(0) == 0)
    def _():
        for ref in (sums_ref, usum0, usum1):
            ref[...] = jnp.zeros_like(ref)

    n3, unit, scale = norm_forward(h3_ref[...], gain[2:3, :], shift[2:3, :])
    valid = valid_ref[...] > 0.5
    n3_ref[...] = jnp.where(valid, n3, 0.0).astype(BF16)
    dn3 = jnp.where(valid, cot_ref[...].astype(F32), 0.0)
    dh3 = norm_gradient(dn3, unit, scale, gain[2:3, :])
    dz = dh3.astype(BF16)
    dz_ref[...] = dz
    sums_ref[0:1, :] += jnp.sum(dn3 * unit, 0, keepdims=True)
    sums_ref[1:2, :] += jnp.sum(dn3, 0, keepdims=True)
    sums_ref[2:3, :] += jnp.sum(dz.astype(F32), 0, keepdims=True)
    total = dh3
    sides = ((slope0, out0, in0, du0, usum0), (slope1, out1, in1, du1, usum1))
    for slope, reduce, expand, du_ref, usum in sides:
        du = (dot_nn(dz, reduce[...]) * slope[...].astype(F32)).astype(BF16)
        du_ref[...] = du
        usum[0:1, :] += jnp.sum(du.astype(F32), 0, keepdims=True)
        total = total + dot_nt(du, expand[...])
    dn2_ref[...] = total


def ffn_backward(h3, cot, valid, slope, ffn, gain, shift):
    rows, width = h3.shape
    units = slope[0].shape[1]
    wide, thin, long = [plain_rows(rows // 2, w) for w in (width, 1, units)]

    def side(column):
        return pl.BlockSpec(
            (width, units), lambda step: (0, column), pipeline_mode=pl.Buffered(1)
        )

    return pl.pallas_call(
        ffn_backward_kernel,
        grid=(2,),
        in_specs=[wide, wide, thin, long, long, side(0), side(0), side(1), side(1)]
        + [plain_fixed((3, width))] * 2,
        out_specs=[wide, wide, wide, plain_fixed((8, width)), long, long]
        + [plain_fixed((8, units))] * 2,
        out_shape=[
            kept((rows, width), BF16),
            kept((rows, width), BF16),
            kept((rows, width), F32),
            kept((8, width), F32),
            kept((rows, units), BF16),
            kept((rows, units), BF16),
            kept((8, units), F32),
            kept((8, units), F32),
        ],
        cost_estimate=pl.CostEstimate(flops=1000, bytes_accessed=1000, transcendentals=0),
        name="ffn_backward",
    )(h3, cot, valid, *slope, ffn[0], ffn[1], ffn[0], ffn[1], gain, shift)


def fixed_spec(shape, *index):
    place = index or (0,) * len(shape)
    return pl.BlockSpec(shape, lambda block, meta: place)


def mid_forward(meta, inputs, attn, memory, mid, in_pair, out_bias, gain, shift, score_scale):
    rows, width = inputs.shape
    half = attn[0].shape[1]
    blocks = rows // BLOCK
    memory_rows = memory.shape[0]
    weights = [fixed_spec((width, half), 0, m[1] + c) for c in (0, 1, 3, 4, 2) for m in mid]
    tall = GROUP * BLOCK
    wide, thin, narrow = row_spec(width, tall), row_spec(1, tall), row_spec(half, tall)
    memory_spec = fixed_spec((memory_rows, half))
    outs = pl.pallas_call(
        functools.partial(mid_forward_kernel, score_scale),
        grid_spec=pltpu.PrefetchScalarGridSpec(
            num_scalar_prefetch=1,
            grid=(pl.cdiv(blocks, GROUP),),
            in_specs=[wide, narrow, narrow, fixed_spec(memory.shape)]
            + weights
            + [fixed_spec((4, half))] * 2
            + [fixed_spec((3, width))] * 3,
            out_specs=[wide, thin, wide, thin, wide, wide, lse_spec(GROUP)]
            + [narrow] * 4
            + [memory_spec] * 4,
            scratch_shapes=[pltpu.VMEM((half, memory_rows), BF16)] * 2,
        ),
        out_shape=[
            kept((rows, width), F32),
            kept((rows, 1), F32),
            kept((rows, width), F32),
            kept((rows, 1), F32),
            kept((rows, width), BF16),
            kept((rows, width), BF16),
            kept((blocks, 8, 2 * BLOCK), F32),
        ]
        + [kept((rows, half), BF16)] * 4
        + [kept((memory_rows, half), BF16)] * 4,
        cost_estimate=pl.CostEstimate(
            flops=(24 * rows * width * half) // LIGHT, bytes_accessed=(20 * rows * width) // LIGHT, transcendentals=0
        ),
        name="mid_forward",
    )(meta, inputs, *attn, memory, *[m[0] for _ in range(5) for m in mid], *in_pair, out_bias, gain, shift)
    return outs[:7], outs[7:9], outs[9:11], outs[11:13], outs[13:15]


def mid_backward(meta, dn2, saved, cq, ck, cv, mid, gain, score_scale):
    unit1, scale1, unit2, scale2, lse = saved
    rows, width = dn2.shape
    half = cq[0].shape[1]
    blocks = rows // BLOCK
    memory_rows = ck[0].shape[0]
    tall = GROUP * BLOCK
    wide, thin, narrow = row_spec(width, tall), row_spec(1, tall), row_spec(half, tall)
    memory_spec = fixed_spec((memory_rows, half))
    weights = [fixed_spec((width, half), 0, m[1] + c) for c in (0, 1, 2) for m in mid]
    outs = pl.pallas_call(
        functools.partial(mid_backward_kernel, score_scale, rows),
        grid_spec=pltpu.PrefetchScalarGridSpec(
            num_scalar_prefetch=1,
            grid=(pl.cdiv(blocks, GROUP),),
            in_specs=[wide, wide, thin, wide, thin, lse_spec(GROUP)]
            + [narrow] * 2
            + [memory_spec] * 4
            + weights
            + [fixed_spec((3, width))],
            out_specs=[wide, wide, wide, fixed_spec((8, width))]
            + [narrow] * 4
            + [fixed_spec((memory_rows, 4 * half))] * 2,
            scratch_shapes=[pltpu.VMEM((tall, half), BF16)] * 2
            + [pltpu.VMEM((half, memory_rows), BF16)] * 2
            + [pltpu.VMEM((memory_rows, half), F32)] * 4,
        ),
        out_shape=[
            kept((rows, width), BF16),
            kept((rows, width), F32),
            kept((rows, width), BF16),
            kept((8, width), F32),
        ]
        + [kept((rows, half), BF16)] * 4
        + [kept((memory_rows, 4 * half), F32), kept((memory_rows, 4 * half), BF16)],
        cost_estimate=pl.CostEstimate(
            flops=(24 * rows * width * half) // LIGHT, bytes_accessed=(20 * rows * width) // LIGHT, transcendentals=0
        ),
        name="mid_backward",
    )(meta, dn2, unit2, scale2, unit1, scale1, lse, *cq, *ck, *cv, *[m[0] for _ in range(3) for m in mid], gain)
    return outs[:4], outs[4:6], outs[6:8], outs[8], outs[9]


def input_backward_kernel(score_scale, base_ref, dq_ref, own_ref, got_ref, wq, wk, wv, dx_ref, pair_ref, sums_ref):
    @pl.when(pl.program_id(0) == 0)
    def _():
        sums_ref[...] = jnp.zeros_like(sums_ref)

    half = dq_ref.shape[1]
    pair = (own_ref[...] + got_ref[...].astype(F32)).astype(BF16)
    pair_ref[...] = pair
    dq = dq_ref[...]
    dk, dv = pair[:, :half], pair[:, half:]
    sums_ref[0:1, :] += score_scale * jnp.sum(dq.astype(F32), 0, keepdims=True)
    sums_ref[1:2, :] += jnp.sum(dv.astype(F32), 0, keepdims=True)
    total = score_scale * dot_nt(dq, wq[...]) + dot_nt(dk, wk[...]) + dot_nt(dv, wv[...])
    dx_ref[...] = (base_ref[...] + total).astype(dx_ref.dtype)


def plain_rows(rows, width):
    return pl.BlockSpec((rows, width), lambda step: (step, 0))


def plain_fixed(shape, *index):
    place = index or (0,) * len(shape)
    return pl.BlockSpec(shape, lambda step: place)


def input_backward(base, dq, own, got, weight, score_scale, kind):
    rows, width = base.shape
    half = dq.shape[1]
    tall = rows // 2
    return pl.pallas_call(
        functools.partial(input_backward_kernel, score_scale),
        grid=(2,),
        in_specs=[plain_rows(tall, width), plain_rows(tall, half)]
        + [plain_rows(tall, 2 * half)] * 2
        + [plain_fixed((width, half), 0, i) for i in range(3)],
        out_specs=[plain_rows(tall, width), plain_rows(tall, 2 * half), plain_fixed((8, half))],
        out_shape=[
            kept((rows, width), kind),
            kept((rows, 2 * half), BF16),
            kept((8, half), F32),
        ],
        cost_estimate=light_cost(),
        name="input_backward",
    )(base, dq, own, got, weight, weight, weight)


def swap(value):
    return lax.ppermute(value, "tensor", [(0, 1), (1, 0)])


def hop(value, bits):
    return lax.ppermute(value, "dp", [(i, i ^ bits) for i in range(16)])


def assemble_kernel(meta, own_ref, first_ref, second_ref, third_ref, out_ref):
    for low, ref in enumerate((own_ref, first_ref, second_ref, third_ref)):
        out_ref[0, pl.ds(meta[1] ^ low, 1)] = ref[...]


def plane_line(value):
    return jnp.stack([value, hop(value, 4), hop(value, 8), hop(value, 12)])


def low_groups(line):
    return (line, hop(line, 1), hop(line, 2), hop(line, 3))


def assemble(groups):
    rows, count = groups[0].shape[1:]
    index = lax.axis_index("dp")
    meta = jnp.stack([index // 4, index % 4]).astype(jnp.int32)
    spec = pl.BlockSpec((1, rows, count), lambda i, meta: (i ^ meta[0], 0, 0))
    full = pl.pallas_call(
        assemble_kernel,
        grid_spec=pltpu.PrefetchScalarGridSpec(
            num_scalar_prefetch=1,
            grid=(4,),
            in_specs=[spec] * 4,
            out_specs=pl.BlockSpec((1, 4, rows, count), lambda i, meta: (i, 0, 0, 0)),
        ),
        out_shape=kept((4, 4, rows, count), groups[0].dtype),
        cost_estimate=light_cost(),
        name="assemble",
    )(meta, *groups)
    return full.reshape(16 * rows, count)


def total_of(parts):
    return functools.reduce(jnp.add, [part.astype(F32) for part in parts])


def scatter_low(groups):
    received = [hop(groups[low], low) for low in (1, 2, 3)]
    return total_of([groups[0]] + received).astype(BF16)


def scatter_plane(line):
    plane = lax.axis_index("dp") // 4

    def pick(other):
        return lax.dynamic_index_in_dim(line, plane ^ other, 0, keepdims=False)

    received = [hop(pick(other), 4 * other) for other in (1, 2, 3)]
    return total_of([pick(0)] + received)


def wide_scatter(value, groups=None):
    return lax.psum_scatter(
        value, "dp", scatter_dimension=0, tiled=True, axis_index_groups=groups
    )


def sum_low(value):
    return total_of([value] + [hop(value, bits) for bits in (1, 2, 3)])


def sum_planes(value):
    return total_of([value] + [hop(value, 4 * bits) for bits in (1, 2, 3)])


def rows_at(value, ids):
    return value.at[ids].get(mode="promise_in_bounds")


def tie(*values):
    return lax.optimization_barrier(values)


def body(
    tokens,
    encoder,
    lengths,
    deal,
    self_project,
    self_output,
    cross_query,
    cross_memory,
    cross_output,
    hidden_in,
    hidden_out,
    in_bias,
    out_bias,
    hidden_bias,
    norm_gain,
    norm_bias,
    cotangent,
):
    score_scale = 1.0 / math.sqrt(HD)
    dp_count = lax.axis_size("dp")
    dp_index = lax.axis_index("dp")
    tensor_index = lax.axis_index("tensor")
    piece = tokens.shape[1]
    width = tokens.shape[2]
    slots = piece * dp_count
    half = self_project.shape[2]
    units = hidden_in.shape[1]
    shard = self_project.shape[0]
    memory_rows = encoder.shape[1]
    spans = slots // BLOCK
    blocks = (slots + slots // 2) // BLOCK + 1
    rows = blocks * BLOCK
    per_block = BLOCK // piece

    pair_ids = lax.dynamic_slice_in_dim(deal, 2 * dp_index, 2)
    pair_len = rows_at(lengths, pair_ids)
    pieces_used = (pair_len + 2 * piece - 1) // (2 * piece)
    blocks_used = (pieces_used * piece + BLOCK - 1) // BLOCK
    first_blocks = blocks_used[0]
    all_blocks = first_blocks + blocks_used[1]
    meta = jnp.stack([first_blocks, all_blocks, tensor_index]).astype(jnp.int32)

    block_ids = jnp.arange(blocks, dtype=jnp.int32)
    block_seq = (block_ids >= first_blocks).astype(jnp.int32)
    block_local = jnp.minimum(block_ids - block_seq * first_blocks, spans - 1)
    piece_ids = (
        (block_local[:, None] * per_block + jnp.arange(per_block, dtype=jnp.int32)[None, :]) * 2
        + block_seq[:, None]
    ).reshape(-1)
    slot_ids = block_local[:, None] * BLOCK + jnp.arange(BLOCK, dtype=jnp.int32)[None, :]
    positions = ((slot_ids // piece) * 2 + tensor_index) * piece + slot_ids % piece
    row_valid = (
        (positions < jnp.where(block_seq == 1, pair_len[1], pair_len[0])[:, None])
        & (block_ids < all_blocks)[:, None]
    ).reshape(rows, 1)

    send_piece = jnp.arange(dp_count, dtype=jnp.int32)
    spare = jnp.where(
        pieces_used[0] % per_block != 0, first_blocks * per_block - 1, rows // piece - 1
    )
    send_start = jnp.stack([0 * first_blocks, first_blocks * per_block])
    send_ids = jnp.where(
        send_piece[:, None] < pieces_used[None, :],
        send_start[None, :] + send_piece[:, None],
        spare,
    ).reshape(-1)
    inverse = jnp.zeros_like(deal).at[deal].set(jnp.arange(deal.shape[0], dtype=jnp.int32))

    def home_pieces(value):
        return rows_at(value.reshape(rows // piece, piece, width), send_ids)

    def go_home(outgoing):
        return lax.all_to_all(outgoing, "dp", split_axis=0, concat_axis=0, tiled=True)

    def order(value):
        return rows_at(value, deal)

    def arrive(ordered):
        return lax.all_to_all(ordered, "dp", split_axis=0, concat_axis=0, tiled=True)

    def pack(arrived, ids):
        return rows_at(arrived, ids).reshape(rows, width)

    quick = dp_count == 16
    both = (0, 1)
    biases = jnp.concatenate([in_bias.reshape(-1), hidden_bias])
    bias_pair = (biases, swap(biases))
    in_pair = [b[: 4 * half].reshape(4, half) for b in bias_pair]
    hidden_pair = [b[None, 4 * half :] for b in bias_pair]

    memory_full = jnp.concatenate([encoder, swap(encoder)], 1).reshape(4 * memory_rows, width)
    affine = (norm_gain[1:2], norm_bias[1:2] + out_bias[2:3])
    early = (row_valid.astype(F32), affine, in_pair, hidden_pair, meta, piece_ids, memory_full, send_ids, inverse)
    ordered = order(tokens)
    qkv_shard_in = self_project.reshape(shard, 3 * half)
    mid_shard_in = jnp.concatenate(
        [self_output.T, cross_query, cross_output.T, cross_memory.reshape(shard, 2 * half)], 1
    )

    def slow_gather(value):
        return lax.all_gather(value, "dp", axis=0, tiled=True)

    ordered_cot = order(cotangent)
    if quick:
        qkv_line = plane_line(qkv_shard_in)
        qkv_line, ordered = tie(qkv_line, ordered)
        qkv_groups = low_groups(qkv_line)
        arrived = arrive(ordered)
        ordered_cot, arrived, qkv_groups, early = tie(ordered_cot, arrived, qkv_groups, early)
        qkv_own = assemble(qkv_groups)
    else:
        arrived = arrive(ordered)
        qkv_own = slow_gather(qkv_shard_in)
    qkv_weight = (qkv_own, swap(qkv_own))
    valid_rows, affine, in_pair, hidden_pair, meta, piece_ids, memory_full = early[:7]
    send_ids, inverse = early[7:]
    inputs = pack(arrived, piece_ids)
    arrived_cot = arrive(ordered_cot)

    rest_own = slow_gather(jnp.concatenate([hidden_in, hidden_out.T, mid_shard_in], 1))

    def columns(pair, start, count):
        return [lax.slice_in_dim(pair[h], start, start + count, axis=1) for h in both]


    queries = [None, None]
    near = [None, None]
    attn = [None, None]
    lse = [None, None]
    for h in both:
        queries[h], near[h] = project(inputs, qkv_weight[h], in_pair[h], score_scale)
    far = [swap(near[1 - h]) for h in both]
    attn[1], lse[1] = attend_forward(meta, queries[1], near[1], far[1], piece, spans)
    attn[1], queries[0], far[0] = tie(attn[1], queries[0], far[0])
    attn[0], lse[0] = attend_forward(meta, queries[0], near[0], far[0], piece, spans)
    rest_own, attn[0] = tie(rest_own, attn[0])
    rest_far = swap(rest_own)
    mid_weight = [(rest, 2 * units // half) for rest in (rest_own, rest_far)]
    saved, cqs, cattn, cks, cvs = mid_forward(
        meta, inputs, attn, memory_full, mid_weight, in_pair, out_bias, norm_gain, norm_bias, score_scale
    )
    unit1, scale1, unit2, scale2, cross_in, hidden, clse = saved
    act = [None, None]
    slope = [None, None]
    act[0], slope[0], total = ffn_forward(
        True, hidden, unit2, rest_own, hidden_pair[0], *affine
    )
    act[1], slope[1], total = ffn_forward(
        False, hidden, total, rest_far, hidden_pair[1], *affine
    )
    arrived_cot, total = tie(arrived_cot, total)
    ffn_weight = (rest_own, rest_far)
    n3, dz, dn2, sums3, du0, du1, usum0, usum1 = ffn_backward(
        total, pack(arrived_cot, piece_ids), valid_rows, slope, ffn_weight, norm_gain, norm_bias
    )
    du = (du0, du1)
    output_back = go_home(home_pieces(n3))

    low_meta = jnp.reshape(dp_index % 4, (1,)).astype(jnp.int32)

    fixed = FIXED if quick else PLAIN
    one = (0,)
    far_in = weight_grads(low_meta, [hidden], [du[1]], one, (1.0,), fixed)
    far_out = weight_grads(low_meta, [dz], [act[1]], one, (1.0,), fixed)
    ffn_grads = weight_grads(
        low_meta, [hidden], [du[0]], one, (1.0,), fixed, swap(far_in), 2 * units
    )
    ffn_grads = weight_grads(
        low_meta, [dz], [act[0]], one, (1.0,), fixed, swap(far_out), 2 * units, ffn_grads
    )
    ffn_grads, dn2 = tie(ffn_grads, dn2)
    ffn_line = wide_scatter(ffn_grads.reshape(width, 2 * units), LOW_GROUPS if quick else None)
    rows_back, dcq, da, memory_near, memory_far = mid_backward(
        meta, dn2, (unit1, scale1, unit2, scale2, clse), cqs, cks, cvs, mid_weight, norm_gain, score_scale
    )
    dy2, dh1, dy, sums = rows_back
    da = list(da)
    memory_far, output_back = tie(memory_far, output_back)
    memory_sum, grad_memory, memory_bias = memory_backward(
        memory_near, swap(memory_far), mid_weight
    )
    grad_encoder = grad_memory.reshape(2, memory_rows, width)
    mid_factors = (1.0, score_scale, 1.0, 1.0, 1.0)
    far_mid = weight_grads(
        low_meta,
        [dy, cross_in, dy2],
        [attn[1], dcq[1], cattn[1]],
        (0, 1, 2),
        mid_factors[:3],
        fixed,
    )
    mid_grads = weight_grads(
        low_meta,
        [dy, cross_in, dy2, memory_full],
        [attn[0], dcq[0], cattn[0], (memory_sum, 0), (memory_sum, 1)],
        (0, 1, 2, 3, 3),
        mid_factors,
        fixed,
        swap(far_mid),
    )
    mid_grads, da[0], da[1] = tie(mid_grads, da[0], da[1])
    mid_line = wide_scatter(mid_grads.reshape(width, 5 * half), LOW_GROUPS if quick else None)
    dq = [None, None]
    own = [None, None]
    out = [None, None]
    for h in both:
        dq[h], own[h], out[h] = attend_backward(
            meta, queries[h], da[h], lse[h], near[h], far[h], piece, spans
        )
        if h == 0:
            da[1], dq[0], ffn_line = tie(da[1], dq[0], ffn_line)
    factors = (score_scale, 1.0, 1.0)
    got_far, got_near = swap(out[0]), swap(out[1])
    dx_far, pair_far, sums_far = input_backward(
        dh1, dq[1], own[1], got_far, qkv_weight[1], score_scale, F32
    )
    relative = RELATIVE if quick else PLAIN
    far_grads = weight_grads(
        low_meta, [inputs], [dq[1], (pair_far, 0), (pair_far, 1)], (0, 0, 0), factors, relative
    )
    far_grads, dx_far, got_near, ffn_line = tie(far_grads, dx_far, got_near, ffn_line)
    far_grads = swap(far_grads)
    dx, pair_near, sums_near = input_backward(
        dx_far, dq[0], own[0], got_near, qkv_weight[0], score_scale, BF16
    )
    grad_out = home_pieces(dx)
    grad_out, far_grads, output_back = tie(grad_out, far_grads, output_back)
    output = rows_at(output_back, inverse)
    far_grads, mid_line = tie(far_grads, mid_line)
    ffn_shard = wide_scatter(ffn_line, PLANE_GROUPS) if quick else ffn_line
    mid_shard = wide_scatter(mid_line, PLANE_GROUPS) if quick else mid_line
    ffn_shard, mid_shard = ffn_shard.astype(F32), mid_shard.astype(F32)
    qkv_grads = weight_grads(
        low_meta,
        [inputs],
        [dq[0], (pair_near, 0), (pair_near, 1)],
        (0, 0, 0),
        factors,
        relative,
        far_grads,
    )
    sums, sums3, sums_near, sums_far, usum0, usum1, memory_bias, grad_out = tie(
        sums, sums3, sums_near, sums_far, usum0, usum1, memory_bias, grad_out
    )
    grad_back = go_home(grad_out)
    sums_qkv = [sums_near, sums_far]

    def global_order(pair):
        own_first = jnp.concatenate(pair, -1)
        other_first = jnp.concatenate(pair[::-1], -1)
        return jnp.where(tensor_index == 0, own_first, other_first)

    in_rows = global_order(
        [
            jnp.stack(
                [
                    sums_qkv[h][0],
                    sums_qkv[h][1],
                    score_scale * sums[6, h * half : (h + 1) * half],
                    memory_bias[0, h * half : (h + 1) * half],
                ]
            )
            for h in both
        ]
    )
    hidden_row = global_order([usum0[0], usum1[0]])
    out_rows = jnp.stack([sums[5], sums[2], sums3[2]])
    gain_rows = jnp.stack([sums[3], sums[0], sums3[0]])
    shift_rows = jnp.stack([sums[4], sums[1], sums3[1]])
    small = jnp.concatenate(
        [
            in_rows.reshape(-1),
            hidden_row,
            out_rows.reshape(-1),
            gain_rows.reshape(-1),
            shift_rows.reshape(-1),
        ]
    )
    if quick:
        small = small + swap(small)
        small, qkv_grads = tie(small, qkv_grads)
        qkv_line = scatter_low(qkv_grads)
        small = sum_low(small)
        qkv_line, grad_back, mid_shard, ffn_shard, small = tie(
            qkv_line, grad_back, mid_shard, ffn_shard, small
        )
        qkv_shard = scatter_plane(qkv_line)
        small = sum_planes(small)
    else:
        qkv_shard = wide_scatter(qkv_grads).astype(F32)
        small = lax.psum(small, ("dp", "tensor"))
    grad_tokens = rows_at(grad_back, inverse)
    in_end = 8 * half
    hidden_end = in_end + 2 * units
    in_total = small[:in_end].reshape(4, 2 * half)
    hidden_total = small[in_end:hidden_end]
    rest = small[hidden_end:].reshape(3, 3, width)
    return (
        output,
        grad_tokens,
        grad_encoder,
        qkv_shard.reshape(shard, 3, half),
        mid_shard[:, :half].T,
        mid_shard[:, half : 2 * half],
        mid_shard[:, 3 * half :].reshape(shard, 2, half),
        mid_shard[:, 2 * half : 3 * half].T,
        ffn_shard[:, :units],
        ffn_shard[:, units:].T,
        lax.dynamic_slice_in_dim(in_total, tensor_index * half, half, 1),
        rest[0],
        lax.dynamic_slice_in_dim(hidden_total, tensor_index * units, units, 0),
        rest[1],
        rest[2],
    )


def solution(mesh):
    in_specs = (
        P(None, ("dp", "tensor"), None),
        P("dp", "tensor", None),
        P(),
        P(),
        P("dp", None, "tensor"),
        P("tensor", "dp"),
        P("dp", "tensor"),
        P("dp", None, "tensor"),
        P("tensor", "dp"),
        P("dp", "tensor"),
        P("tensor", "dp"),
        P(None, "tensor"),
        P(),
        P("tensor"),
        P(),
        P(),
        P(None, ("dp", "tensor"), None),
    )
    out_specs = (
        P(None, ("dp", "tensor"), None),
        P(None, ("dp", "tensor"), None),
        P("dp", "tensor", None),
        P("dp", None, "tensor"),
        P("tensor", "dp"),
        P("dp", "tensor"),
        P("dp", None, "tensor"),
        P("tensor", "dp"),
        P("dp", "tensor"),
        P("tensor", "dp"),
        P(None, "tensor"),
        P(),
        P("tensor"),
        P(),
        P(),
    )
    return jax.shard_map(body, mesh=mesh, in_specs=in_specs, out_specs=out_specs, check_vma=False)
```

```python
import functools
import math

import jax
import jax.numpy as jnp
from jax import lax
from jax.experimental import pallas as pl
from jax.experimental.pallas import tpu as pltpu
from jax.sharding import PartitionSpec as P

HD = 64
EPSILON = 1e-05
MASKED = -1e30
BLOCK = 128
LOW_GROUPS = [[4 * plane + low for low in range(4)] for plane in range(4)]
PLANE_GROUPS = [[low + 4 * plane for plane in range(4)] for low in range(4)]
GROUP = 4
PLAIN = 0
RELATIVE = 1
FIXED = 2
PAIR = 2 * HD
F32 = jnp.float32
BF16 = jnp.bfloat16


def dot_nn(left, right):
    return lax.dot_general(left, right, (((1,), (0,)), ((), ())), preferred_element_type=F32)


def dot_nt(left, right):
    return lax.dot_general(left, right, (((1,), (1,)), ((), ())), preferred_element_type=F32)


def dot_tn(left, right):
    return lax.dot_general(left, right, (((0,), (0,)), ((), ())), preferred_element_type=F32)


def lane_low(shape):
    return lax.broadcasted_iota(jnp.int32, shape, 1) < HD


def stack_heads(rows):
    low = lane_low(rows.shape)
    zero = jnp.zeros_like(rows)
    return jnp.concatenate([jnp.where(low, rows, zero), jnp.where(low, zero, rows)], 0)


def unstack_heads(transposed):
    both = transposed.T
    low = lane_low((BLOCK, PAIR))
    return jnp.where(low, both[:BLOCK], both[BLOCK:])


def block_place(meta):
    block = pl.program_id(0)
    first_blocks = meta[0]
    second = block >= first_blocks
    start = jnp.where(second, first_blocks, 0)
    return block, block - start, start, second.astype(jnp.int32), block < meta[1]


def diagonal_mask(own, piece, tensor_index):
    key = lax.broadcasted_iota(jnp.int32, (BLOCK, 2 * BLOCK), 0)
    query = lax.broadcasted_iota(jnp.int32, (BLOCK, 2 * BLOCK), 1) & (BLOCK - 1)
    if own:
        return key <= query
    shift = piece.bit_length() - 1
    return (key >> shift) < (query >> shift) + tensor_index


def mask_scores(scores, mask):
    keys = scores.shape[0]
    last = jnp.where(mask, scores[keys - BLOCK :], MASKED)
    if keys == BLOCK:
        return last
    return jnp.concatenate([scores[: keys - BLOCK], last], 0)


def pair_columns(pair):
    return slice(pair * PAIR, (pair + 1) * PAIR)


def run_spans(spans, local, start, active, run):
    base = pl.multiple_of(start * BLOCK, BLOCK)
    for step in range(spans):
        pl.when(active & (local == step))(functools.partial(run, base, (step + 1) * BLOCK))


def forward_kernel(piece, spans, meta, q_ref, *refs):
    pairs_in = refs[:2]
    out_ref, lse_ref = refs[2:4]
    flipped = refs[4:6]
    block, local, start, _, active = block_place(meta)
    half = q_ref.shape[1]

    @pl.when(block == 0)
    def _():
        for part in range(2):
            flipped[part][...] = pairs_in[part][:, half:].astype(F32).T.astype(BF16)

    def run(base, span):
        place = pl.ds(base, span)
        masks = [diagonal_mask(part == 0, piece, meta[2]) for part in range(2)]
        for pair in range(half // PAIR):
            cols = pair_columns(pair)
            stacked = stack_heads(q_ref[:, cols])
            scores = [
                mask_scores(dot_nt(pairs_in[part][place, cols], stacked), masks[part])
                for part in range(2)
            ]
            top = jnp.maximum(
                jnp.max(scores[0], 0, keepdims=True), jnp.max(scores[1], 0, keepdims=True)
            )
            exps = [jnp.exp(tile - top) for tile in scores]
            total = jnp.sum(exps[0], 0, keepdims=True) + jnp.sum(exps[1], 0, keepdims=True)
            result = dot_nn(flipped[0][cols, place], exps[0].astype(BF16)) + dot_nn(
                flipped[1][cols, place], exps[1].astype(BF16)
            )
            out_ref[:, cols] = unstack_heads(result / total).astype(BF16)
            lse_ref[0, pair : pair + 1, :] = top + jnp.log(total)

    run_spans(spans, local, start, active, run)

    @pl.when(jnp.logical_not(active))
    def _():
        out_ref[...] = jnp.zeros_like(out_ref)
        lse_ref[...] = jnp.zeros_like(lse_ref)


def backward_kernel(piece, spans, meta, q_ref, g_ref, lse_ref, *refs):
    pairs_in = refs[:2]
    dq_ref = refs[2]
    outs = refs[3:5]
    sums = refs[5:7]
    block, local, start, _, active = block_place(meta)
    half = q_ref.shape[1]

    @pl.when(block == 0)
    def _():
        for part in range(2):
            sums[part][...] = jnp.zeros_like(sums[part])

    def run(base, span):
        place = pl.ds(base, span)
        masks = [diagonal_mask(part == 0, piece, meta[2]) for part in range(2)]
        for pair in range(half // PAIR):
            cols = pair_columns(pair)
            value_cols = slice(half + pair * PAIR, half + (pair + 1) * PAIR)
            queries = stack_heads(q_ref[:, cols])
            grads = stack_heads(g_ref[:, cols])
            lse = lse_ref[0, pair : pair + 1, :]
            probs = []
            grad_probs = []
            for part in range(2):
                tile = mask_scores(dot_nt(pairs_in[part][place, cols], queries), masks[part])
                probs.append(jnp.exp(tile - lse))
                grad_probs.append(dot_nt(pairs_in[part][place, value_cols], grads))
            row_dot = jnp.sum(probs[0] * grad_probs[0], 0, keepdims=True) + jnp.sum(
                probs[1] * grad_probs[1], 0, keepdims=True
            )
            grad_query = None
            for part in range(2):
                grad_score = (probs[part] * (grad_probs[part] - row_dot)).astype(BF16)
                sums[part][place, value_cols] += dot_nn(probs[part].astype(BF16), grads)
                sums[part][place, cols] += dot_nn(grad_score, queries)
                term = dot_tn(grad_score, pairs_in[part][place, cols])
                grad_query = term if grad_query is None else grad_query + term
            low = lane_low((BLOCK, PAIR))
            dq_ref[:, cols] = jnp.where(low, grad_query[:BLOCK], grad_query[BLOCK:]).astype(BF16)

    run_spans(spans, local, start, active, run)

    @pl.when(jnp.logical_not(active))
    def _():
        dq_ref[...] = jnp.zeros_like(dq_ref)

    @pl.when(block == pl.num_programs(0) - 1)
    def _():
        for part in range(2):
            outs[part][...] = sums[part][...].astype(outs[part].dtype)


def row_spec(width, rows=BLOCK):
    return pl.BlockSpec((rows, width), lambda block, meta: (block, 0))


def whole_spec(rows, width):
    return pl.BlockSpec((rows, width), lambda block, meta: (0, 0))


def lse_spec(group=1):
    return pl.BlockSpec((group, 8, 2 * BLOCK), lambda block, meta: (block, 0, 0))


def kept(shape, kind):
    return jax.ShapeDtypeStruct(shape, kind)


def light_cost():
    return pl.CostEstimate(flops=1000, bytes_accessed=1000, transcendentals=0)


def attend_forward(meta, queries, near, far, piece, spans):
    rows, half = queries.shape
    blocks = rows // BLOCK
    return pl.pallas_call(
        functools.partial(forward_kernel, piece, spans),
        grid_spec=pltpu.PrefetchScalarGridSpec(
            num_scalar_prefetch=1,
            grid=(blocks,),
            in_specs=[row_spec(half)] + [whole_spec(rows, 2 * half)] * 2,
            out_specs=[row_spec(half), lse_spec()],
            scratch_shapes=[pltpu.VMEM((half, rows), BF16)] * 2,
        ),
        out_shape=[kept((rows, half), BF16), kept((blocks, 8, 2 * BLOCK), F32)],
        cost_estimate=light_cost(),
        name="attend_forward",
    )(meta, queries, near, far)


def attend_backward(meta, queries, grads, lse, near, far, piece, spans):
    rows, half = queries.shape
    return pl.pallas_call(
        functools.partial(backward_kernel, piece, spans),
        grid_spec=pltpu.PrefetchScalarGridSpec(
            num_scalar_prefetch=1,
            grid=(rows // BLOCK,),
            in_specs=[row_spec(half), row_spec(half), lse_spec()]
            + [whole_spec(rows, 2 * half)] * 2,
            out_specs=[row_spec(half)] + [whole_spec(rows, 2 * half)] * 2,
            scratch_shapes=[pltpu.VMEM((rows, 2 * half), F32)] * 2,
        ),
        out_shape=[
            kept((rows, half), BF16),
            kept((rows, 2 * half), F32),
            kept((rows, 2 * half), BF16),
        ],
        cost_estimate=light_cost(),
        name="attend_backward",
    )(meta, queries, grads, lse, near, far)


def project_kernel(score_scale, x_ref, wq, wk, wv, bias, q_ref, pair_ref):
    rows = x_ref[...]
    half = q_ref.shape[1]
    q_ref[...] = ((dot_nn(rows, wq[...]) + bias[0:1, :]) * score_scale).astype(BF16)
    pair_ref[:, :half] = dot_nn(rows, wk[...]).astype(BF16)
    pair_ref[:, half:] = (dot_nn(rows, wv[...]) + bias[1:2, :]).astype(BF16)


def project(inputs, weight, bias, score_scale):
    rows, width = inputs.shape
    half = bias.shape[1]
    return pl.pallas_call(
        functools.partial(project_kernel, score_scale),
        grid=(2,),
        in_specs=[plain_rows(rows // 2, width)]
        + [plain_fixed((width, half), 0, i) for i in range(3)]
        + [plain_fixed((4, half))],
        out_specs=[plain_rows(rows // 2, half), plain_rows(rows // 2, 2 * half)],
        out_shape=[kept((rows, half), BF16), kept((rows, 2 * half), BF16)],
        cost_estimate=light_cost(),
        name="project",
    )(inputs, weight, weight, weight, bias)


def grads_kernel(sides, counts, factors, extra_steps, fills, kind, meta, *refs):
    lefts = refs[: max(sides) + 1]
    rights = refs[len(lefts) : len(lefts) + len(counts)]
    extra_ref = refs[len(lefts) + len(counts)]
    out_ref = refs[-1]
    step = pl.program_id(0)
    begin = 0
    for index, count in enumerate(counts):
        extra = begin < extra_steps

        @pl.when((step >= begin) & (step < begin + count))
        def _(index=index, extra=extra):
            result = dot_tn(lefts[sides[index]][...], rights[index][...])
            if factors[index] != 1.0:
                result = result * factors[index]
            if kind == PLAIN:
                if extra:
                    result = result + extra_ref[...].astype(F32)
                out_ref[...] = result.astype(BF16)
                return
            size = out_ref.shape[2]
            for plane in range(4):
                for low in range(4):
                    row = (plane * 4 + low) * size
                    place = pl.ds(low if kind == FIXED else meta[0] ^ low, 1)
                    part = result[row : row + size]
                    if extra:
                        part = part + extra_ref[place, plane].astype(F32)[0]
                    out_ref[place, plane] = part.astype(BF16)[None]

        begin += count


def weight_grads(meta, lefts, rights, sides, factors, kind, extra=None, room=None, into=None):
    chunk = min(2 * 384, rights[0].shape[1])
    shifts = [right[1] if isinstance(right, tuple) else 0 for right in rights]
    counts = [1 if isinstance(right, tuple) else right.shape[1] // chunk for right in rights]
    rights = [right[0] if isinstance(right, tuple) else right for right in rights]
    width = lefts[0].shape[1]
    steps = sum(counts)
    total = room or steps * chunk
    start = total // chunk - steps if into is not None else 0
    begins = [sum(counts[:i]) for i in range(len(counts))]

    def right_spec(index):
        return pl.BlockSpec(
            (rights[index].shape[0], chunk),
            lambda step, meta: (
                0,
                shifts[index] + jnp.clip(step - begins[index], 0, counts[index] - 1),
            ),
        )

    def tile_spec(place):
        if kind == PLAIN:
            return pl.BlockSpec((width, chunk), lambda step, meta: (0, place(step)))
        return pl.BlockSpec(
            (4, 4, width // 16, chunk), lambda step, meta: (0, 0, 0, place(step))
        )

    extra_steps = extra.shape[-1] // chunk if extra is not None else 0
    operands = [*lefts, *rights]
    specs = [pl.BlockSpec(left.shape, lambda step, meta: (0, 0)) for left in lefts]
    specs += [right_spec(index) for index in range(len(rights))]
    if extra is not None:
        operands.append(extra)
        specs.append(tile_spec(lambda step: jnp.minimum(step, extra_steps - 1)))
    if into is not None:
        operands.append(into)
        specs.append(pl.BlockSpec(memory_space=pl.ANY))
    return pl.pallas_call(
        functools.partial(
            grads_kernel, sides, counts, factors, extra_steps, into is not None, kind
        ),
        grid_spec=pltpu.PrefetchScalarGridSpec(
            num_scalar_prefetch=1,
            grid=(steps,),
            in_specs=specs,
            out_specs=tile_spec(lambda step: start + step),
        ),
        out_shape=jax.ShapeDtypeStruct(
            (width, total) if kind == PLAIN else (4, 4, width // 16, total), BF16
        ),
        input_output_aliases={len(operands): 0} if into is not None else {},
        cost_estimate=light_cost(),
        name="weight_grads",
    )(meta, *operands)


def norm_forward(hidden, gain, shift):
    center = hidden - jnp.mean(hidden, -1, keepdims=True)
    spread = jnp.mean(center * center, -1, keepdims=True)
    scale = lax.rsqrt(spread + EPSILON)
    unit = center * scale
    return unit * gain + shift, unit, scale


def norm_gradient(grad, unit, scale, gain):
    inner = grad * gain
    mean_inner = jnp.mean(inner, -1, keepdims=True)
    mean_unit = jnp.mean(inner * unit, -1, keepdims=True)
    return scale * (inner - mean_inner - unit * mean_unit)


def sub_blocks(meta, keys_each, run, skip):
    def one(sub, carry):
        block = pl.program_id(0) * GROUP + sub
        second = (block >= meta[0]).astype(jnp.int32)
        place = pl.ds(pl.multiple_of(second * keys_each, keys_each), keys_each)
        rows = pl.ds(pl.multiple_of(sub * BLOCK, BLOCK), BLOCK)
        pl.when(block < meta[1])(functools.partial(run, sub, rows, place))
        pl.when(block >= meta[1])(functools.partial(skip, sub, rows))
        return carry

    lax.fori_loop(0, GROUP, one, 0)


def mid_forward_kernel(score_scale, meta, x_ref, attn0, attn1, memory_ref, *refs):
    attn = (attn0, attn1)
    self_out, query_w, memory_k, memory_v, cross_out = [refs[2 * i : 2 * i + 2] for i in range(5)]
    bias0, bias1, out_bias, gain, shift = refs[10:15]
    unit1_ref, scale1_ref, unit2_ref, scale2_ref, cross_in_ref, hidden_ref, lse_ref = refs[15:22]
    cq_refs, cattn_refs, ck_refs, cv_refs = [refs[22 + 2 * i : 24 + 2 * i] for i in range(4)]
    flipped = refs[30:32]
    half = attn0.shape[1]
    keys_each = memory_ref.shape[0] // 2

    @pl.when(pl.program_id(0) == 0)
    def _():
        for h, bias in enumerate((bias0, bias1)):
            ck_refs[h][...] = dot_nn(memory_ref[...], memory_k[h][...]).astype(BF16)
            value = dot_nn(memory_ref[...], memory_v[h][...]) + bias[3:4, :]
            cv_refs[h][...] = value.astype(BF16)
            flipped[h][...] = value.T.astype(BF16)

    branch = dot_nt(attn[0][...], self_out[0][...]) + dot_nt(attn[1][...], self_out[1][...])
    n1, unit1, scale1 = norm_forward(
        x_ref[...].astype(F32) + branch + out_bias[0:1, :], gain[0:1, :], shift[0:1, :]
    )
    unit1_ref[...] = unit1
    scale1_ref[...] = scale1
    cross_in = n1.astype(BF16)
    cross_in_ref[...] = cross_in
    for h, bias in enumerate((bias0, bias1)):
        query = (dot_nn(cross_in, query_w[h][...]) + bias[2:3, :]) * score_scale
        cq_refs[h][...] = query.astype(BF16)

    def run(sub, rows, place):
        for h in range(2):
            for pair in range(half // PAIR):
                cols = pair_columns(pair)
                tile = dot_nt(ck_refs[h][place, cols], stack_heads(cq_refs[h][rows, cols]))
                top = jnp.max(tile, 0, keepdims=True)
                exps = jnp.exp(tile - top)
                total = jnp.sum(exps, 0, keepdims=True)
                result = dot_nn(flipped[h][cols, place], exps.astype(BF16))
                cattn_refs[h][rows, cols] = unstack_heads(result / total).astype(BF16)
                row = h * (half // PAIR) + pair
                lse_ref[sub, row : row + 1, :] = top + jnp.log(total)

    def skip(sub, rows):
        lse_ref[sub] = jnp.zeros(lse_ref.shape[1:], F32)
        for h in range(2):
            cattn_refs[h][rows, :] = jnp.zeros((BLOCK, half), BF16)

    sub_blocks(meta, keys_each, run, skip)
    branch = dot_nt(cattn_refs[0][...], cross_out[0][...]) + dot_nt(
        cattn_refs[1][...], cross_out[1][...]
    )
    n1 = unit1_ref[...] * gain[0:1, :] + shift[0:1, :]
    n2, unit2, scale2 = norm_forward(n1 + branch + out_bias[1:2, :], gain[1:2, :], shift[1:2, :])
    unit2_ref[...] = unit2
    scale2_ref[...] = scale2
    hidden_ref[...] = n2.astype(BF16)


def mid_backward_kernel(score_scale, total_rows, meta, dn2_ref, unit2_ref, scale2_ref, unit1_ref, scale1_ref, lse_ref, *refs):
    cq_refs, ck_refs, cv_refs = [refs[2 * i : 2 * i + 2] for i in range(3)]
    self_out, query_w, cross_out = [refs[6 + 2 * i : 8 + 2 * i] for i in range(3)]
    gain = refs[12]
    dy2_ref, dh1_ref, dy_ref, sums_ref = refs[13:17]
    dcq_refs, da_refs = refs[17:19], refs[19:21]
    near_ref, far_ref = refs[21:23]
    dca_refs, flipped, dck_refs, dcv_refs = [refs[23 + 2 * i : 25 + 2 * i] for i in range(4)]
    half = cq_refs[0].shape[1]
    keys_each = ck_refs[0].shape[0] // 2
    here = pl.program_id(0) * GROUP * BLOCK + lax.broadcasted_iota(
        jnp.int32, (GROUP * BLOCK, 1), 0
    )
    inside = here < total_rows

    def load(ref):
        return jnp.where(inside, ref[...], 0.0)

    @pl.when(pl.program_id(0) == 0)
    def _():
        sums_ref[...] = jnp.zeros_like(sums_ref)
        for h in range(2):
            flipped[h][...] = ck_refs[h][...].astype(F32).T.astype(BF16)
            dck_refs[h][...] = jnp.zeros_like(dck_refs[h])
            dcv_refs[h][...] = jnp.zeros_like(dcv_refs[h])

    dn2 = load(dn2_ref)
    unit2 = load(unit2_ref)
    dh2 = norm_gradient(dn2, unit2, load(scale2_ref), gain[1:2, :])
    dh1_ref[...] = dh2
    dy2 = dh2.astype(BF16)
    dy2_ref[...] = dy2
    sums_ref[0:1, :] += jnp.sum(dn2 * unit2, 0, keepdims=True)
    sums_ref[1:2, :] += jnp.sum(dn2, 0, keepdims=True)
    sums_ref[2:3, :] += jnp.sum(dy2.astype(F32), 0, keepdims=True)
    for h in range(2):
        dca_refs[h][...] = dot_nn(dy2, cross_out[h][...]).astype(BF16)

    def run(sub, rows, place):
        for h in range(2):
            for pair in range(half // PAIR):
                cols = pair_columns(pair)
                row = h * (half // PAIR) + pair
                queries = stack_heads(cq_refs[h][rows, cols])
                grads = stack_heads(dca_refs[h][rows, cols])
                tile = dot_nt(ck_refs[h][place, cols], queries)
                probs = jnp.exp(tile - lse_ref[sub, row : row + 1, :])
                grad_probs = dot_nt(cv_refs[h][place, cols], grads)
                row_dot = jnp.sum(probs * grad_probs, 0, keepdims=True)
                grad_score = (probs * (grad_probs - row_dot)).astype(BF16)
                dcv_refs[h][place, cols] += dot_nn(probs.astype(BF16), grads)
                dck_refs[h][place, cols] += dot_nn(grad_score, queries)
                term = dot_nn(flipped[h][cols, place], grad_score)
                dcq_refs[h][rows, cols] = unstack_heads(term).astype(BF16)

    def skip(sub, rows):
        for h in range(2):
            dcq_refs[h][rows, :] = jnp.zeros((BLOCK, half), BF16)

    sub_blocks(meta, keys_each, run, skip)
    dn1 = dh1_ref[...]
    for h in range(2):
        dcq = dcq_refs[h][...]
        dn1 = dn1 + score_scale * dot_nt(dcq, query_w[h][...])
        sums_ref[6:7, h * half : (h + 1) * half] += jnp.sum(dcq.astype(F32), 0, keepdims=True)
    unit1 = load(unit1_ref)
    dh1 = norm_gradient(dn1, unit1, load(scale1_ref), gain[0:1, :])
    dy = dh1.astype(BF16)
    dh1_ref[...] = dh1
    dy_ref[...] = dy
    sums_ref[3:4, :] += jnp.sum(dn1 * unit1, 0, keepdims=True)
    sums_ref[4:5, :] += jnp.sum(dn1, 0, keepdims=True)
    sums_ref[5:6, :] += jnp.sum(dy.astype(F32), 0, keepdims=True)
    for h in range(2):
        da_refs[h][...] = dot_nn(dy, self_out[h][...]).astype(BF16)

    @pl.when(pl.program_id(0) == pl.num_programs(0) - 1)
    def _():
        own = keys_each // 2
        for index, ref in enumerate((dck_refs[0], dck_refs[1], dcv_refs[0], dcv_refs[1])):
            near_ref[:, index * half : (index + 1) * half] = ref[...]
            far = slice((index ^ 1) * half, ((index ^ 1) + 1) * half)
            for seq in range(2):
                base = seq * keys_each
                middle, end = base + own, base + keys_each
                far_ref[middle:end, far] = ref[base:middle, :].astype(BF16)
                far_ref[base:middle, far] = ref[middle:end, :].astype(BF16)


def memory_backward_kernel(near_ref, got_ref, wk0, wv0, wk1, wv1, sum_ref, encoder_ref, bias_ref):
    total = (near_ref[...] + got_ref[...].astype(F32)).astype(BF16)
    half = wk0.shape[1]
    sum_ref[:, :half] = total[:, :half]
    sum_ref[:, half:] = total[:, 2 * half : 3 * half]
    own = total.shape[0] // 4
    mine = jnp.concatenate([total[:own], total[2 * own : 3 * own]], 0)
    grad = dot_nt(mine[:, :half], wk0[...]) + dot_nt(mine[:, half : 2 * half], wk1[...])
    grad = grad + dot_nt(mine[:, 2 * half : 3 * half], wv0[...])
    encoder_ref[...] = (grad + dot_nt(mine[:, 3 * half :], wv1[...])).astype(BF16)
    bias = jnp.sum(mine[:, 2 * half :].astype(F32), 0, keepdims=True)
    bias_ref[...] = jnp.broadcast_to(bias, bias_ref.shape)


def memory_backward(near, got, mid):
    rows, span = near.shape
    half = span // 4
    width = mid[0][0].shape[0]
    columns = [plain_fixed((width, half), 0, m[1] + c) for m in mid for c in (3, 4)]
    return pl.pallas_call(
        memory_backward_kernel,
        grid=(1,),
        in_specs=[plain_fixed((rows, span))] * 2 + columns,
        out_specs=[
            plain_fixed((rows, 2 * half)),
            plain_fixed((rows // 2, width)),
            plain_fixed((8, 2 * half)),
        ],
        out_shape=[
            kept((rows, 2 * half), BF16),
            kept((rows // 2, width), BF16),
            kept((8, 2 * half), F32),
        ],
        cost_estimate=light_cost(),
        name="memory_backward",
    )(near, got, *[m[0] for m in mid for _ in range(2)])


def ffn_forward_kernel(first, hidden_ref, base_ref, expand, reduce, bias, gain, shift, act_ref, slope_ref, total_ref):
    pre = dot_nn(hidden_ref[...], expand[...]) + bias[0:1, :]
    phi = 0.5 * (1.0 + lax.erf(pre * (1.0 / math.sqrt(2.0))))
    density = jnp.exp(-0.5 * pre * pre) * (1.0 / math.sqrt(2.0 * math.pi))
    act = (pre * phi).astype(BF16)
    act_ref[...] = act
    slope_ref[...] = (phi + pre * density).astype(BF16)
    base = base_ref[...]
    if first:
        base = base * gain[0:1, :] + shift[0:1, :]
    total_ref[...] = base + dot_nt(act, reduce[...])


def ffn_forward(first, hidden, base, weight, bias, gain, shift):
    rows, width = hidden.shape
    units = bias.shape[1]
    tall = rows // 2
    wide, long = plain_rows(tall, width), plain_rows(tall, units)

    def side(column):
        return pl.BlockSpec(
            (width, units), lambda step: (0, column), pipeline_mode=pl.Buffered(1)
        )

    return pl.pallas_call(
        functools.partial(ffn_forward_kernel, first),
        grid=(2,),
        in_specs=[wide, wide, side(0), side(1), plain_fixed((1, units))]
        + [plain_fixed((1, width))] * 2,
        out_specs=[long, long, wide],
        out_shape=[
            kept((rows, units), BF16),
            kept((rows, units), BF16),
            kept((rows, width), F32),
        ],
        cost_estimate=light_cost(),
        name="ffn_forward",
    )(hidden, base, weight, weight, bias, gain, shift)


def ffn_backward_kernel(h3_ref, cot_ref, valid_ref, slope0, slope1, in0, in1, out0, out1, gain, shift, n3_ref, dz_ref, dn2_ref, sums_ref, du0, du1, usum0, usum1):
    @pl.when(pl.program_id(0) == 0)
    def _():
        for ref in (sums_ref, usum0, usum1):
            ref[...] = jnp.zeros_like(ref)

    n3, unit, scale = norm_forward(h3_ref[...], gain[2:3, :], shift[2:3, :])
    valid = valid_ref[...] > 0.5
    n3_ref[...] = jnp.where(valid, n3, 0.0).astype(BF16)
    dn3 = jnp.where(valid, cot_ref[...].astype(F32), 0.0)
    dh3 = norm_gradient(dn3, unit, scale, gain[2:3, :])
    dz = dh3.astype(BF16)
    dz_ref[...] = dz
    sums_ref[0:1, :] += jnp.sum(dn3 * unit, 0, keepdims=True)
    sums_ref[1:2, :] += jnp.sum(dn3, 0, keepdims=True)
    sums_ref[2:3, :] += jnp.sum(dz.astype(F32), 0, keepdims=True)
    total = dh3
    sides = ((slope0, out0, in0, du0, usum0), (slope1, out1, in1, du1, usum1))
    for slope, reduce, expand, du_ref, usum in sides:
        du = (dot_nn(dz, reduce[...]) * slope[...].astype(F32)).astype(BF16)
        du_ref[...] = du
        usum[0:1, :] += jnp.sum(du.astype(F32), 0, keepdims=True)
        total = total + dot_nt(du, expand[...])
    dn2_ref[...] = total


def ffn_backward(h3, cot, valid, slope, ffn, gain, shift):
    rows, width = h3.shape
    units = slope[0].shape[1]
    wide, thin, long = [plain_rows(rows // 2, w) for w in (width, 1, units)]

    def side(column):
        return pl.BlockSpec(
            (width, units), lambda step: (0, column), pipeline_mode=pl.Buffered(1)
        )

    return pl.pallas_call(
        ffn_backward_kernel,
        grid=(2,),
        in_specs=[wide, wide, thin, long, long, side(0), side(0), side(1), side(1)]
        + [plain_fixed((3, width))] * 2,
        out_specs=[wide, wide, wide, plain_fixed((8, width)), long, long]
        + [plain_fixed((8, units))] * 2,
        out_shape=[
            kept((rows, width), BF16),
            kept((rows, width), BF16),
            kept((rows, width), F32),
            kept((8, width), F32),
            kept((rows, units), BF16),
            kept((rows, units), BF16),
            kept((8, units), F32),
            kept((8, units), F32),
        ],
        cost_estimate=pl.CostEstimate(flops=1000, bytes_accessed=1000, transcendentals=0),
        name="ffn_backward",
    )(h3, cot, valid, *slope, ffn[0], ffn[1], ffn[0], ffn[1], gain, shift)


def fixed_spec(shape, *index):
    place = index or (0,) * len(shape)
    return pl.BlockSpec(shape, lambda block, meta: place)


def mid_forward(meta, inputs, attn, memory, mid, in_pair, out_bias, gain, shift, score_scale):
    rows, width = inputs.shape
    half = attn[0].shape[1]
    blocks = rows // BLOCK
    memory_rows = memory.shape[0]
    weights = [fixed_spec((width, half), 0, m[1] + c) for c in (0, 1, 3, 4, 2) for m in mid]
    tall = GROUP * BLOCK
    wide, thin, narrow = row_spec(width, tall), row_spec(1, tall), row_spec(half, tall)
    memory_spec = fixed_spec((memory_rows, half))
    outs = pl.pallas_call(
        functools.partial(mid_forward_kernel, score_scale),
        grid_spec=pltpu.PrefetchScalarGridSpec(
            num_scalar_prefetch=1,
            grid=(pl.cdiv(blocks, GROUP),),
            in_specs=[wide, narrow, narrow, fixed_spec(memory.shape)]
            + weights
            + [fixed_spec((4, half))] * 2
            + [fixed_spec((3, width))] * 3,
            out_specs=[wide, thin, wide, thin, wide, wide, lse_spec(GROUP)]
            + [narrow] * 4
            + [memory_spec] * 4,
            scratch_shapes=[pltpu.VMEM((half, memory_rows), BF16)] * 2,
        ),
        out_shape=[
            kept((rows, width), F32),
            kept((rows, 1), F32),
            kept((rows, width), F32),
            kept((rows, 1), F32),
            kept((rows, width), BF16),
            kept((rows, width), BF16),
            kept((blocks, 8, 2 * BLOCK), F32),
        ]
        + [kept((rows, half), BF16)] * 4
        + [kept((memory_rows, half), BF16)] * 4,
        cost_estimate=light_cost(),
        name="mid_forward",
    )(meta, inputs, *attn, memory, *[m[0] for _ in range(5) for m in mid], *in_pair, out_bias, gain, shift)
    return outs[:7], outs[7:9], outs[9:11], outs[11:13], outs[13:15]


def mid_backward(meta, dn2, saved, cq, ck, cv, mid, gain, score_scale):
    unit1, scale1, unit2, scale2, lse = saved
    rows, width = dn2.shape
    half = cq[0].shape[1]
    blocks = rows // BLOCK
    memory_rows = ck[0].shape[0]
    tall = GROUP * BLOCK
    wide, thin, narrow = row_spec(width, tall), row_spec(1, tall), row_spec(half, tall)
    memory_spec = fixed_spec((memory_rows, half))
    weights = [fixed_spec((width, half), 0, m[1] + c) for c in (0, 1, 2) for m in mid]
    outs = pl.pallas_call(
        functools.partial(mid_backward_kernel, score_scale, rows),
        grid_spec=pltpu.PrefetchScalarGridSpec(
            num_scalar_prefetch=1,
            grid=(pl.cdiv(blocks, GROUP),),
            in_specs=[wide, wide, thin, wide, thin, lse_spec(GROUP)]
            + [narrow] * 2
            + [memory_spec] * 4
            + weights
            + [fixed_spec((3, width))],
            out_specs=[wide, wide, wide, fixed_spec((8, width))]
            + [narrow] * 4
            + [fixed_spec((memory_rows, 4 * half))] * 2,
            scratch_shapes=[pltpu.VMEM((tall, half), BF16)] * 2
            + [pltpu.VMEM((half, memory_rows), BF16)] * 2
            + [pltpu.VMEM((memory_rows, half), F32)] * 4,
        ),
        out_shape=[
            kept((rows, width), BF16),
            kept((rows, width), F32),
            kept((rows, width), BF16),
            kept((8, width), F32),
        ]
        + [kept((rows, half), BF16)] * 4
        + [kept((memory_rows, 4 * half), F32), kept((memory_rows, 4 * half), BF16)],
        cost_estimate=light_cost(),
        name="mid_backward",
    )(meta, dn2, unit2, scale2, unit1, scale1, lse, *cq, *ck, *cv, *[m[0] for _ in range(3) for m in mid], gain)
    return outs[:4], outs[4:6], outs[6:8], outs[8], outs[9]


def input_backward_kernel(score_scale, base_ref, dq_ref, own_ref, got_ref, wq, wk, wv, dx_ref, pair_ref, sums_ref):
    @pl.when(pl.program_id(0) == 0)
    def _():
        sums_ref[...] = jnp.zeros_like(sums_ref)

    half = dq_ref.shape[1]
    pair = (own_ref[...] + got_ref[...].astype(F32)).astype(BF16)
    pair_ref[...] = pair
    dq = dq_ref[...]
    dk, dv = pair[:, :half], pair[:, half:]
    sums_ref[0:1, :] += score_scale * jnp.sum(dq.astype(F32), 0, keepdims=True)
    sums_ref[1:2, :] += jnp.sum(dv.astype(F32), 0, keepdims=True)
    total = score_scale * dot_nt(dq, wq[...]) + dot_nt(dk, wk[...]) + dot_nt(dv, wv[...])
    dx_ref[...] = (base_ref[...] + total).astype(dx_ref.dtype)


def plain_rows(rows, width):
    return pl.BlockSpec((rows, width), lambda step: (step, 0))


def plain_fixed(shape, *index):
    place = index or (0,) * len(shape)
    return pl.BlockSpec(shape, lambda step: place)


def input_backward(base, dq, own, got, weight, score_scale, kind):
    rows, width = base.shape
    half = dq.shape[1]
    tall = rows // 2
    return pl.pallas_call(
        functools.partial(input_backward_kernel, score_scale),
        grid=(2,),
        in_specs=[plain_rows(tall, width), plain_rows(tall, half)]
        + [plain_rows(tall, 2 * half)] * 2
        + [plain_fixed((width, half), 0, i) for i in range(3)],
        out_specs=[plain_rows(tall, width), plain_rows(tall, 2 * half), plain_fixed((8, half))],
        out_shape=[
            kept((rows, width), kind),
            kept((rows, 2 * half), BF16),
            kept((8, half), F32),
        ],
        cost_estimate=light_cost(),
        name="input_backward",
    )(base, dq, own, got, weight, weight, weight)


def swap(value):
    return lax.ppermute(value, "tensor", [(0, 1), (1, 0)])


def hop(value, bits):
    return lax.ppermute(value, "dp", [(i, i ^ bits) for i in range(16)])


def pack_kernel(*refs):
    start = 0
    for ref in refs[:-1]:
        refs[-1][:, start : start + ref.shape[1]] = ref[...]
        start += ref.shape[1]


def pack_shards(*parts):
    shard = parts[0].shape[0]
    total = sum(part.shape[1] for part in parts)
    return pl.pallas_call(
        pack_kernel,
        grid=(1,),
        in_specs=[plain_fixed(part.shape) for part in parts],
        out_specs=plain_fixed((shard, total)),
        out_shape=kept((shard, total), BF16),
        cost_estimate=light_cost(),
        name="pack_shards",
    )(*parts)


def assemble_kernel(meta, own_ref, first_ref, second_ref, third_ref, out_ref):
    for low, ref in enumerate((own_ref, first_ref, second_ref, third_ref)):
        out_ref[0, pl.ds(meta[1] ^ low, 1)] = ref[...]


def plane_line(value):
    return jnp.stack([value, hop(value, 4), hop(value, 8), hop(value, 12)])


def low_groups(line):
    return (line, hop(line, 1), hop(line, 2), hop(line, 3))


def assemble(groups):
    rows, count = groups[0].shape[1:]
    index = lax.axis_index("dp")
    meta = jnp.stack([index // 4, index % 4]).astype(jnp.int32)
    spec = pl.BlockSpec((1, rows, count), lambda i, meta: (i ^ meta[0], 0, 0))
    full = pl.pallas_call(
        assemble_kernel,
        grid_spec=pltpu.PrefetchScalarGridSpec(
            num_scalar_prefetch=1,
            grid=(4,),
            in_specs=[spec] * 4,
            out_specs=pl.BlockSpec((1, 4, rows, count), lambda i, meta: (i, 0, 0, 0)),
        ),
        out_shape=kept((4, 4, rows, count), groups[0].dtype),
        cost_estimate=light_cost(),
        name="assemble",
    )(meta, *groups)
    return full.reshape(16 * rows, count)


def total_of(parts):
    return functools.reduce(jnp.add, [part.astype(F32) for part in parts])


def scatter_low(groups):
    received = [hop(groups[low], low) for low in (1, 2, 3)]
    return total_of([groups[0]] + received).astype(BF16)


def scatter_plane(line):
    plane = lax.axis_index("dp") // 4

    def pick(other):
        return lax.dynamic_index_in_dim(line, plane ^ other, 0, keepdims=False)

    received = [hop(pick(other), 4 * other) for other in (1, 2, 3)]
    return total_of([pick(0)] + received)


def wide_scatter(value, groups=None):
    return lax.psum_scatter(
        value, "dp", scatter_dimension=0, tiled=True, axis_index_groups=groups
    )


def sum_low(value):
    return total_of([value] + [hop(value, bits) for bits in (1, 2, 3)])


def sum_planes(value):
    return total_of([value] + [hop(value, 4 * bits) for bits in (1, 2, 3)])


def rows_at(value, ids):
    return value.at[ids].get(mode="promise_in_bounds")


def tie(*values):
    return lax.optimization_barrier(values)


def body(
    tokens,
    encoder,
    lengths,
    deal,
    self_project,
    self_output,
    cross_query,
    cross_memory,
    cross_output,
    hidden_in,
    hidden_out,
    in_bias,
    out_bias,
    hidden_bias,
    norm_gain,
    norm_bias,
    cotangent,
):
    score_scale = 1.0 / math.sqrt(HD)
    dp_count = lax.axis_size("dp")
    dp_index = lax.axis_index("dp")
    tensor_index = lax.axis_index("tensor")
    piece = tokens.shape[1]
    width = tokens.shape[2]
    slots = piece * dp_count
    half = self_project.shape[2]
    units = hidden_in.shape[1]
    shard = self_project.shape[0]
    memory_rows = encoder.shape[1]
    spans = slots // BLOCK
    blocks = (slots + slots // 2) // BLOCK + 1
    rows = blocks * BLOCK
    per_block = BLOCK // piece

    pair_ids = lax.dynamic_slice_in_dim(deal, 2 * dp_index, 2)
    pair_len = rows_at(lengths, pair_ids)
    pieces_used = (pair_len + 2 * piece - 1) // (2 * piece)
    blocks_used = (pieces_used * piece + BLOCK - 1) // BLOCK
    first_blocks = blocks_used[0]
    all_blocks = first_blocks + blocks_used[1]
    meta = jnp.stack([first_blocks, all_blocks, tensor_index]).astype(jnp.int32)

    block_ids = jnp.arange(blocks, dtype=jnp.int32)
    block_seq = (block_ids >= first_blocks).astype(jnp.int32)
    block_local = jnp.minimum(block_ids - block_seq * first_blocks, spans - 1)
    piece_ids = (
        (block_local[:, None] * per_block + jnp.arange(per_block, dtype=jnp.int32)[None, :]) * 2
        + block_seq[:, None]
    ).reshape(-1)
    slot_ids = block_local[:, None] * BLOCK + jnp.arange(BLOCK, dtype=jnp.int32)[None, :]
    positions = ((slot_ids // piece) * 2 + tensor_index) * piece + slot_ids % piece
    row_valid = (
        (positions < jnp.where(block_seq == 1, pair_len[1], pair_len[0])[:, None])
        & (block_ids < all_blocks)[:, None]
    ).reshape(rows, 1)

    send_piece = jnp.arange(dp_count, dtype=jnp.int32)
    spare = jnp.where(
        pieces_used[0] % per_block != 0, first_blocks * per_block - 1, rows // piece - 1
    )
    send_start = jnp.stack([0 * first_blocks, first_blocks * per_block])
    send_ids = jnp.where(
        send_piece[:, None] < pieces_used[None, :],
        send_start[None, :] + send_piece[:, None],
        spare,
    ).reshape(-1)
    inverse = jnp.zeros_like(deal).at[deal].set(jnp.arange(deal.shape[0], dtype=jnp.int32))

    def home_pieces(value):
        return rows_at(value.reshape(rows // piece, piece, width), send_ids)

    def go_home(outgoing):
        return lax.all_to_all(outgoing, "dp", split_axis=0, concat_axis=0, tiled=True)

    def order(value):
        return rows_at(value, deal)

    def arrive(ordered):
        return lax.all_to_all(ordered, "dp", split_axis=0, concat_axis=0, tiled=True)

    def pack(arrived, ids):
        return rows_at(arrived, ids).reshape(rows, width)

    quick = dp_count == 16
    both = (0, 1)
    biases = jnp.concatenate([in_bias.reshape(-1), hidden_bias])
    bias_pair = (biases, swap(biases))
    in_pair = [b[: 4 * half].reshape(4, half) for b in bias_pair]
    hidden_pair = [b[None, 4 * half :] for b in bias_pair]

    memory_full = jnp.concatenate([encoder, swap(encoder)], 1).reshape(4 * memory_rows, width)
    affine = (norm_gain[1:2], norm_bias[1:2] + out_bias[2:3])
    early = (row_valid.astype(F32), affine, in_pair, hidden_pair, meta, piece_ids, memory_full, send_ids, inverse)
    ordered = order(tokens)
    qkv_shard_in = self_project.reshape(shard, 3 * half)
    def slow_gather(value):
        return lax.all_gather(value, "dp", axis=0, tiled=True)

    ordered_cot = order(cotangent)
    if quick:
        qkv_line = plane_line(qkv_shard_in)
        qkv_line, ordered = tie(qkv_line, ordered)
        qkv_groups = low_groups(qkv_line)
        arrived = arrive(ordered)
        ordered_cot, arrived, qkv_groups, early = tie(ordered_cot, arrived, qkv_groups, early)
        qkv_own = assemble(qkv_groups)
    else:
        arrived = arrive(ordered)
        qkv_own = slow_gather(qkv_shard_in)
    qkv_weight = (qkv_own, swap(qkv_own))
    valid_rows, affine, in_pair, hidden_pair, meta, piece_ids, memory_full = early[:7]
    send_ids, inverse = early[7:]
    inputs = pack(arrived, piece_ids)
    arrived_cot = arrive(ordered_cot)

    rest_own = slow_gather(
        pack_shards(
            hidden_in,
            hidden_out.T,
            self_output.T,
            cross_query,
            cross_output.T,
            cross_memory.reshape(shard, 2 * half),
        )
    )


    queries = [None, None]
    near = [None, None]
    attn = [None, None]
    lse = [None, None]
    for h in both:
        queries[h], near[h] = project(inputs, qkv_weight[h], in_pair[h], score_scale)
    far = [swap(near[1 - h]) for h in both]
    attn[1], lse[1] = attend_forward(meta, queries[1], near[1], far[1], piece, spans)
    attn[1], queries[0], far[0] = tie(attn[1], queries[0], far[0])
    attn[0], lse[0] = attend_forward(meta, queries[0], near[0], far[0], piece, spans)
    rest_own, attn[0] = tie(rest_own, attn[0])
    rest_far = swap(rest_own)
    mid_weight = [(rest, 2 * units // half) for rest in (rest_own, rest_far)]
    saved, cqs, cattn, cks, cvs = mid_forward(
        meta, inputs, attn, memory_full, mid_weight, in_pair, out_bias, norm_gain, norm_bias, score_scale
    )
    unit1, scale1, unit2, scale2, cross_in, hidden, clse = saved
    act = [None, None]
    slope = [None, None]
    act[0], slope[0], total = ffn_forward(
        True, hidden, unit2, rest_own, hidden_pair[0], *affine
    )
    act[1], slope[1], total = ffn_forward(
        False, hidden, total, rest_far, hidden_pair[1], *affine
    )
    arrived_cot, total = tie(arrived_cot, total)
    ffn_weight = (rest_own, rest_far)
    n3, dz, dn2, sums3, du0, du1, usum0, usum1 = ffn_backward(
        total, pack(arrived_cot, piece_ids), valid_rows, slope, ffn_weight, norm_gain, norm_bias
    )
    du = (du0, du1)
    output_back = go_home(home_pieces(n3))

    low_meta = jnp.reshape(dp_index % 4, (1,)).astype(jnp.int32)

    fixed = FIXED if quick else PLAIN
    one = (0,)
    far_in = weight_grads(low_meta, [hidden], [du[1]], one, (1.0,), fixed)
    far_out = weight_grads(low_meta, [dz], [act[1]], one, (1.0,), fixed)
    ffn_grads = weight_grads(
        low_meta, [hidden], [du[0]], one, (1.0,), fixed, swap(far_in), 2 * units
    )
    ffn_grads = weight_grads(
        low_meta, [dz], [act[0]], one, (1.0,), fixed, swap(far_out), 2 * units, ffn_grads
    )
    ffn_grads, dn2 = tie(ffn_grads, dn2)
    ffn_line = wide_scatter(ffn_grads.reshape(width, 2 * units), LOW_GROUPS if quick else None)
    rows_back, dcq, da, memory_near, memory_far = mid_backward(
        meta, dn2, (unit1, scale1, unit2, scale2, clse), cqs, cks, cvs, mid_weight, norm_gain, score_scale
    )
    dy2, dh1, dy, sums = rows_back
    da = list(da)
    memory_far, output_back = tie(memory_far, output_back)
    memory_sum, grad_memory, memory_bias = memory_backward(
        memory_near, swap(memory_far), mid_weight
    )
    grad_encoder = grad_memory.reshape(2, memory_rows, width)
    mid_factors = (1.0, score_scale, 1.0, 1.0, 1.0)
    far_mid = weight_grads(
        low_meta,
        [dy, cross_in, dy2],
        [attn[1], dcq[1], cattn[1]],
        (0, 1, 2),
        mid_factors[:3],
        fixed,
    )
    mid_grads = weight_grads(
        low_meta,
        [dy, cross_in, dy2, memory_full],
        [attn[0], dcq[0], cattn[0], (memory_sum, 0), (memory_sum, 1)],
        (0, 1, 2, 3, 3),
        mid_factors,
        fixed,
        swap(far_mid),
    )
    mid_grads, da[0], da[1] = tie(mid_grads, da[0], da[1])
    mid_line = wide_scatter(mid_grads.reshape(width, 5 * half), LOW_GROUPS if quick else None)
    dq = [None, None]
    own = [None, None]
    out = [None, None]
    for h in both:
        dq[h], own[h], out[h] = attend_backward(
            meta, queries[h], da[h], lse[h], near[h], far[h], piece, spans
        )
        if h == 0:
            da[1], dq[0], ffn_line = tie(da[1], dq[0], ffn_line)
    factors = (score_scale, 1.0, 1.0)
    got_far, got_near = swap(out[0]), swap(out[1])
    dx_far, pair_far, sums_far = input_backward(
        dh1, dq[1], own[1], got_far, qkv_weight[1], score_scale, F32
    )
    relative = RELATIVE if quick else PLAIN
    far_grads = weight_grads(
        low_meta, [inputs], [dq[1], (pair_far, 0), (pair_far, 1)], (0, 0, 0), factors, relative
    )
    far_grads, dx_far, got_near, ffn_line = tie(far_grads, dx_far, got_near, ffn_line)
    far_grads = swap(far_grads)
    dx, pair_near, sums_near = input_backward(
        dx_far, dq[0], own[0], got_near, qkv_weight[0], score_scale, BF16
    )
    grad_out = home_pieces(dx)
    grad_out, far_grads, output_back = tie(grad_out, far_grads, output_back)
    output = rows_at(output_back, inverse)
    far_grads, mid_line = tie(far_grads, mid_line)
    ffn_shard = wide_scatter(ffn_line, PLANE_GROUPS) if quick else ffn_line
    mid_shard = wide_scatter(mid_line, PLANE_GROUPS) if quick else mid_line
    ffn_shard, mid_shard = ffn_shard.astype(F32), mid_shard.astype(F32)
    qkv_grads = weight_grads(
        low_meta,
        [inputs],
        [dq[0], (pair_near, 0), (pair_near, 1)],
        (0, 0, 0),
        factors,
        relative,
        far_grads,
    )
    sums, sums3, sums_near, sums_far, usum0, usum1, memory_bias, grad_out = tie(
        sums, sums3, sums_near, sums_far, usum0, usum1, memory_bias, grad_out
    )
    grad_back = go_home(grad_out)
    sums_qkv = [sums_near, sums_far]

    def global_order(pair):
        own_first = jnp.concatenate(pair, -1)
        other_first = jnp.concatenate(pair[::-1], -1)
        return jnp.where(tensor_index == 0, own_first, other_first)

    in_rows = global_order(
        [
            jnp.stack(
                [
                    sums_qkv[h][0],
                    sums_qkv[h][1],
                    score_scale * sums[6, h * half : (h + 1) * half],
                    memory_bias[0, h * half : (h + 1) * half],
                ]
            )
            for h in both
        ]
    )
    hidden_row = global_order([usum0[0], usum1[0]])
    out_rows = jnp.stack([sums[5], sums[2], sums3[2]])
    gain_rows = jnp.stack([sums[3], sums[0], sums3[0]])
    shift_rows = jnp.stack([sums[4], sums[1], sums3[1]])
    small = jnp.concatenate(
        [
            in_rows.reshape(-1),
            hidden_row,
            out_rows.reshape(-1),
            gain_rows.reshape(-1),
            shift_rows.reshape(-1),
        ]
    )
    if quick:
        small = small + swap(small)
        small, qkv_grads = tie(small, qkv_grads)
        qkv_line = scatter_low(qkv_grads)
        small = sum_low(small)
        qkv_line, grad_back, ffn_shard, small = tie(qkv_line, grad_back, ffn_shard, small)
        qkv_shard = scatter_plane(qkv_line)
        small = sum_planes(small)
    else:
        qkv_shard = wide_scatter(qkv_grads).astype(F32)
        small = lax.psum(small, ("dp", "tensor"))
    grad_tokens = rows_at(grad_back, inverse)
    in_end = 8 * half
    hidden_end = in_end + 2 * units
    in_total = small[:in_end].reshape(4, 2 * half)
    hidden_total = small[in_end:hidden_end]
    rest = small[hidden_end:].reshape(3, 3, width)
    return (
        output,
        grad_tokens,
        grad_encoder,
        qkv_shard.reshape(shard, 3, half),
        mid_shard[:, :half].T,
        mid_shard[:, half : 2 * half],
        mid_shard[:, 3 * half :].reshape(shard, 2, half),
        mid_shard[:, 2 * half : 3 * half].T,
        ffn_shard[:, :units],
        ffn_shard[:, units:].T,
        lax.dynamic_slice_in_dim(in_total, tensor_index * half, half, 1),
        rest[0],
        lax.dynamic_slice_in_dim(hidden_total, tensor_index * units, units, 0),
        rest[1],
        rest[2],
    )


def solution(mesh):
    in_specs = (
        P(None, ("dp", "tensor"), None),
        P("dp", "tensor", None),
        P(),
        P(),
        P("dp", None, "tensor"),
        P("tensor", "dp"),
        P("dp", "tensor"),
        P("dp", None, "tensor"),
        P("tensor", "dp"),
        P("dp", "tensor"),
        P("tensor", "dp"),
        P(None, "tensor"),
        P(),
        P("tensor"),
        P(),
        P(),
        P(None, ("dp", "tensor"), None),
    )
    out_specs = (
        P(None, ("dp", "tensor"), None),
        P(None, ("dp", "tensor"), None),
        P("dp", "tensor", None),
        P("dp", None, "tensor"),
        P("tensor", "dp"),
        P("dp", "tensor"),
        P("dp", None, "tensor"),
        P("tensor", "dp"),
        P("dp", "tensor"),
        P("tensor", "dp"),
        P(None, "tensor"),
        P(),
        P("tensor"),
        P(),
        P(),
    )
    return jax.shard_map(body, mesh=mesh, in_specs=in_specs, out_specs=out_specs, check_vma=False)
```

```python
import functools
import math

import jax
import jax.numpy as jnp
from jax import lax
from jax.experimental import pallas as pl
from jax.experimental.pallas import tpu as pltpu
from jax.sharding import PartitionSpec as P

HD = 64
EPSILON = 1e-05
MASKED = -1e30
BLOCK = 128
LOW_GROUPS = [[4 * plane + low for low in range(4)] for plane in range(4)]
PLANE_GROUPS = [[low + 4 * plane for plane in range(4)] for low in range(4)]
GROUP = 4
PLAIN = 0
RELATIVE = 1
FIXED = 2
PAIR = 2 * HD
F32 = jnp.float32
BF16 = jnp.bfloat16


def dot_nn(left, right):
    return lax.dot_general(left, right, (((1,), (0,)), ((), ())), preferred_element_type=F32)


def dot_nt(left, right):
    return lax.dot_general(left, right, (((1,), (1,)), ((), ())), preferred_element_type=F32)


def dot_tn(left, right):
    return lax.dot_general(left, right, (((0,), (0,)), ((), ())), preferred_element_type=F32)


def lane_low(shape):
    return lax.broadcasted_iota(jnp.int32, shape, 1) < HD


def stack_heads(rows):
    low = lane_low(rows.shape)
    zero = jnp.zeros_like(rows)
    return jnp.concatenate([jnp.where(low, rows, zero), jnp.where(low, zero, rows)], 0)


def unstack_heads(transposed):
    both = transposed.T
    low = lane_low((BLOCK, PAIR))
    return jnp.where(low, both[:BLOCK], both[BLOCK:])


def block_place(meta):
    block = pl.program_id(0)
    first_blocks = meta[0]
    second = block >= first_blocks
    start = jnp.where(second, first_blocks, 0)
    return block, block - start, start, second.astype(jnp.int32), block < meta[1]


def diagonal_mask(own, piece, tensor_index):
    key = lax.broadcasted_iota(jnp.int32, (BLOCK, 2 * BLOCK), 0)
    query = lax.broadcasted_iota(jnp.int32, (BLOCK, 2 * BLOCK), 1) & (BLOCK - 1)
    if own:
        return key <= query
    shift = piece.bit_length() - 1
    return (key >> shift) < (query >> shift) + tensor_index


def mask_scores(scores, mask):
    keys = scores.shape[0]
    last = jnp.where(mask, scores[keys - BLOCK :], MASKED)
    if keys == BLOCK:
        return last
    return jnp.concatenate([scores[: keys - BLOCK], last], 0)


def pair_columns(pair):
    return slice(pair * PAIR, (pair + 1) * PAIR)


def run_spans(spans, local, start, active, run):
    base = pl.multiple_of(start * BLOCK, BLOCK)
    for step in range(spans):
        pl.when(active & (local == step))(functools.partial(run, base, (step + 1) * BLOCK))


def forward_kernel(piece, spans, meta, q_ref, *refs):
    pairs_in = refs[:2]
    out_ref, lse_ref = refs[2:4]
    flipped = refs[4:6]
    block, local, start, _, active = block_place(meta)
    half = q_ref.shape[1]

    @pl.when(block == 0)
    def _():
        for part in range(2):
            flipped[part][...] = pairs_in[part][:, half:].astype(F32).T.astype(BF16)

    def run(base, span):
        place = pl.ds(base, span)
        masks = [diagonal_mask(part == 0, piece, meta[2]) for part in range(2)]
        for pair in range(half // PAIR):
            cols = pair_columns(pair)
            stacked = stack_heads(q_ref[:, cols])
            scores = [
                mask_scores(dot_nt(pairs_in[part][place, cols], stacked), masks[part])
                for part in range(2)
            ]
            top = jnp.maximum(
                jnp.max(scores[0], 0, keepdims=True), jnp.max(scores[1], 0, keepdims=True)
            )
            exps = [jnp.exp(tile - top) for tile in scores]
            total = jnp.sum(exps[0], 0, keepdims=True) + jnp.sum(exps[1], 0, keepdims=True)
            result = dot_nn(flipped[0][cols, place], exps[0].astype(BF16)) + dot_nn(
                flipped[1][cols, place], exps[1].astype(BF16)
            )
            out_ref[:, cols] = unstack_heads(result / total).astype(BF16)
            lse_ref[0, pair : pair + 1, :] = top + jnp.log(total)

    run_spans(spans, local, start, active, run)

    @pl.when(jnp.logical_not(active))
    def _():
        out_ref[...] = jnp.zeros_like(out_ref)
        lse_ref[...] = jnp.zeros_like(lse_ref)


def backward_kernel(piece, spans, meta, q_ref, g_ref, lse_ref, *refs):
    pairs_in = refs[:2]
    dq_ref = refs[2]
    outs = refs[3:5]
    sums = refs[5:7]
    block, local, start, _, active = block_place(meta)
    half = q_ref.shape[1]

    @pl.when(block == 0)
    def _():
        for part in range(2):
            sums[part][...] = jnp.zeros_like(sums[part])

    def run(base, span):
        place = pl.ds(base, span)
        masks = [diagonal_mask(part == 0, piece, meta[2]) for part in range(2)]
        for pair in range(half // PAIR):
            cols = pair_columns(pair)
            value_cols = slice(half + pair * PAIR, half + (pair + 1) * PAIR)
            queries = stack_heads(q_ref[:, cols])
            grads = stack_heads(g_ref[:, cols])
            lse = lse_ref[0, pair : pair + 1, :]
            probs = []
            grad_probs = []
            for part in range(2):
                tile = mask_scores(dot_nt(pairs_in[part][place, cols], queries), masks[part])
                probs.append(jnp.exp(tile - lse))
                grad_probs.append(dot_nt(pairs_in[part][place, value_cols], grads))
            row_dot = jnp.sum(probs[0] * grad_probs[0], 0, keepdims=True) + jnp.sum(
                probs[1] * grad_probs[1], 0, keepdims=True
            )
            grad_query = None
            for part in range(2):
                grad_score = (probs[part] * (grad_probs[part] - row_dot)).astype(BF16)
                sums[part][place, value_cols] += dot_nn(probs[part].astype(BF16), grads)
                sums[part][place, cols] += dot_nn(grad_score, queries)
                term = dot_tn(grad_score, pairs_in[part][place, cols])
                grad_query = term if grad_query is None else grad_query + term
            low = lane_low((BLOCK, PAIR))
            dq_ref[:, cols] = jnp.where(low, grad_query[:BLOCK], grad_query[BLOCK:]).astype(BF16)

    run_spans(spans, local, start, active, run)

    @pl.when(jnp.logical_not(active))
    def _():
        dq_ref[...] = jnp.zeros_like(dq_ref)

    @pl.when(block == pl.num_programs(0) - 1)
    def _():
        for part in range(2):
            outs[part][...] = sums[part][...].astype(outs[part].dtype)


def row_spec(width, rows=BLOCK):
    return pl.BlockSpec((rows, width), lambda block, meta: (block, 0))


def whole_spec(rows, width):
    return pl.BlockSpec((rows, width), lambda block, meta: (0, 0))


def lse_spec(group=1):
    return pl.BlockSpec((group, 8, 2 * BLOCK), lambda block, meta: (block, 0, 0))


def kept(shape, kind):
    return jax.ShapeDtypeStruct(shape, kind)


def light_cost():
    return pl.CostEstimate(flops=1000, bytes_accessed=1000, transcendentals=0)


def attend_forward(meta, queries, near, far, piece, spans):
    rows, half = queries.shape
    blocks = rows // BLOCK
    return pl.pallas_call(
        functools.partial(forward_kernel, piece, spans),
        grid_spec=pltpu.PrefetchScalarGridSpec(
            num_scalar_prefetch=1,
            grid=(blocks,),
            in_specs=[row_spec(half)] + [whole_spec(rows, 2 * half)] * 2,
            out_specs=[row_spec(half), lse_spec()],
            scratch_shapes=[pltpu.VMEM((half, rows), BF16)] * 2,
        ),
        out_shape=[kept((rows, half), BF16), kept((blocks, 8, 2 * BLOCK), F32)],
        cost_estimate=light_cost(),
        name="attend_forward",
    )(meta, queries, near, far)


def attend_backward(meta, queries, grads, lse, near, far, piece, spans):
    rows, half = queries.shape
    return pl.pallas_call(
        functools.partial(backward_kernel, piece, spans),
        grid_spec=pltpu.PrefetchScalarGridSpec(
            num_scalar_prefetch=1,
            grid=(rows // BLOCK,),
            in_specs=[row_spec(half), row_spec(half), lse_spec()]
            + [whole_spec(rows, 2 * half)] * 2,
            out_specs=[row_spec(half)] + [whole_spec(rows, 2 * half)] * 2,
            scratch_shapes=[pltpu.VMEM((rows, 2 * half), F32)] * 2,
        ),
        out_shape=[
            kept((rows, half), BF16),
            kept((rows, 2 * half), F32),
            kept((rows, 2 * half), BF16),
        ],
        cost_estimate=light_cost(),
        name="attend_backward",
    )(meta, queries, grads, lse, near, far)


def project_kernel(score_scale, x_ref, wq, wk, wv, bias, q_ref, pair_ref):
    rows = x_ref[...]
    half = q_ref.shape[1]
    q_ref[...] = ((dot_nn(rows, wq[...]) + bias[0:1, :]) * score_scale).astype(BF16)
    pair_ref[:, :half] = dot_nn(rows, wk[...]).astype(BF16)
    pair_ref[:, half:] = (dot_nn(rows, wv[...]) + bias[1:2, :]).astype(BF16)


def project(inputs, weight, bias, score_scale):
    rows, width = inputs.shape
    half = bias.shape[1]
    return pl.pallas_call(
        functools.partial(project_kernel, score_scale),
        grid=(2,),
        in_specs=[plain_rows(rows // 2, width)]
        + [plain_fixed((width, half), 0, i) for i in range(3)]
        + [plain_fixed((4, half))],
        out_specs=[plain_rows(rows // 2, half), plain_rows(rows // 2, 2 * half)],
        out_shape=[kept((rows, half), BF16), kept((rows, 2 * half), BF16)],
        cost_estimate=light_cost(),
        name="project",
    )(inputs, weight, weight, weight, bias)


def grads_kernel(sides, counts, factors, extra_steps, fills, kind, meta, *refs):
    lefts = refs[: max(sides) + 1]
    rights = refs[len(lefts) : len(lefts) + len(counts)]
    extra_ref = refs[len(lefts) + len(counts)]
    out_ref = refs[-1]
    step = pl.program_id(0)
    begin = 0
    for index, count in enumerate(counts):
        extra = begin < extra_steps

        @pl.when((step >= begin) & (step < begin + count))
        def _(index=index, extra=extra):
            result = dot_tn(lefts[sides[index]][...], rights[index][...])
            if factors[index] != 1.0:
                result = result * factors[index]
            if kind == PLAIN:
                if extra:
                    result = result + extra_ref[...].astype(F32)
                out_ref[...] = result.astype(BF16)
                return
            size = out_ref.shape[2]
            for plane in range(4):
                for low in range(4):
                    row = (plane * 4 + low) * size
                    place = pl.ds(low if kind == FIXED else meta[0] ^ low, 1)
                    part = result[row : row + size]
                    if extra:
                        part = part + extra_ref[place, plane].astype(F32)[0]
                    out_ref[place, plane] = part.astype(BF16)[None]

        begin += count


def weight_grads(meta, lefts, rights, sides, factors, kind, extra=None, room=None, into=None):
    chunk = min(2 * 384, rights[0].shape[1])
    shifts = [right[1] if isinstance(right, tuple) else 0 for right in rights]
    counts = [1 if isinstance(right, tuple) else right.shape[1] // chunk for right in rights]
    rights = [right[0] if isinstance(right, tuple) else right for right in rights]
    width = lefts[0].shape[1]
    steps = sum(counts)
    total = room or steps * chunk
    start = total // chunk - steps if into is not None else 0
    begins = [sum(counts[:i]) for i in range(len(counts))]

    def right_spec(index):
        return pl.BlockSpec(
            (rights[index].shape[0], chunk),
            lambda step, meta: (
                0,
                shifts[index] + jnp.clip(step - begins[index], 0, counts[index] - 1),
            ),
        )

    def tile_spec(place):
        if kind == PLAIN:
            return pl.BlockSpec((width, chunk), lambda step, meta: (0, place(step)))
        return pl.BlockSpec(
            (4, 4, width // 16, chunk), lambda step, meta: (0, 0, 0, place(step))
        )

    extra_steps = extra.shape[-1] // chunk if extra is not None else 0
    operands = [*lefts, *rights]
    specs = [pl.BlockSpec(left.shape, lambda step, meta: (0, 0)) for left in lefts]
    specs += [right_spec(index) for index in range(len(rights))]
    if extra is not None:
        operands.append(extra)
        specs.append(tile_spec(lambda step: jnp.minimum(step, extra_steps - 1)))
    if into is not None:
        operands.append(into)
        specs.append(pl.BlockSpec(memory_space=pl.ANY))
    return pl.pallas_call(
        functools.partial(
            grads_kernel, sides, counts, factors, extra_steps, into is not None, kind
        ),
        grid_spec=pltpu.PrefetchScalarGridSpec(
            num_scalar_prefetch=1,
            grid=(steps,),
            in_specs=specs,
            out_specs=tile_spec(lambda step: start + step),
        ),
        out_shape=jax.ShapeDtypeStruct(
            (width, total) if kind == PLAIN else (4, 4, width // 16, total), BF16
        ),
        input_output_aliases={len(operands): 0} if into is not None else {},
        cost_estimate=light_cost(),
        name="weight_grads",
    )(meta, *operands)


def norm_forward(hidden, gain, shift):
    center = hidden - jnp.mean(hidden, -1, keepdims=True)
    spread = jnp.mean(center * center, -1, keepdims=True)
    scale = lax.rsqrt(spread + EPSILON)
    unit = center * scale
    return unit * gain + shift, unit, scale


def norm_gradient(grad, unit, scale, gain):
    inner = grad * gain
    mean_inner = jnp.mean(inner, -1, keepdims=True)
    mean_unit = jnp.mean(inner * unit, -1, keepdims=True)
    return scale * (inner - mean_inner - unit * mean_unit)


def sub_blocks(meta, keys_each, run, skip):
    def one(sub, carry):
        block = pl.program_id(0) * GROUP + sub
        second = (block >= meta[0]).astype(jnp.int32)
        place = pl.ds(pl.multiple_of(second * keys_each, keys_each), keys_each)
        rows = pl.ds(pl.multiple_of(sub * BLOCK, BLOCK), BLOCK)
        pl.when(block < meta[1])(functools.partial(run, sub, rows, place))
        pl.when(block >= meta[1])(functools.partial(skip, sub, rows))
        return carry

    lax.fori_loop(0, GROUP, one, 0)


def mid_forward_kernel(score_scale, meta, x_ref, attn0, attn1, memory_ref, *refs):
    attn = (attn0, attn1)
    self_out, query_w, memory_k, memory_v, cross_out = [refs[2 * i : 2 * i + 2] for i in range(5)]
    bias0, bias1, out_bias, gain, shift = refs[10:15]
    unit1_ref, scale1_ref, unit2_ref, scale2_ref, cross_in_ref, hidden_ref, lse_ref = refs[15:22]
    cq_refs, cattn_refs, ck_refs, cv_refs = [refs[22 + 2 * i : 24 + 2 * i] for i in range(4)]
    flipped = refs[30:32]
    half = attn0.shape[1]
    keys_each = memory_ref.shape[0] // 2

    @pl.when(pl.program_id(0) == 0)
    def _():
        for h, bias in enumerate((bias0, bias1)):
            ck_refs[h][...] = dot_nn(memory_ref[...], memory_k[h][...]).astype(BF16)
            value = dot_nn(memory_ref[...], memory_v[h][...]) + bias[3:4, :]
            cv_refs[h][...] = value.astype(BF16)
            flipped[h][...] = value.T.astype(BF16)

    branch = dot_nt(attn[0][...], self_out[0][...]) + dot_nt(attn[1][...], self_out[1][...])
    n1, unit1, scale1 = norm_forward(
        x_ref[...].astype(F32) + branch + out_bias[0:1, :], gain[0:1, :], shift[0:1, :]
    )
    unit1_ref[...] = unit1
    scale1_ref[...] = scale1
    cross_in = n1.astype(BF16)
    cross_in_ref[...] = cross_in
    for h, bias in enumerate((bias0, bias1)):
        query = (dot_nn(cross_in, query_w[h][...]) + bias[2:3, :]) * score_scale
        cq_refs[h][...] = query.astype(BF16)

    def run(sub, rows, place):
        for h in range(2):
            for pair in range(half // PAIR):
                cols = pair_columns(pair)
                tile = dot_nt(ck_refs[h][place, cols], stack_heads(cq_refs[h][rows, cols]))
                top = jnp.max(tile, 0, keepdims=True)
                exps = jnp.exp(tile - top)
                total = jnp.sum(exps, 0, keepdims=True)
                result = dot_nn(flipped[h][cols, place], exps.astype(BF16))
                cattn_refs[h][rows, cols] = unstack_heads(result / total).astype(BF16)
                row = h * (half // PAIR) + pair
                lse_ref[sub, row : row + 1, :] = top + jnp.log(total)

    def skip(sub, rows):
        lse_ref[sub] = jnp.zeros(lse_ref.shape[1:], F32)
        for h in range(2):
            cattn_refs[h][rows, :] = jnp.zeros((BLOCK, half), BF16)

    sub_blocks(meta, keys_each, run, skip)
    branch = dot_nt(cattn_refs[0][...], cross_out[0][...]) + dot_nt(
        cattn_refs[1][...], cross_out[1][...]
    )
    n1 = unit1_ref[...] * gain[0:1, :] + shift[0:1, :]
    n2, unit2, scale2 = norm_forward(n1 + branch + out_bias[1:2, :], gain[1:2, :], shift[1:2, :])
    unit2_ref[...] = unit2
    scale2_ref[...] = scale2
    hidden_ref[...] = n2.astype(BF16)


def mid_backward_kernel(score_scale, total_rows, meta, dn2_ref, unit2_ref, scale2_ref, unit1_ref, scale1_ref, lse_ref, *refs):
    cq_refs, ck_refs, cv_refs = [refs[2 * i : 2 * i + 2] for i in range(3)]
    self_out, query_w, cross_out = [refs[6 + 2 * i : 8 + 2 * i] for i in range(3)]
    gain = refs[12]
    dy2_ref, dh1_ref, dy_ref, sums_ref = refs[13:17]
    dcq_refs, da_refs = refs[17:19], refs[19:21]
    near_ref, far_ref = refs[21:23]
    dca_refs, flipped, dck_refs, dcv_refs = [refs[23 + 2 * i : 25 + 2 * i] for i in range(4)]
    half = cq_refs[0].shape[1]
    keys_each = ck_refs[0].shape[0] // 2
    here = pl.program_id(0) * GROUP * BLOCK + lax.broadcasted_iota(
        jnp.int32, (GROUP * BLOCK, 1), 0
    )
    inside = here < total_rows

    def load(ref):
        return jnp.where(inside, ref[...], 0.0)

    @pl.when(pl.program_id(0) == 0)
    def _():
        sums_ref[...] = jnp.zeros_like(sums_ref)
        for h in range(2):
            flipped[h][...] = ck_refs[h][...].astype(F32).T.astype(BF16)
            dck_refs[h][...] = jnp.zeros_like(dck_refs[h])
            dcv_refs[h][...] = jnp.zeros_like(dcv_refs[h])

    dn2 = load(dn2_ref)
    unit2 = load(unit2_ref)
    dh2 = norm_gradient(dn2, unit2, load(scale2_ref), gain[1:2, :])
    dh1_ref[...] = dh2
    dy2 = dh2.astype(BF16)
    dy2_ref[...] = dy2
    sums_ref[0:1, :] += jnp.sum(dn2 * unit2, 0, keepdims=True)
    sums_ref[1:2, :] += jnp.sum(dn2, 0, keepdims=True)
    sums_ref[2:3, :] += jnp.sum(dy2.astype(F32), 0, keepdims=True)
    for h in range(2):
        dca_refs[h][...] = dot_nn(dy2, cross_out[h][...]).astype(BF16)

    def run(sub, rows, place):
        for h in range(2):
            for pair in range(half // PAIR):
                cols = pair_columns(pair)
                row = h * (half // PAIR) + pair
                queries = stack_heads(cq_refs[h][rows, cols])
                grads = stack_heads(dca_refs[h][rows, cols])
                tile = dot_nt(ck_refs[h][place, cols], queries)
                probs = jnp.exp(tile - lse_ref[sub, row : row + 1, :])
                grad_probs = dot_nt(cv_refs[h][place, cols], grads)
                row_dot = jnp.sum(probs * grad_probs, 0, keepdims=True)
                grad_score = (probs * (grad_probs - row_dot)).astype(BF16)
                dcv_refs[h][place, cols] += dot_nn(probs.astype(BF16), grads)
                dck_refs[h][place, cols] += dot_nn(grad_score, queries)
                term = dot_nn(flipped[h][cols, place], grad_score)
                dcq_refs[h][rows, cols] = unstack_heads(term).astype(BF16)

    def skip(sub, rows):
        for h in range(2):
            dcq_refs[h][rows, :] = jnp.zeros((BLOCK, half), BF16)

    sub_blocks(meta, keys_each, run, skip)
    dn1 = dh1_ref[...]
    for h in range(2):
        dcq = dcq_refs[h][...]
        dn1 = dn1 + score_scale * dot_nt(dcq, query_w[h][...])
        sums_ref[6:7, h * half : (h + 1) * half] += jnp.sum(dcq.astype(F32), 0, keepdims=True)
    unit1 = load(unit1_ref)
    dh1 = norm_gradient(dn1, unit1, load(scale1_ref), gain[0:1, :])
    dy = dh1.astype(BF16)
    dh1_ref[...] = dh1
    dy_ref[...] = dy
    sums_ref[3:4, :] += jnp.sum(dn1 * unit1, 0, keepdims=True)
    sums_ref[4:5, :] += jnp.sum(dn1, 0, keepdims=True)
    sums_ref[5:6, :] += jnp.sum(dy.astype(F32), 0, keepdims=True)
    for h in range(2):
        da_refs[h][...] = dot_nn(dy, self_out[h][...]).astype(BF16)

    @pl.when(pl.program_id(0) == pl.num_programs(0) - 1)
    def _():
        own = keys_each // 2
        for index, ref in enumerate((dck_refs[0], dck_refs[1], dcv_refs[0], dcv_refs[1])):
            near_ref[:, index * half : (index + 1) * half] = ref[...]
            far = slice((index ^ 1) * half, ((index ^ 1) + 1) * half)
            for seq in range(2):
                base = seq * keys_each
                middle, end = base + own, base + keys_each
                far_ref[middle:end, far] = ref[base:middle, :].astype(BF16)
                far_ref[base:middle, far] = ref[middle:end, :].astype(BF16)


def memory_backward_kernel(near_ref, got_ref, wk0, wv0, wk1, wv1, sum_ref, encoder_ref, bias_ref):
    total = (near_ref[...] + got_ref[...].astype(F32)).astype(BF16)
    half = wk0.shape[1]
    sum_ref[:, :half] = total[:, :half]
    sum_ref[:, half:] = total[:, 2 * half : 3 * half]
    own = total.shape[0] // 4
    mine = jnp.concatenate([total[:own], total[2 * own : 3 * own]], 0)
    grad = dot_nt(mine[:, :half], wk0[...]) + dot_nt(mine[:, half : 2 * half], wk1[...])
    grad = grad + dot_nt(mine[:, 2 * half : 3 * half], wv0[...])
    encoder_ref[...] = (grad + dot_nt(mine[:, 3 * half :], wv1[...])).astype(BF16)
    bias = jnp.sum(mine[:, 2 * half :].astype(F32), 0, keepdims=True)
    bias_ref[...] = jnp.broadcast_to(bias, bias_ref.shape)


def memory_backward(near, got, mid):
    rows, span = near.shape
    half = span // 4
    width = mid[0][0].shape[0]
    columns = [plain_fixed((width, half), 0, m[1] + c) for m in mid for c in (3, 4)]
    return pl.pallas_call(
        memory_backward_kernel,
        grid=(1,),
        in_specs=[plain_fixed((rows, span))] * 2 + columns,
        out_specs=[
            plain_fixed((rows, 2 * half)),
            plain_fixed((rows // 2, width)),
            plain_fixed((8, 2 * half)),
        ],
        out_shape=[
            kept((rows, 2 * half), BF16),
            kept((rows // 2, width), BF16),
            kept((8, 2 * half), F32),
        ],
        cost_estimate=light_cost(),
        name="memory_backward",
    )(near, got, *[m[0] for m in mid for _ in range(2)])


def ffn_forward_kernel(first, hidden_ref, base_ref, expand, reduce, bias, gain, shift, act_ref, slope_ref, total_ref):
    pre = dot_nn(hidden_ref[...], expand[...]) + bias[0:1, :]
    phi = 0.5 * (1.0 + lax.erf(pre * (1.0 / math.sqrt(2.0))))
    density = jnp.exp(-0.5 * pre * pre) * (1.0 / math.sqrt(2.0 * math.pi))
    act = (pre * phi).astype(BF16)
    act_ref[...] = act
    slope_ref[...] = (phi + pre * density).astype(BF16)
    base = base_ref[...]
    if first:
        base = base * gain[0:1, :] + shift[0:1, :]
    total_ref[...] = base + dot_nt(act, reduce[...])


def ffn_forward(first, hidden, base, weight, bias, gain, shift):
    rows, width = hidden.shape
    units = bias.shape[1]
    tall = rows // 2
    wide, long = plain_rows(tall, width), plain_rows(tall, units)

    def side(column):
        return pl.BlockSpec(
            (width, units), lambda step: (0, column), pipeline_mode=pl.Buffered(1)
        )

    return pl.pallas_call(
        functools.partial(ffn_forward_kernel, first),
        grid=(2,),
        in_specs=[wide, wide, side(0), side(1), plain_fixed((1, units))]
        + [plain_fixed((1, width))] * 2,
        out_specs=[long, long, wide],
        out_shape=[
            kept((rows, units), BF16),
            kept((rows, units), BF16),
            kept((rows, width), F32),
        ],
        cost_estimate=light_cost(),
        name="ffn_forward",
    )(hidden, base, weight, weight, bias, gain, shift)


def ffn_backward_kernel(h3_ref, cot_ref, valid_ref, slope0, slope1, in0, in1, out0, out1, gain, shift, n3_ref, dz_ref, dn2_ref, sums_ref, du0, du1, usum0, usum1):
    @pl.when(pl.program_id(0) == 0)
    def _():
        for ref in (sums_ref, usum0, usum1):
            ref[...] = jnp.zeros_like(ref)

    n3, unit, scale = norm_forward(h3_ref[...], gain[2:3, :], shift[2:3, :])
    valid = valid_ref[...] > 0.5
    n3_ref[...] = jnp.where(valid, n3, 0.0).astype(BF16)
    dn3 = jnp.where(valid, cot_ref[...].astype(F32), 0.0)
    dh3 = norm_gradient(dn3, unit, scale, gain[2:3, :])
    dz = dh3.astype(BF16)
    dz_ref[...] = dz
    sums_ref[0:1, :] += jnp.sum(dn3 * unit, 0, keepdims=True)
    sums_ref[1:2, :] += jnp.sum(dn3, 0, keepdims=True)
    sums_ref[2:3, :] += jnp.sum(dz.astype(F32), 0, keepdims=True)
    total = dh3
    sides = ((slope0, out0, in0, du0, usum0), (slope1, out1, in1, du1, usum1))
    for slope, reduce, expand, du_ref, usum in sides:
        du = (dot_nn(dz, reduce[...]) * slope[...].astype(F32)).astype(BF16)
        du_ref[...] = du
        usum[0:1, :] += jnp.sum(du.astype(F32), 0, keepdims=True)
        total = total + dot_nt(du, expand[...])
    dn2_ref[...] = total


def ffn_backward(h3, cot, valid, slope, ffn, gain, shift):
    rows, width = h3.shape
    units = slope[0].shape[1]
    wide, thin, long = [plain_rows(rows // 2, w) for w in (width, 1, units)]

    def side(column):
        return pl.BlockSpec(
            (width, units), lambda step: (0, column), pipeline_mode=pl.Buffered(1)
        )

    return pl.pallas_call(
        ffn_backward_kernel,
        grid=(2,),
        in_specs=[wide, wide, thin, long, long, side(0), side(0), side(1), side(1)]
        + [plain_fixed((3, width))] * 2,
        out_specs=[wide, wide, wide, plain_fixed((8, width)), long, long]
        + [plain_fixed((8, units))] * 2,
        out_shape=[
            kept((rows, width), BF16),
            kept((rows, width), BF16),
            kept((rows, width), F32),
            kept((8, width), F32),
            kept((rows, units), BF16),
            kept((rows, units), BF16),
            kept((8, units), F32),
            kept((8, units), F32),
        ],
        cost_estimate=pl.CostEstimate(flops=1000, bytes_accessed=1000, transcendentals=0),
        name="ffn_backward",
    )(h3, cot, valid, *slope, ffn[0], ffn[1], ffn[0], ffn[1], gain, shift)


def fixed_spec(shape, *index):
    place = index or (0,) * len(shape)
    return pl.BlockSpec(shape, lambda block, meta: place)


def mid_forward(meta, inputs, attn, memory, mid, in_pair, out_bias, gain, shift, score_scale):
    rows, width = inputs.shape
    half = attn[0].shape[1]
    blocks = rows // BLOCK
    memory_rows = memory.shape[0]
    weights = [fixed_spec((width, half), 0, m[1] + c) for c in (0, 1, 3, 4, 2) for m in mid]
    tall = GROUP * BLOCK
    wide, thin, narrow = row_spec(width, tall), row_spec(1, tall), row_spec(half, tall)
    memory_spec = fixed_spec((memory_rows, half))
    outs = pl.pallas_call(
        functools.partial(mid_forward_kernel, score_scale),
        grid_spec=pltpu.PrefetchScalarGridSpec(
            num_scalar_prefetch=1,
            grid=(pl.cdiv(blocks, GROUP),),
            in_specs=[wide, narrow, narrow, fixed_spec(memory.shape)]
            + weights
            + [fixed_spec((4, half))] * 2
            + [fixed_spec((3, width))] * 3,
            out_specs=[wide, thin, wide, thin, wide, wide, lse_spec(GROUP)]
            + [narrow] * 4
            + [memory_spec] * 4,
            scratch_shapes=[pltpu.VMEM((half, memory_rows), BF16)] * 2,
        ),
        out_shape=[
            kept((rows, width), F32),
            kept((rows, 1), F32),
            kept((rows, width), F32),
            kept((rows, 1), F32),
            kept((rows, width), BF16),
            kept((rows, width), BF16),
            kept((blocks, 8, 2 * BLOCK), F32),
        ]
        + [kept((rows, half), BF16)] * 4
        + [kept((memory_rows, half), BF16)] * 4,
        cost_estimate=light_cost(),
        name="mid_forward",
    )(meta, inputs, *attn, memory, *[m[0] for _ in range(5) for m in mid], *in_pair, out_bias, gain, shift)
    return outs[:7], outs[7:9], outs[9:11], outs[11:13], outs[13:15]


def mid_backward(meta, dn2, saved, cq, ck, cv, mid, gain, score_scale):
    unit1, scale1, unit2, scale2, lse = saved
    rows, width = dn2.shape
    half = cq[0].shape[1]
    blocks = rows // BLOCK
    memory_rows = ck[0].shape[0]
    tall = GROUP * BLOCK
    wide, thin, narrow = row_spec(width, tall), row_spec(1, tall), row_spec(half, tall)
    memory_spec = fixed_spec((memory_rows, half))
    weights = [fixed_spec((width, half), 0, m[1] + c) for c in (0, 1, 2) for m in mid]
    outs = pl.pallas_call(
        functools.partial(mid_backward_kernel, score_scale, rows),
        grid_spec=pltpu.PrefetchScalarGridSpec(
            num_scalar_prefetch=1,
            grid=(pl.cdiv(blocks, GROUP),),
            in_specs=[wide, wide, thin, wide, thin, lse_spec(GROUP)]
            + [narrow] * 2
            + [memory_spec] * 4
            + weights
            + [fixed_spec((3, width))],
            out_specs=[wide, wide, wide, fixed_spec((8, width))]
            + [narrow] * 4
            + [fixed_spec((memory_rows, 4 * half))] * 2,
            scratch_shapes=[pltpu.VMEM((tall, half), BF16)] * 2
            + [pltpu.VMEM((half, memory_rows), BF16)] * 2
            + [pltpu.VMEM((memory_rows, half), F32)] * 4,
        ),
        out_shape=[
            kept((rows, width), BF16),
            kept((rows, width), F32),
            kept((rows, width), BF16),
            kept((8, width), F32),
        ]
        + [kept((rows, half), BF16)] * 4
        + [kept((memory_rows, 4 * half), F32), kept((memory_rows, 4 * half), BF16)],
        cost_estimate=light_cost(),
        name="mid_backward",
    )(meta, dn2, unit2, scale2, unit1, scale1, lse, *cq, *ck, *cv, *[m[0] for _ in range(3) for m in mid], gain)
    return outs[:4], outs[4:6], outs[6:8], outs[8], outs[9]


def input_backward_kernel(score_scale, base_ref, dq_ref, own_ref, got_ref, wq, wk, wv, dx_ref, pair_ref, sums_ref):
    @pl.when(pl.program_id(0) == 0)
    def _():
        sums_ref[...] = jnp.zeros_like(sums_ref)

    half = dq_ref.shape[1]
    pair = (own_ref[...] + got_ref[...].astype(F32)).astype(BF16)
    pair_ref[...] = pair
    dq = dq_ref[...]
    dk, dv = pair[:, :half], pair[:, half:]
    sums_ref[0:1, :] += score_scale * jnp.sum(dq.astype(F32), 0, keepdims=True)
    sums_ref[1:2, :] += jnp.sum(dv.astype(F32), 0, keepdims=True)
    total = score_scale * dot_nt(dq, wq[...]) + dot_nt(dk, wk[...]) + dot_nt(dv, wv[...])
    dx_ref[...] = (base_ref[...] + total).astype(dx_ref.dtype)


def plain_rows(rows, width):
    return pl.BlockSpec((rows, width), lambda step: (step, 0))


def plain_fixed(shape, *index):
    place = index or (0,) * len(shape)
    return pl.BlockSpec(shape, lambda step: place)


def input_backward(base, dq, own, got, weight, score_scale, kind):
    rows, width = base.shape
    half = dq.shape[1]
    tall = rows // 2
    return pl.pallas_call(
        functools.partial(input_backward_kernel, score_scale),
        grid=(2,),
        in_specs=[plain_rows(tall, width), plain_rows(tall, half)]
        + [plain_rows(tall, 2 * half)] * 2
        + [plain_fixed((width, half), 0, i) for i in range(3)],
        out_specs=[plain_rows(tall, width), plain_rows(tall, 2 * half), plain_fixed((8, half))],
        out_shape=[
            kept((rows, width), kind),
            kept((rows, 2 * half), BF16),
            kept((8, half), F32),
        ],
        cost_estimate=light_cost(),
        name="input_backward",
    )(base, dq, own, got, weight, weight, weight)


def swap(value):
    return lax.ppermute(value, "tensor", [(0, 1), (1, 0)])


def hop(value, bits):
    return lax.ppermute(value, "dp", [(i, i ^ bits) for i in range(16)])


def pack_kernel(*refs):
    start = 0
    for ref in refs[:-1]:
        refs[-1][:, start : start + ref.shape[1]] = ref[...]
        start += ref.shape[1]


def pack_shards(*parts):
    shard = parts[0].shape[0]
    total = sum(part.shape[1] for part in parts)
    return pl.pallas_call(
        pack_kernel,
        grid=(1,),
        in_specs=[plain_fixed(part.shape) for part in parts],
        out_specs=plain_fixed((shard, total)),
        out_shape=kept((shard, total), BF16),
        cost_estimate=light_cost(),
        name="pack_shards",
    )(*parts)


def assemble_kernel(meta, own_ref, first_ref, second_ref, third_ref, out_ref):
    for low, ref in enumerate((own_ref, first_ref, second_ref, third_ref)):
        out_ref[0, pl.ds(meta[1] ^ low, 1)] = ref[...]


def plane_line(value):
    return jnp.stack([value, hop(value, 4), hop(value, 8), hop(value, 12)])


def low_groups(line):
    return (line, hop(line, 1), hop(line, 2), hop(line, 3))


def assemble(groups):
    rows, count = groups[0].shape[1:]
    index = lax.axis_index("dp")
    meta = jnp.stack([index // 4, index % 4]).astype(jnp.int32)
    spec = pl.BlockSpec((1, rows, count), lambda i, meta: (i ^ meta[0], 0, 0))
    full = pl.pallas_call(
        assemble_kernel,
        grid_spec=pltpu.PrefetchScalarGridSpec(
            num_scalar_prefetch=1,
            grid=(4,),
            in_specs=[spec] * 4,
            out_specs=pl.BlockSpec((1, 4, rows, count), lambda i, meta: (i, 0, 0, 0)),
        ),
        out_shape=kept((4, 4, rows, count), groups[0].dtype),
        cost_estimate=light_cost(),
        name="assemble",
    )(meta, *groups)
    return full.reshape(16 * rows, count)


def total_of(parts):
    return functools.reduce(jnp.add, [part.astype(F32) for part in parts])


def scatter_low(groups):
    received = [hop(groups[low], low) for low in (1, 2, 3)]
    return total_of([groups[0]] + received).astype(BF16)


def scatter_plane(line):
    plane = lax.axis_index("dp") // 4

    def pick(other):
        return lax.dynamic_index_in_dim(line, plane ^ other, 0, keepdims=False)

    received = [hop(pick(other), 4 * other) for other in (1, 2, 3)]
    return total_of([pick(0)] + received)


def wide_scatter(value, groups=None):
    return lax.psum_scatter(
        value, "dp", scatter_dimension=0, tiled=True, axis_index_groups=groups
    )


def sum_low(value):
    return total_of([value] + [hop(value, bits) for bits in (1, 2, 3)])


def sum_planes(value):
    return total_of([value] + [hop(value, 4 * bits) for bits in (1, 2, 3)])


def rows_at(value, ids):
    return value.at[ids].get(mode="promise_in_bounds")


def tie(*values):
    return lax.optimization_barrier(values)


def body(
    tokens,
    encoder,
    lengths,
    deal,
    self_project,
    self_output,
    cross_query,
    cross_memory,
    cross_output,
    hidden_in,
    hidden_out,
    in_bias,
    out_bias,
    hidden_bias,
    norm_gain,
    norm_bias,
    cotangent,
):
    score_scale = 1.0 / math.sqrt(HD)
    dp_count = lax.axis_size("dp")
    dp_index = lax.axis_index("dp")
    tensor_index = lax.axis_index("tensor")
    piece = tokens.shape[1]
    width = tokens.shape[2]
    slots = piece * dp_count
    half = self_project.shape[2]
    units = hidden_in.shape[1]
    shard = self_project.shape[0]
    memory_rows = encoder.shape[1]
    spans = slots // BLOCK
    blocks = (slots + slots // 2) // BLOCK + 1
    rows = blocks * BLOCK
    per_block = BLOCK // piece

    pair_ids = lax.dynamic_slice_in_dim(deal, 2 * dp_index, 2)
    pair_len = rows_at(lengths, pair_ids)
    pieces_used = (pair_len + 2 * piece - 1) // (2 * piece)
    blocks_used = (pieces_used * piece + BLOCK - 1) // BLOCK
    first_blocks = blocks_used[0]
    all_blocks = first_blocks + blocks_used[1]
    meta = jnp.stack([first_blocks, all_blocks, tensor_index]).astype(jnp.int32)

    block_ids = jnp.arange(blocks, dtype=jnp.int32)
    block_seq = (block_ids >= first_blocks).astype(jnp.int32)
    block_local = jnp.minimum(block_ids - block_seq * first_blocks, spans - 1)
    piece_ids = (
        (block_local[:, None] * per_block + jnp.arange(per_block, dtype=jnp.int32)[None, :]) * 2
        + block_seq[:, None]
    ).reshape(-1)
    slot_ids = block_local[:, None] * BLOCK + jnp.arange(BLOCK, dtype=jnp.int32)[None, :]
    positions = ((slot_ids // piece) * 2 + tensor_index) * piece + slot_ids % piece
    row_valid = (
        (positions < jnp.where(block_seq == 1, pair_len[1], pair_len[0])[:, None])
        & (block_ids < all_blocks)[:, None]
    ).reshape(rows, 1)

    send_piece = jnp.arange(dp_count, dtype=jnp.int32)
    spare = jnp.where(
        pieces_used[0] % per_block != 0, first_blocks * per_block - 1, rows // piece - 1
    )
    send_start = jnp.stack([0 * first_blocks, first_blocks * per_block])
    send_ids = jnp.where(
        send_piece[:, None] < pieces_used[None, :],
        send_start[None, :] + send_piece[:, None],
        spare,
    ).reshape(-1)
    inverse = jnp.zeros_like(deal).at[deal].set(jnp.arange(deal.shape[0], dtype=jnp.int32))

    def home_pieces(value):
        return rows_at(value.reshape(rows // piece, piece, width), send_ids)

    def go_home(outgoing):
        return lax.all_to_all(outgoing, "dp", split_axis=0, concat_axis=0, tiled=True)

    def order(value):
        return rows_at(value, deal)

    def arrive(ordered):
        return lax.all_to_all(ordered, "dp", split_axis=0, concat_axis=0, tiled=True)

    def pack(arrived, ids):
        return rows_at(arrived, ids).reshape(rows, width)

    quick = dp_count == 16
    both = (0, 1)
    biases = jnp.concatenate([in_bias.reshape(-1), hidden_bias])
    bias_pair = (biases, swap(biases))
    in_pair = [b[: 4 * half].reshape(4, half) for b in bias_pair]
    hidden_pair = [b[None, 4 * half :] for b in bias_pair]

    memory_full = jnp.concatenate([encoder, swap(encoder)], 1).reshape(4 * memory_rows, width)
    affine = (norm_gain[1:2], norm_bias[1:2] + out_bias[2:3])
    early = (row_valid.astype(F32), affine, in_pair, hidden_pair, meta, piece_ids, memory_full, send_ids, inverse)
    ordered = order(tokens)
    qkv_shard_in = self_project.reshape(shard, 3 * half)
    def slow_gather(value):
        return lax.all_gather(value, "dp", axis=0, tiled=True)

    ordered_cot = order(cotangent)
    if quick:
        qkv_line = plane_line(qkv_shard_in)
        qkv_line, ordered = tie(qkv_line, ordered)
        qkv_groups = low_groups(qkv_line)
        arrived = arrive(ordered)
        ordered_cot, arrived, qkv_groups, early = tie(ordered_cot, arrived, qkv_groups, early)
        qkv_own = assemble(qkv_groups)
    else:
        arrived = arrive(ordered)
        qkv_own = slow_gather(qkv_shard_in)
    qkv_weight = (qkv_own, swap(qkv_own))
    valid_rows, affine, in_pair, hidden_pair, meta, piece_ids, memory_full = early[:7]
    send_ids, inverse = early[7:]
    inputs = pack(arrived, piece_ids)
    arrived_cot = arrive(ordered_cot)

    rest_own = slow_gather(
        pack_shards(
            hidden_in,
            hidden_out.T,
            self_output.T,
            cross_query,
            cross_output.T,
            cross_memory.reshape(shard, 2 * half),
        )
    )


    queries = [None, None]
    near = [None, None]
    attn = [None, None]
    lse = [None, None]
    for h in both:
        queries[h], near[h] = project(inputs, qkv_weight[h], in_pair[h], score_scale)
    far = [swap(near[1 - h]) for h in both]
    attn[1], lse[1] = attend_forward(meta, queries[1], near[1], far[1], piece, spans)
    attn[1], queries[0], far[0] = tie(attn[1], queries[0], far[0])
    attn[0], lse[0] = attend_forward(meta, queries[0], near[0], far[0], piece, spans)
    rest_own, attn[0] = tie(rest_own, attn[0])
    rest_far = swap(rest_own)
    mid_weight = [(rest, 2 * units // half) for rest in (rest_own, rest_far)]
    saved, cqs, cattn, cks, cvs = mid_forward(
        meta, inputs, attn, memory_full, mid_weight, in_pair, out_bias, norm_gain, norm_bias, score_scale
    )
    unit1, scale1, unit2, scale2, cross_in, hidden, clse = saved
    act = [None, None]
    slope = [None, None]
    act[0], slope[0], total = ffn_forward(
        True, hidden, unit2, rest_own, hidden_pair[0], *affine
    )
    act[1], slope[1], total = ffn_forward(
        False, hidden, total, rest_far, hidden_pair[1], *affine
    )
    arrived_cot, total = tie(arrived_cot, total)
    ffn_weight = (rest_own, rest_far)
    n3, dz, dn2, sums3, du0, du1, usum0, usum1 = ffn_backward(
        total, pack(arrived_cot, piece_ids), valid_rows, slope, ffn_weight, norm_gain, norm_bias
    )
    du = (du0, du1)
    output_back = go_home(home_pieces(n3))

    low_meta = jnp.reshape(dp_index % 4, (1,)).astype(jnp.int32)

    fixed = FIXED if quick else PLAIN
    one = (0,)
    far_in = weight_grads(low_meta, [hidden], [du[1]], one, (1.0,), fixed)
    far_out = weight_grads(low_meta, [dz], [act[1]], one, (1.0,), fixed)
    ffn_grads = weight_grads(
        low_meta, [hidden], [du[0]], one, (1.0,), fixed, swap(far_in), 2 * units
    )
    ffn_grads = weight_grads(
        low_meta, [dz], [act[0]], one, (1.0,), fixed, swap(far_out), 2 * units, ffn_grads
    )
    ffn_grads, dn2 = tie(ffn_grads, dn2)
    ffn_line = wide_scatter(ffn_grads.reshape(width, 2 * units), LOW_GROUPS if quick else None)
    rows_back, dcq, da, memory_near, memory_far = mid_backward(
        meta, dn2, (unit1, scale1, unit2, scale2, clse), cqs, cks, cvs, mid_weight, norm_gain, score_scale
    )
    dy2, dh1, dy, sums = rows_back
    da = list(da)
    memory_far, output_back = tie(memory_far, output_back)
    memory_sum, grad_memory, memory_bias = memory_backward(
        memory_near, swap(memory_far), mid_weight
    )
    grad_encoder = grad_memory.reshape(2, memory_rows, width)
    mid_factors = (1.0, score_scale, 1.0, 1.0, 1.0)
    far_mid = weight_grads(
        low_meta,
        [dy, cross_in, dy2],
        [attn[1], dcq[1], cattn[1]],
        (0, 1, 2),
        mid_factors[:3],
        fixed,
    )
    mid_grads = weight_grads(
        low_meta,
        [dy, cross_in, dy2, memory_full],
        [attn[0], dcq[0], cattn[0], (memory_sum, 0), (memory_sum, 1)],
        (0, 1, 2, 3, 3),
        mid_factors,
        fixed,
        swap(far_mid),
    )
    mid_grads, da[0], da[1] = tie(mid_grads, da[0], da[1])
    mid_line = wide_scatter(mid_grads.reshape(width, 5 * half), LOW_GROUPS if quick else None)
    dq = [None, None]
    own = [None, None]
    out = [None, None]
    for h in both:
        dq[h], own[h], out[h] = attend_backward(
            meta, queries[h], da[h], lse[h], near[h], far[h], piece, spans
        )
        if h == 0:
            da[1], dq[0], ffn_line = tie(da[1], dq[0], ffn_line)
    factors = (score_scale, 1.0, 1.0)
    got_far, got_near = swap(out[0]), swap(out[1])
    dx_far, pair_far, sums_far = input_backward(
        dh1, dq[1], own[1], got_far, qkv_weight[1], score_scale, F32
    )
    relative = RELATIVE if quick else PLAIN
    far_grads = weight_grads(
        low_meta, [inputs], [dq[1], (pair_far, 0), (pair_far, 1)], (0, 0, 0), factors, relative
    )
    far_grads, dx_far, got_near, ffn_line = tie(far_grads, dx_far, got_near, ffn_line)
    far_grads = swap(far_grads)
    dx, pair_near, sums_near = input_backward(
        dx_far, dq[0], own[0], got_near, qkv_weight[0], score_scale, BF16
    )
    grad_out = home_pieces(dx)
    grad_out, far_grads, output_back = tie(grad_out, far_grads, output_back)
    output = rows_at(output_back, inverse)
    far_grads, mid_line = tie(far_grads, mid_line)
    ffn_shard = wide_scatter(ffn_line, PLANE_GROUPS) if quick else ffn_line
    ffn_shard = ffn_shard.astype(F32)
    qkv_grads = weight_grads(
        low_meta,
        [inputs],
        [dq[0], (pair_near, 0), (pair_near, 1)],
        (0, 0, 0),
        factors,
        relative,
        far_grads,
    )
    sums, sums3, sums_near, sums_far, usum0, usum1, memory_bias, grad_out = tie(
        sums, sums3, sums_near, sums_far, usum0, usum1, memory_bias, grad_out
    )
    grad_back = go_home(grad_out)
    sums_qkv = [sums_near, sums_far]

    def global_order(pair):
        own_first = jnp.concatenate(pair, -1)
        other_first = jnp.concatenate(pair[::-1], -1)
        return jnp.where(tensor_index == 0, own_first, other_first)

    in_rows = global_order(
        [
            jnp.stack(
                [
                    sums_qkv[h][0],
                    sums_qkv[h][1],
                    score_scale * sums[6, h * half : (h + 1) * half],
                    memory_bias[0, h * half : (h + 1) * half],
                ]
            )
            for h in both
        ]
    )
    hidden_row = global_order([usum0[0], usum1[0]])
    out_rows = jnp.stack([sums[5], sums[2], sums3[2]])
    gain_rows = jnp.stack([sums[3], sums[0], sums3[0]])
    shift_rows = jnp.stack([sums[4], sums[1], sums3[1]])
    small = jnp.concatenate(
        [
            in_rows.reshape(-1),
            hidden_row,
            out_rows.reshape(-1),
            gain_rows.reshape(-1),
            shift_rows.reshape(-1),
        ]
    )
    if quick:
        small = small + swap(small)
        small, qkv_grads = tie(small, qkv_grads)
        qkv_line = scatter_low(qkv_grads)
        small = sum_low(small)
        qkv_line, grad_back, ffn_shard, small, mid_line = tie(
            qkv_line, grad_back, ffn_shard, small, mid_line
        )
        shards = scatter_plane(
            jnp.concatenate([qkv_line, mid_line.reshape(4, shard, 5 * half)], 2)
        )
        qkv_shard, mid_shard = shards[:, : 3 * half], shards[:, 3 * half :]
        small = sum_planes(small)
    else:
        qkv_shard = wide_scatter(qkv_grads).astype(F32)
        mid_shard = mid_line.astype(F32)
        small = lax.psum(small, ("dp", "tensor"))
    grad_tokens = rows_at(grad_back, inverse)
    in_end = 8 * half
    hidden_end = in_end + 2 * units
    in_total = small[:in_end].reshape(4, 2 * half)
    hidden_total = small[in_end:hidden_end]
    rest = small[hidden_end:].reshape(3, 3, width)
    return (
        output,
        grad_tokens,
        grad_encoder,
        qkv_shard.reshape(shard, 3, half),
        mid_shard[:, :half].T,
        mid_shard[:, half : 2 * half],
        mid_shard[:, 3 * half :].reshape(shard, 2, half),
        mid_shard[:, 2 * half : 3 * half].T,
        ffn_shard[:, :units],
        ffn_shard[:, units:].T,
        lax.dynamic_slice_in_dim(in_total, tensor_index * half, half, 1),
        rest[0],
        lax.dynamic_slice_in_dim(hidden_total, tensor_index * units, units, 0),
        rest[1],
        rest[2],
    )


def solution(mesh):
    in_specs = (
        P(None, ("dp", "tensor"), None),
        P("dp", "tensor", None),
        P(),
        P(),
        P("dp", None, "tensor"),
        P("tensor", "dp"),
        P("dp", "tensor"),
        P("dp", None, "tensor"),
        P("tensor", "dp"),
        P("dp", "tensor"),
        P("tensor", "dp"),
        P(None, "tensor"),
        P(),
        P("tensor"),
        P(),
        P(),
        P(None, ("dp", "tensor"), None),
    )
    out_specs = (
        P(None, ("dp", "tensor"), None),
        P(None, ("dp", "tensor"), None),
        P("dp", "tensor", None),
        P("dp", None, "tensor"),
        P("tensor", "dp"),
        P("dp", "tensor"),
        P("dp", None, "tensor"),
        P("tensor", "dp"),
        P("dp", "tensor"),
        P("tensor", "dp"),
        P(None, "tensor"),
        P(),
        P("tensor"),
        P(),
        P(),
    )
    return jax.shard_map(body, mesh=mesh, in_specs=in_specs, out_specs=out_specs, check_vma=False)
```
